32 devices in a mesh: expert: 8 (over z, x), hidden: 4 (over y, core).
Axes of the slice: x: 2, y: 2, z: 4, core: 2. Of those that a mesh axis runs over, the one named last changes fastest.
Arguments:
- tokens: bfloat16 [2, 16384, 512], P(None, ('expert', 'hidden')), may hold values from -6 to 6
- grad_out: bfloat16 [2, 16384, 512], P(None, ('expert', 'hidden')), may hold values from -6 to 6
- attn_routes: int32 [2, 16384, 4], P(None, ('expert', 'hidden')), may hold values from 0 to 23, all different within a row
- ffn_routes: int32 [2, 16384, 2], P(None, ('expert', 'hidden')), may hold values from 0 to 15, all different within a row; in each aligned block of 512 rows (0 to 511, 512 to 1023, ..., all dimensions but the last counted through in order) at most 128 rows name the same one
- segments: int32 [2, 64, 256], P(None, ('expert', 'hidden')), may hold values from 0 to 3, never falling along the last dimension, each value on 1 to 128 neighbouring positions
- pad_mask: int32 [2, 16384], P(None, ('expert', 'hidden')), may hold values 0 or 1
- norm1_gain: float32 [512], replicated, may hold values from 0.5 to 1.5
- norm1_bias: float32 [512], replicated, may hold values from -0.6 to 0.6
- attn_router: bfloat16 [512, 24], replicated, may hold values from -0.125 to 0.125
- query_w: bfloat16 [512, 1536], replicated, may hold values from -0.25 to 0.25
- key_w: bfloat16 [512, 64], replicated, may hold values from -0.25 to 0.25
- value_w: bfloat16 [512, 64], replicated, may hold values from -0.25 to 0.25
- attn_proj: bfloat16 [1536, 512], replicated, may hold values from -2 to 2
- norm2_gain: float32 [512], replicated, may hold values from 0.5 to 1.5
- norm2_bias: float32 [512], replicated, may hold values from -0.6 to 0.6
- ffn_router: bfloat16 [512, 16], replicated, may hold values from -0.1875 to 0.1875
- expert_in: bfloat16 [16, 512, 2048], P('expert', None, 'hidden'), may hold values from -0.25 to 0.25
- expert_out: bfloat16 [16, 2048, 512], P('expert', 'hidden'), may hold values from -0.1875 to 0.1875
- halt_w: float32 [512], replicated, may hold values from -0.25 to 0.25
- halt_b: float32 [1], replicated, may hold values from -2.5 to 2.5
Outputs:
- result: bfloat16 [2, 16384, 512], P(None, ('expert', 'hidden'))
- grad_tokens: float32 [2, 16384, 512], P(None, ('expert', 'hidden'))
- grad_norm1_gain: float32 [512], replicated
- grad_norm1_bias: float32 [512], replicated
- grad_attn_router: float32 [512, 24], replicated
- grad_query_w: float32 [512, 1536], replicated
- grad_key_w: float32 [512, 64], replicated
- grad_value_w: float32 [512, 64], replicated
- grad_attn_proj: float32 [1536, 512], replicated
- grad_norm2_gain: float32 [512], replicated
- grad_norm2_bias: float32 [512], replicated
- grad_ffn_router: float32 [512, 16], replicated
- grad_expert_in: float32 [16, 512, 2048], P('expert', None, 'hidden')
- grad_expert_out: float32 [16, 2048, 512], P('expert', 'hidden')
- grad_halt_w: float32 [512], replicated
- grad_halt_b: float32 [1], replicated
The draws below stay inside these ranges and needn't reach their ends.
Inputs may be any that keep to these rules, and one draw needn't show every extreme that they name: `attn_routes`: each token names 4 different attention experts. `ffn_routes`: each token names 2 different feed-forward experts; in each micro-batch the 512 tokens of one device name no expert more than 128 times, a bound that some block reaches. `segments`: along a packed row the numbers never fall, and each of the 4 numbers covers 1 to 128 positions.
All inputs are finite; a program needn't handle non-finite values. No bound on the sum of `pad_mask` on one device may be relied on, other than what follows from the above.
Results may differ from the reference program's by a relative error of at most 0.015.
The reference program's roundings to bfloat16 on the way count: a program that leaves them out, or rounds other values in their place, can miss the bound.
Values may be sent and summed in bfloat16 or wider, within the bound.
A program may use at most 256 MiB of HBM per device.

```python
import math
from functools import partial
import jax
import jax.numpy as jnp
import numpy as np
from jax import lax

D = 512
NATT = 24
HD = 64
FF = 2048
TOPA = 4
TOPF = 2
MB = 2
SEQ = 256
PAIRS = 4
ATT_BLOCK = 512
TOK_DEV = 512
EXPERTS = 16
CAP = 128
TOKENS = 16384
SEQS = 64
N_EXPERT = 8
N_HIDDEN = 4


def with_ends(entries, rng, low, high):
    shape = entries.shape
    spot = [jax.random.randint(jax.random.fold_in(rng, axis), (), 0, shape[axis]) for axis in range(len(shape))]
    entries = entries.at[tuple(spot)].set(low)
    longest = shape.index(max(shape))
    spot[longest] = (spot[longest] + 1) % shape[longest]
    return entries.at[tuple(spot)].set(high)


def levels(stream_key, dims, cuts, low, top_value):
    level = 1.0
    for position, blocks in cuts:
        heights = jax.random.uniform(jax.random.fold_in(jax.random.fold_in(stream_key, 6), position), (blocks,), jnp.float32, low / len(cuts), top_value / len(cuts))
        level = level * jnp.repeat(jnp.exp(heights), dims[position] // blocks).reshape((-1,) + (1,) * (len(dims) - 1 - position))
    return level


def different_ones(key, rows, count, top, lift):
    order = jax.random.permutation(jax.random.fold_in(key, 1), count)
    pull = order
    for power in range(3):
        pull = pull * pull // count
    pull = pull * lift // count
    chance = jax.random.randint(jax.random.fold_in(key, 2), (rows, count), 0, 4096) + pull
    sure = jax.random.permutation(jax.random.fold_in(key, 3), rows)[jnp.arange(count) % rows]
    chance = jnp.where(jnp.arange(rows)[:, None] == sure[None, :], 1 << 14, chance)
    score = chance * count + jnp.arange(count)
    return lax.top_k(score.astype(jnp.int32), top)[1].astype(jnp.int32)


def split_up(amount, total, most, slope):
    portions = [(1 << 20) // math.isqrt(standing ** slope) + 1 for standing in range(2, amount + 1)]
    spare, given = total - most - (amount - 1), [1] * (amount - 1)
    while spare > 0:
        free = [i for i in range(amount - 1) if given[i] < most]
        pool, remaining = sum([portions[i] for i in free]), spare
        for i in free:
            addition = min(most - given[i], max(1, remaining * portions[i] // pool), spare)
            given[i] = given[i] + addition
            spare = spare - addition
    return np.array([most] + given)


def ragged_sizes(rng, number_of, total, bound, lean):
    if number_of == 2:
        one = jax.random.randint(rng, (), max(1, total - bound), min(bound, total - 1) + 1)
        return jnp.stack([one, total - one])
    sizes = jnp.asarray(split_up(number_of, total, bound, lean), jnp.int32)
    twos = (number_of - 1) // 2
    donor, receiver = sizes[1:1 + 2 * twos:2], sizes[2:2 + 2 * twos:2]
    slack = jnp.minimum(donor - 1, bound - receiver)
    shifted = jax.random.randint(jax.random.fold_in(rng, 1), (twos,), 0, 1 << 20) % (slack + 1)
    sizes = sizes.at[1:1 + 2 * twos:2].set(donor - shifted).at[2:2 + 2 * twos:2].set(receiver + shifted)
    return sizes[jax.random.permutation(jax.random.fold_in(rng, 2), number_of)]


def deal_out(key, own, number, rows, amount, top, bound, lean):
    order = jax.random.permutation(key, amount)
    crowded, ordinary = load_shares(amount, rows * top, bound, lean, True), load_shares(amount, rows * top, bound, lean, False)
    places = jnp.arange(amount)

    def named(tallies, rotation):
        used = int((tallies > 0).sum())
        fixed = max(1, used // 4)
        shifted = fixed + (places - fixed + rotation * (used - fixed)) % max(1, amount - fixed)
        return jnp.zeros((amount,), jnp.int32).at[order[jnp.where(places < fixed, places, shifted)]].set(jnp.asarray(tallies, jnp.int32))

    tallies = jnp.where(number % 4 == 0, named(crowded, number // 4), named(ordinary, number - number // 4 - 1))
    mixed = jax.random.permutation(jax.random.fold_in(own, 3), amount)
    giver, taker = mixed[0:amount // 2 * 2:2], mixed[1:amount // 2 * 2:2]
    slack = jnp.minimum(tallies[giver] - 1, bound - tallies[taker]) // 2
    slack = jnp.where((giver == order[0]) | (taker == order[0]) | (tallies[taker] == 0), 0, jnp.maximum(slack, 0))
    shifted = jax.random.randint(jax.random.fold_in(own, 4), (amount // 2,), 0, 1 << 20) % (slack + 1)
    tallies = tallies.at[giver].add(-shifted).at[taker].add(shifted)
    labels = jnp.searchsorted(jnp.cumsum(tallies), jnp.arange(rows * top), side="right").astype(jnp.int32)
    grid = labels.reshape(top, rows).T
    grid = grid[jax.random.permutation(jax.random.fold_in(own, 1), rows)]
    rotation = jax.random.randint(jax.random.fold_in(own, 2), (rows, 1), 0, top)
    return jnp.take_along_axis(grid, (jnp.arange(top)[None, :] + rotation) % top, axis=1)


def load_shares(amount, total, limit, lean, full):
    weights = [(1 << 20) // math.isqrt(standing ** lean) + 1 for standing in range(1, amount + 1)]
    largest = limit if full else min(limit, max(-(-total // amount), total * weights[0] // sum(weights)))
    least = 1 if total - largest >= amount - 1 else 0
    holding, rest = [largest] + [least] * (amount - 1), total - largest - least * (amount - 1)
    while rest > 0:
        free = [i for i in range(1, amount) if holding[i] < largest] or [i for i in range(1, amount) if holding[i] < limit]
        whole, remaining = sum([weights[i] for i in free]), rest
        for i in free:
            more = min(limit - holding[i], max(1, remaining * weights[i] // whole), rest)
            holding[i] = holding[i] + more
            rest = rest - more
    return np.array(holding)


def scatter_about(own_key, extent, scale, limit, cuts=(), held_as=jnp.bfloat16):
    drawn = scale * jax.random.normal(own_key, extent, jnp.float32)
    if cuts:
        drawn = drawn * levels(own_key, extent, cuts, -0.22, 0.18)
    return jnp.clip(drawn, -limit, limit).astype(held_as)


def setup_inputs(seed: int = 0) -> dict:
    key_list = jax.random.split(jax.random.key(seed), 21)
    tokens = scatter_about(key_list[0], (MB, TOKENS, D), 1.0, 6.0, ((1, 32),))
    grad_out = scatter_about(key_list[1], (MB, TOKENS, D), 1.0, 6.0, ((1, 32),))
    attn_routes = different_ones(key_list[2], MB * TOKENS, NATT, TOPA, 1365).reshape((MB, TOKENS, TOPA))
    ffn_routes_keys = jax.random.split(jax.random.fold_in(key_list[3], 1), MB * TOKENS // TOK_DEV)
    ffn_routes_turns = jax.random.permutation(jax.random.fold_in(key_list[3], 3), MB * TOKENS // TOK_DEV)
    ffn_routes = jax.vmap(lambda own, number: deal_out(jax.random.fold_in(key_list[3], 2), own, number, TOK_DEV, EXPERTS, TOPF, CAP, 2))(ffn_routes_keys, ffn_routes_turns).reshape((MB, TOKENS, TOPF))
    segments = jax.vmap(lambda own: jnp.searchsorted(jnp.cumsum(ragged_sizes(own, PAIRS, SEQ, SEQ // 2, 1)), jnp.arange(SEQ), side="right"))(jax.random.split(key_list[4], MB * SEQS)).reshape((MB, SEQS, SEQ)).astype(jnp.int32)
    pad_mask = with_ends((jax.random.randint(key_list[5], (MB, TOKENS), 0, 8) < 7).astype(jnp.int32), jax.random.fold_in(key_list[5], 1), 0, 1)
    norm1_gain = jnp.clip(1.0 + 0.1 * jax.random.normal(key_list[6], (D,), jnp.float32), 0.5, 1.5)
    norm1_bias = scatter_about(key_list[7], (D,), 0.1, 0.6, (), jnp.float32)
    attn_router = scatter_about(key_list[8], (D, NATT), (4 * D) ** -0.5, 0.125)
    query_w = scatter_about(key_list[9], (D, NATT * HD), D ** -0.5, 0.25)
    key_w = scatter_about(key_list[10], (D, HD), D ** -0.5, 0.25)
    value_w = scatter_about(key_list[11], (D, HD), D ** -0.5, 0.25)
    attn_proj = scatter_about(key_list[12], (NATT * HD, D), 8 ** -0.5, 2.0)
    norm2_gain = jnp.clip(1.0 + 0.1 * jax.random.normal(key_list[13], (D,), jnp.float32), 0.5, 1.5)
    norm2_bias = scatter_about(key_list[14], (D,), 0.1, 0.6, (), jnp.float32)
    ffn_router = scatter_about(key_list[15], (D, EXPERTS), (2 * D) ** -0.5, 0.1875)
    expert_in = scatter_about(key_list[16], (EXPERTS, D, FF), D ** -0.5, 0.25, ((0, 8), (2, 4)))
    expert_out = scatter_about(key_list[17], (EXPERTS, FF, D), (FF // 2) ** -0.5, 0.1875, ((0, 8), (1, 4)))
    halt_w = scatter_about(key_list[18], (D,), D ** -0.5, 0.25, (), jnp.float32)
    halt_b = scatter_about(key_list[19], (1,), 1.0, 2.5, (), jnp.float32)
    return {"tokens": tokens, "grad_out": grad_out, "attn_routes": attn_routes, "ffn_routes": ffn_routes, "segments": segments, "pad_mask": pad_mask, "norm1_gain": norm1_gain, "norm1_bias": norm1_bias, "attn_router": attn_router, "query_w": query_w, "key_w": key_w, "value_w": value_w, "attn_proj": attn_proj, "norm2_gain": norm2_gain, "norm2_bias": norm2_bias, "ffn_router": ffn_router, "expert_in": expert_in, "expert_out": expert_out, "halt_w": halt_w, "halt_b": halt_b}


PRECISE = lax.Precision.HIGHEST

@jax.custom_vjp
def low(v):
    return lax.optimization_barrier(v.astype(jnp.bfloat16)).astype(jnp.float32)

@jax.custom_vjp
def low_back(v):
    return v

def low_keep(v):
    return (low(v), None)

def low_pass(kept, grad):
    return (grad,)

def back_keep(v):
    return (v, None)

def back_low(kept, grad):
    return (low(grad),)
low.defvjp(low_keep, low_pass)
low_back.defvjp(back_keep, back_low)

def layer_norm(value, gain, shift):
    center = value - lax.optimization_barrier(jnp.mean(value, axis=-1, keepdims=True))
    spread = lax.optimization_barrier(jnp.mean(center * center, axis=-1, keepdims=True))
    return center * lax.rsqrt(spread + 1e-05) * gain + shift

def attend_block(operands):
    query_sel, keys, values, segment, padding = operands
    place = jnp.arange(segment.shape[0])
    same_row = place[:, None] // SEQ == place[None, :] // SEQ
    same_pair = segment[:, None] == segment[None, :]
    visible = (padding[None, :] == 1) | (place[:, None] == place[None, :])
    allowed = same_row & same_pair & visible
    scores = low_back(jnp.einsum('qkh,jh->qkj', query_sel, keys, precision=PRECISE) * HD ** (-0.5))
    scores = jnp.where(allowed[:, None, :], scores, -1e+30)
    weights = low(jax.nn.softmax(scores, axis=-1))
    return low_back(jnp.einsum('qkj,jh->qkh', weights, values, precision=PRECISE))

def expert_rows(operands):
    rows, first, second = operands
    pre = low_back(jnp.dot(rows, first, precision=PRECISE))
    act = low(jax.nn.gelu(pre))
    return low(low_back(jnp.dot(act, second, precision=PRECISE)))

def dispatch_table(route_ffn):
    flat_route = route_ffn.reshape(-1).astype(jnp.int32)
    onehot = (flat_route[:, None] == jnp.arange(EXPERTS, dtype=jnp.int32)[None, :]).astype(jnp.int32)
    rank = lax.optimization_barrier(jnp.sum((jnp.cumsum(onehot, axis=0) - 1) * onehot, axis=1)).astype(jnp.int32)
    depth = N_EXPERT * N_HIDDEN * CAP
    slot = (flat_route * depth + rank).astype(jnp.int32)
    owner = (jnp.arange(flat_route.shape[0], dtype=jnp.int32) // TOPF).astype(jnp.int32)
    source = jnp.zeros((EXPERTS * depth,), jnp.int32).at[slot].set(owner)
    filled = jnp.zeros((EXPERTS * depth,), jnp.float32).at[slot].set(1.0)
    return (source, filled, slot)

def forward(state_in, params, tables):
    route_attn, route_ffn, segment, padding, source, filled, slot = tables
    gain_one, bias_one, router_attn, query_w, key_w, value_w, proj_w, gain_two, bias_two, router_ffn, first_w, second_w, halt_w, halt_b = params
    tok_rows = state_in.shape[0]
    normed = low(layer_norm(state_in, gain_one, bias_one))
    logits_attn = low_back(jnp.dot(normed, router_attn, precision=PRECISE))
    gate_attn = jax.nn.softmax(jnp.take_along_axis(logits_attn, route_attn, axis=1), axis=-1)
    query_all = low(low_back(jnp.dot(normed, query_w, precision=PRECISE))).reshape(tok_rows, NATT, HD)
    keys = low(low_back(jnp.dot(normed, key_w, precision=PRECISE)))
    values = low(low_back(jnp.dot(normed, value_w, precision=PRECISE)))
    query_sel = jnp.take_along_axis(query_all, route_attn[:, :, None], axis=1)
    blocks = tok_rows // ATT_BLOCK
    heads = lax.map(jax.checkpoint(attend_block), (query_sel.reshape(blocks, ATT_BLOCK, TOPA, HD), keys.reshape(blocks, ATT_BLOCK, HD), values.reshape(blocks, ATT_BLOCK, HD), segment.reshape(blocks, ATT_BLOCK), padding.reshape(blocks, ATT_BLOCK))).reshape(tok_rows, TOPA, HD)
    select = (route_attn[:, :, None] == jnp.arange(NATT, dtype=jnp.int32)[None, None, :]).astype(jnp.float32)
    mixed = jnp.einsum('tke,tkh->teh', select, gate_attn[:, :, None] * heads, precision=PRECISE)
    mixed = low(low_back(mixed.reshape(tok_rows, NATT * HD)))
    attn_part = low_back(jnp.dot(mixed, proj_w, precision=PRECISE))
    state_mid = state_in + attn_part
    normed_two = low(layer_norm(state_mid, gain_two, bias_two))
    logits_ffn = low_back(jnp.dot(normed_two, router_ffn, precision=PRECISE))
    gate_ffn = jax.nn.softmax(jnp.take_along_axis(logits_ffn, route_ffn, axis=1), axis=-1)
    slot_rows = low_back(normed_two[source]) * filled[:, None]
    expert_res = lax.map(jax.checkpoint(expert_rows), (slot_rows.reshape(EXPERTS, -1, D), first_w, second_w))
    picked = expert_res.reshape(-1, D)[slot].reshape(tok_rows, TOPF, D)
    state_end = state_mid + lax.optimization_barrier(jnp.sum(gate_ffn[:, :, None] * picked, axis=1))
    halting = jax.nn.sigmoid(lax.optimization_barrier(jnp.sum(state_end * halt_w, axis=-1, keepdims=True)) + halt_b)
    return state_in + halting * (state_end - state_in)

def reference(tokens, grad_out, attn_routes, ffn_routes, segments, pad_mask, norm1_gain, norm1_bias, attn_router, query_w, key_w, value_w, attn_proj, norm2_gain, norm2_bias, ffn_router, expert_in, expert_out, halt_w, halt_b):
    params = (norm1_gain.astype(jnp.float32), norm1_bias.astype(jnp.float32), attn_router.astype(jnp.float32), query_w.astype(jnp.float32), key_w.astype(jnp.float32), value_w.astype(jnp.float32), attn_proj.astype(jnp.float32), norm2_gain.astype(jnp.float32), norm2_bias.astype(jnp.float32), ffn_router.astype(jnp.float32), expert_in.astype(jnp.float32), expert_out.astype(jnp.float32), halt_w.astype(jnp.float32), halt_b.astype(jnp.float32))
    totals = jax.tree.map(jnp.zeros_like, params)
    results = []
    grads_in = []
    for micro in range(MB):
        source, filled, slot = dispatch_table(ffn_routes[micro])
        tables = (attn_routes[micro], ffn_routes[micro], segments[micro].reshape(-1), pad_mask[micro], source, filled, slot)
        outcome, pullback = jax.vjp(partial(forward, tables=tables), tokens[micro].astype(jnp.float32), params)
        grad_state, grad_params = pullback(grad_out[micro].astype(jnp.float32))
        results.append(outcome.astype(jnp.bfloat16))
        grads_in.append(grad_state)
        totals = jax.tree.map(jnp.add, totals, grad_params)
    return (jnp.stack(results), jnp.stack(grads_in), totals[0], totals[1], totals[2], totals[3], totals[4], totals[5], totals[6], totals[7], totals[8], totals[9], totals[10], totals[11], totals[12], totals[13])
```

```python
import functools
import math

import jax
import jax.numpy as jnp
from jax import lax
from jax.experimental import pallas as pl
from jax.experimental.pallas import tpu as pltpu
from jax.sharding import PartitionSpec as P

SEQ = 256
LANES = 128
F32 = jnp.float32
BF16 = jnp.bfloat16
GELU_C = math.sqrt(2.0 / math.pi)
GELU_A = 0.044715
VMEM_LIMIT = 60 * 1024 * 1024


def mm(left, right):
    return jnp.dot(left, right, preferred_element_type=F32)


def mm_nt(left, right):
    return lax.dot_general(left, right, (((1,), (1,)), ((), ())), preferred_element_type=F32)


def mm_tn(left, right):
    return lax.dot_general(left, right, (((0,), (0,)), ((), ())), preferred_element_type=F32)


def lane_iota(rows, lanes=LANES):
    return lax.broadcasted_iota(jnp.int32, (rows, lanes), 1)


def norm_parts(value):
    center = value - jnp.mean(value, axis=-1, keepdims=True)
    rstd = lax.rsqrt(jnp.mean(center * center, axis=-1, keepdims=True) + 1e-05)
    return center * rstd, rstd


def norm_back(hat, rstd, gain, grad):
    scaled = grad * gain
    first = jnp.mean(scaled, axis=-1, keepdims=True)
    second = jnp.mean(scaled * hat, axis=-1, keepdims=True)
    return rstd * (scaled - first - hat * second)


def fold_rows(value):
    return jnp.sum(value, axis=0, keepdims=True)


def pick_head(tiles, route, lane):
    pair = lax.shift_right_logical(route, 1)
    out = tiles[0]
    for j in range(1, len(tiles)):
        out = jnp.where(pair == j, tiles[j], out)
    odd = (route & 1) == 1
    return jnp.where(odd, pltpu.roll(out, LANES // 2, 1), out)


def place_heads(parts, routes, count, lane):
    half = lax.shift_right_logical(lane, 6)
    kept = [jnp.where(half == (r & 1), p, 0.0) for p, r in zip(parts, routes)]
    pairs = [lax.shift_right_logical(r, 1) for r in routes]
    tiles = []
    for j in range(count):
        total = jnp.where(pairs[0] == j, kept[0], 0.0)
        for k, p in zip(kept[1:], pairs[1:]):
            total = total + jnp.where(p == j, k, 0.0)
        tiles.append(total)
    return tiles


def softmax_cols(cols):
    top = functools.reduce(jnp.maximum, cols)
    expo = [jnp.exp(c - top) for c in cols]
    total = functools.reduce(jnp.add, expo)
    return [e / total for e in expo]


def put_cols(cols, rows, width):
    lane = lane_iota(rows, width)
    out = jnp.zeros((rows, width), cols[0].dtype)
    for i, c in enumerate(cols):
        out = jnp.where(lane == i, c, out)
    return out


def split_three(value):
    high = value.astype(BF16)
    rest = value - high.astype(F32)
    middle = rest.astype(BF16)
    last = (rest - middle.astype(F32)).astype(BF16)
    return jnp.concatenate([high.astype(F32), middle.astype(F32), last.astype(F32)], axis=0).astype(BF16)


def join_three(value):
    n = value.shape[0] // 3
    return value[:n] + value[n : 2 * n] + value[2 * n :]


def row_to_col(row):
    n = row.shape[1]
    place = lax.broadcasted_iota(jnp.int32, (n, n), 0)
    other = lax.broadcasted_iota(jnp.int32, (n, n), 1)
    return jnp.sum(jnp.where(place == other, row, 0.0), axis=-1, keepdims=True)


def dispatch(slot_rows, values, out_ref):
    chunk = 256
    tokens = values[0].shape[0]
    spot = lax.broadcasted_iota(jnp.int32, (chunk, tokens), 0)

    def body(k, carry):
        base = spot + k * chunk
        if len(values) == 1:
            pick = jnp.where((base == slot_rows[0]) | (base == slot_rows[1]), 1.0, 0.0).astype(BF16)
            out = mm(pick, values[0][...])
        else:
            out = mm(jnp.where(base == slot_rows[0], 1.0, 0.0).astype(BF16), values[0][...])
            out = out + mm(jnp.where(base == slot_rows[1], 1.0, 0.0).astype(BF16), values[1][...])
        out_ref[pl.ds(pl.multiple_of(k * chunk, chunk), chunk), :] = out.astype(BF16)
        return carry

    lax.fori_loop(0, out_ref.shape[0] // chunk, body, 0)


def route_kernel(capacity, row_ref, col_ref, grad_ref, slotrow_ref, slotcol_ref, out_ref):
    tokens = grad_ref.shape[1]
    before = lax.broadcasted_iota(jnp.int32, (tokens, tokens), 0)
    after = lax.broadcasted_iota(jnp.int32, (tokens, tokens), 1)
    upper = jnp.where(before < after, 1.0, 0.0).astype(BF16)
    lower = jnp.where(before > after, 1.0, 0.0).astype(BF16)
    sub = lax.broadcasted_iota(jnp.int32, (LANES, tokens), 0)
    row = row_ref[0]
    named = [jnp.where(sub == row[2 + i : 3 + i, :], 1.0, 0.0) for i in range(2)]
    rank = mm((named[0] + named[1]).astype(BF16), upper)
    slots = [
        fold_rows(named[i] * rank).astype(jnp.int32) + row[2 + i : 3 + i, :] * capacity for i in range(2)
    ]
    sub8 = lax.broadcasted_iota(jnp.int32, (8, tokens), 0)
    slotrow_ref[...] = jnp.where(sub8 == 0, slots[0], slots[1])
    lanes = lane_iota(tokens)
    col = col_ref[0]
    named_c = [jnp.where(lanes == col[:, 4 + i : 5 + i], 1.0, 0.0) for i in range(2)]
    rank_c = mm(lower, (named_c[0] + named_c[1]).astype(BF16))
    slots_c = [
        jnp.sum(named_c[i] * rank_c, axis=-1, keepdims=True).astype(jnp.int32) + col[:, 4 + i : 5 + i] * capacity
        for i in range(2)
    ]
    slotcol_ref[...] = put_cols(slots_c, tokens, slotcol_ref.shape[1])
    dispatch(slots, [grad_ref.at[0]], out_ref)


def route_step(micro, row, col, grad, slots, capacity):
    _, count, width = grad.shape
    out_shape = (
        jax.ShapeDtypeStruct((8, count), jnp.int32),
        jax.ShapeDtypeStruct((count, 8), jnp.int32),
        jax.ShapeDtypeStruct((slots, width), BF16),
    )
    return pl.pallas_call(
        functools.partial(route_kernel, capacity),
        grid=(1,),
        out_shape=out_shape,
        in_specs=[
            pl.BlockSpec((1, 8, count), lambda i: (micro, 0, 0)),
            pl.BlockSpec((1, count, 8), lambda i: (micro, 0, 0)),
            pl.BlockSpec((1, count, width), lambda i: (micro, 0, 0)),
        ],
        out_specs=[pl.BlockSpec(o.shape, lambda i: (0, 0)) for o in out_shape],
        compiler_params=pltpu.CompilerParams(vmem_limit_bytes=VMEM_LIMIT),
        cost_estimate=pl.CostEstimate(flops=2 * count * width * slots, bytes_accessed=3 << 20, transcendentals=0),
        name="route_step",
    )(row, col, grad)


def attention_forward_kernel(
    x_ref, grad_ref, col_ref, row_ref, slotrow_ref, vec_ref, hb_ref, qw_ref, kvr_ref, proj_ref, frw_ref,
    mid_ref, n2_ref, normed_ref, mixed_ref, probs_ref, qs_ref, kv_ref, gates_ref, scal_ref, out_ref,
    n2_all,
):
    step = pl.program_id(0)
    rows = x_ref.shape[1]
    top_attn = 4
    lane = lane_iota(rows)
    x = x_ref[0].astype(F32)
    col = col_ref[0]
    row = row_ref[0]
    hat, _ = norm_parts(x)
    normed = (hat * vec_ref[0:1, :] + vec_ref[1:2, :]).astype(BF16)
    normed_ref[...] = normed
    kvr = mm(normed, kvr_ref[...])
    kv = kvr[:, :LANES].astype(BF16)
    kv_ref[...] = kv
    logits = kvr[:, LANES:]
    routes = [col[:, i : i + 1] for i in range(top_attn)]
    picked = [
        jnp.sum(jnp.where(lane == r, logits, 0.0), axis=-1, keepdims=True) for r in routes
    ]
    gates = softmax_cols(picked)
    query = mm(normed, qw_ref[...])
    heads_pairs = query.shape[1] // LANES
    tiles = [query[:, j * LANES : (j + 1) * LANES] for j in range(heads_pairs)]
    low = lane < LANES // 2
    same = col[:, 6:7] == row[0:1, :]
    place = lax.broadcasted_iota(jnp.int32, (rows, rows), 0)
    other = lax.broadcasted_iota(jnp.int32, (rows, rows), 1)
    allowed = same & ((row[1:2, :] == 1) | (place == other))
    scale = 0.125
    shares = []
    for i in range(top_attn):
        sel = jnp.where(low, pick_head(tiles, routes[i], lane), 0.0).astype(BF16)
        qs_ref[0, i] = sel
        scores = mm_nt(sel, kv) * scale
        scores = jnp.where(allowed, scores, -1e30)
        expo = jnp.exp(scores - jnp.max(scores, axis=-1, keepdims=True))
        probs = (expo * (1.0 / jnp.sum(expo, axis=-1, keepdims=True))).astype(BF16)
        probs_ref[0, i] = probs
        heads = mm(probs, kv) * gates[i]
        shares.append(jnp.where(low, pltpu.roll(heads, LANES // 2, 1), heads))
    mixed_tiles = place_heads(shares, routes, heads_pairs, lane)
    mixed = jnp.concatenate([t.astype(BF16) for t in mixed_tiles], axis=1)
    mixed_ref[...] = mixed
    mid = x + mm(mixed, proj_ref[...])
    mid_ref[...] = mid
    hat2, _ = norm_parts(mid)
    n2 = (hat2 * vec_ref[2:3, :] + vec_ref[3:4, :]).astype(BF16)
    n2_ref[...] = n2
    n2_all[pl.ds(pl.multiple_of(step * rows, rows), rows), :] = n2
    logits_ffn = mm(n2, frw_ref[...])
    gates_ffn = softmax_cols(
        [
            jnp.sum(jnp.where(lane == col[:, 4 + i : 5 + i], logits_ffn, 0.0), axis=-1, keepdims=True)
            for i in range(2)
        ]
    )
    gates_ref[...] = put_cols(gates, rows, gates_ref.shape[1])
    stop = jnp.sum(mid * vec_ref[4:5, :], axis=-1, keepdims=True) + hb_ref[0:1, 0:1]
    pull = jnp.sum(grad_ref[0].astype(F32) * (mid - x), axis=-1, keepdims=True)
    scal_ref[...] = jnp.transpose(put_cols([stop, pull] + gates_ffn, rows, LANES))[:8, :]

    @pl.when(step == pl.num_programs(0) - 1)
    def _():
        dispatch([slotrow_ref[0:1, :], slotrow_ref[1:2, :]], [n2_all], out_ref)


def attention_forward(micro, tokens, grad, col, row, slotrow, vec, hb, qw, kvr, proj, frw, slots):
    _, count, width = tokens.shape
    steps = count // SEQ
    inner = qw.shape[1]
    whole = lambda a: pl.BlockSpec(a.shape, lambda r: (0,) * a.ndim)
    out_shape = (
        jax.ShapeDtypeStruct((count, width), F32),
        jax.ShapeDtypeStruct((count, width), BF16),
        jax.ShapeDtypeStruct((count, width), BF16),
        jax.ShapeDtypeStruct((count, inner), BF16),
        jax.ShapeDtypeStruct((steps, 4, SEQ, SEQ), BF16),
        jax.ShapeDtypeStruct((steps, 4, SEQ, LANES), BF16),
        jax.ShapeDtypeStruct((count, LANES), BF16),
        jax.ShapeDtypeStruct((count, 8), F32),
        jax.ShapeDtypeStruct((8, count), F32),
        jax.ShapeDtypeStruct((slots, width), BF16),
    )
    by_row = lambda c: pl.BlockSpec((SEQ, c), lambda r: (r, 0))
    return pl.pallas_call(
        attention_forward_kernel,
        grid=(steps,),
        out_shape=out_shape,
        in_specs=[
            pl.BlockSpec((1, SEQ, width), lambda r: (micro, r, 0)),
            pl.BlockSpec((1, SEQ, width), lambda r: (micro, r, 0)),
            pl.BlockSpec((1, SEQ, 8), lambda r: (micro, r, 0)),
            pl.BlockSpec((1, 8, SEQ), lambda r: (micro, 0, r)),
            whole(slotrow), whole(vec), whole(hb), whole(qw), whole(kvr), whole(proj), whole(frw),
        ],
        out_specs=[
            by_row(width), by_row(width), by_row(width), by_row(inner),
            pl.BlockSpec((1, 4, SEQ, SEQ), lambda r: (r, 0, 0, 0)),
            pl.BlockSpec((1, 4, SEQ, LANES), lambda r: (r, 0, 0, 0)),
            by_row(LANES), by_row(8),
            pl.BlockSpec((8, SEQ), lambda r: (0, r)),
            pl.BlockSpec((slots, width), lambda r: (0, 0)),
        ],
        scratch_shapes=[pltpu.VMEM((count, width), BF16)],
        compiler_params=pltpu.CompilerParams(vmem_limit_bytes=VMEM_LIMIT),
        cost_estimate=pl.CostEstimate(
            flops=2 * count * width * (2 * inner + 256 + slots), bytes_accessed=12 << 20, transcendentals=count * 4 * SEQ
        ),
        name="attention_forward",
    )(tokens, grad, col, row, slotrow, vec, hb, qw, kvr, proj, frw)


def gelu_parts(pre):
    square = pre * pre
    inner = jnp.tanh(GELU_C * pre * (1.0 + GELU_A * square))
    return square, inner


def expert_forward_kernel(rows_ref, grad_ref, vec_ref, first_ref, second_ref, out_ref, scal_ref, total):
    part = pl.program_id(1)
    src, _, cap, width = rows_ref.shape
    rows = rows_ref[...].reshape(src * cap, width)
    pre = mm(rows, first_ref[0, 0])
    _, inner = gelu_parts(pre)
    act = (0.5 * pre * (1.0 + inner)).astype(BF16)
    res = mm(act, second_ref[0, 0])

    @pl.when(part == 0)
    def _():
        total[...] = res

    @pl.when(part > 0)
    def _():
        total[...] += res

    @pl.when(part == pl.num_programs(1) - 1)
    def _():
        halt = split_three(jnp.broadcast_to(vec_ref[4:5, :], (8, width)))
        ones = jnp.ones((8, width), BF16)
        sub8 = lax.broadcasted_iota(jnp.int32, (8, cap), 0)
        for s in range(src):
            low = total[s * cap : (s + 1) * cap, :].astype(BF16)
            out_ref[s, 0] = low
            stop = join_three(mm_nt(halt, low))
            prod = low.astype(F32) * grad_ref[s, 0].astype(F32)
            high = prod.astype(BF16)
            rest = (prod - high.astype(F32)).astype(BF16)
            pull = mm_nt(ones, high) + mm_nt(ones, rest)
            scal_ref[s, 0] = jnp.where(sub8 == 0, stop, pull)


def expert_forward(rows, grad, vec, first, second):
    src, local, cap, width = rows.shape
    parts, _, _, hid = first.shape
    spec_rows = pl.BlockSpec((src, 1, cap, width), lambda e, h: (0, e, 0, 0))
    return pl.pallas_call(
        expert_forward_kernel,
        grid=(local, parts),
        out_shape=(
            jax.ShapeDtypeStruct(rows.shape, BF16),
            jax.ShapeDtypeStruct((src, local, 8, cap), F32),
        ),
        in_specs=[
            spec_rows,
            spec_rows,
            pl.BlockSpec(vec.shape, lambda e, h: (0, 0)),
            pl.BlockSpec((1, 1, width, hid), lambda e, h: (h, e, 0, 0)),
            pl.BlockSpec((1, 1, hid, width), lambda e, h: (h, e, 0, 0)),
        ],
        out_specs=[spec_rows, pl.BlockSpec((src, 1, 8, cap), lambda e, h: (0, e, 0, 0))],
        scratch_shapes=[pltpu.VMEM((src * cap, width), F32)],
        compiler_params=pltpu.CompilerParams(vmem_limit_bytes=VMEM_LIMIT),
        cost_estimate=pl.CostEstimate(
            flops=4 * src * local * cap * width * hid * parts,
            bytes_accessed=6 * src * local * cap * width + 4 * local * parts * width * hid,
            transcendentals=src * local * cap * hid * parts,
        ),
        name="expert_forward",
    )(rows, grad, vec, first, second)


def expert_backward_kernel(add_old, *refs):
    rows_ref, grad_ref, ab_ref, vec_ref, first_ref, second_ref = refs[:6]
    refs = refs[6:]
    if add_old:
        old_first_ref, old_second_ref = refs[:2]
        refs = refs[2:]
    gfirst_ref, gsecond_ref, out_ref, total, gin_all = refs
    part = pl.program_id(1)
    src, _, cap, width = rows_ref.shape

    @pl.when(part == 0)
    def _():
        for s in range(src):
            ab = ab_ref[s, 0]
            scaled = row_to_col(ab[0:1, :]) * grad_ref[s, 0].astype(F32) + row_to_col(ab[1:2, :]) * vec_ref[4:5, :]
            gin_all[s * cap : (s + 1) * cap, :] = scaled.astype(BF16)

    rows = rows_ref[...].reshape(src * cap, width)
    gin = gin_all[...]
    first = first_ref[0, 0]
    second = second_ref[0, 0]
    pre = mm(rows, first)
    gact = mm_nt(gin, second)
    square, inner = gelu_parts(pre)
    half = 0.5 * (1.0 + inner)
    act = (pre * half).astype(BF16)
    slope = half + 0.5 * pre * (1.0 - inner * inner) * (GELU_C + (3.0 * GELU_C * GELU_A) * square)
    gpre = (gact * slope).astype(BF16)
    gsecond = mm_tn(act, gin)
    gfirst = mm_tn(rows, gpre)
    if add_old:
        gsecond = gsecond + old_second_ref[0, 0].astype(F32)
        gfirst = gfirst + old_first_ref[0, 0].astype(F32)
    gsecond_ref[0, 0] = gsecond.astype(BF16)
    gfirst_ref[0, 0] = gfirst.astype(BF16)
    res = mm_nt(gpre, first)

    @pl.when(part == 0)
    def _():
        total[...] = res

    @pl.when(part > 0)
    def _():
        total[...] += res

    @pl.when(part == pl.num_programs(1) - 1)
    def _():
        out_ref[...] = total[...].astype(BF16).reshape(out_ref.shape)


def expert_backward(rows, grad, ab, vec, first, second, old):
    src, local, cap, width = rows.shape
    parts, _, _, hid = first.shape
    spec_rows = pl.BlockSpec((src, 1, cap, width), lambda e, h: (0, e, 0, 0))
    spec_first = pl.BlockSpec((1, 1, width, hid), lambda e, h: (h, e, 0, 0))
    spec_second = pl.BlockSpec((1, 1, hid, width), lambda e, h: (h, e, 0, 0))
    return pl.pallas_call(
        functools.partial(expert_backward_kernel, bool(old)),
        grid=(local, parts),
        out_shape=(
            jax.ShapeDtypeStruct(first.shape, BF16),
            jax.ShapeDtypeStruct(second.shape, BF16),
            jax.ShapeDtypeStruct(rows.shape, BF16),
        ),
        in_specs=[
            spec_rows, spec_rows,
            pl.BlockSpec((src, 1, 8, cap), lambda e, h: (0, e, 0, 0)),
            pl.BlockSpec(vec.shape, lambda e, h: (0, 0)),
            spec_first, spec_second,
        ] + [spec_first, spec_second][: len(old)],
        out_specs=[spec_first, spec_second, spec_rows],
        scratch_shapes=[pltpu.VMEM((src * cap, width), F32), pltpu.VMEM((src * cap, width), BF16)],
        compiler_params=pltpu.CompilerParams(vmem_limit_bytes=VMEM_LIMIT),
        cost_estimate=pl.CostEstimate(
            flops=10 * src * local * cap * width * hid * parts,
            bytes_accessed=6 * src * local * cap * width + 8 * local * parts * width * hid,
            transcendentals=src * local * cap * hid * parts,
        ),
        name="expert_backward",
    )(rows, grad, ab, vec, first, second, *old)


def greet(axis, peers, make_id):
    barrier = pltpu.get_barrier_semaphore()
    me = lax.axis_index(axis)
    for k in range(1, peers):
        pl.semaphore_signal(
            barrier, inc=1, device_id=make_id(lax.rem(me + k, peers)), device_id_type=pl.DeviceIdType.MESH
        )
    pl.semaphore_wait(barrier, peers - 1)
    return me


def scalar_kernel(n_expert, scal_ref, rowsc_ref, slotrow_ref, cols_ref, ab_ref, got, sent, got2, send_sem, recv_sem, send_sem2, recv_sem2):
    local, cap = scal_ref.shape[1], scal_ref.shape[3]
    tokens = rowsc_ref.shape[1]
    other = lax.axis_index("hidden")
    make_id = lambda e: (e, other)
    me = greet("expert", n_expert, make_id)

    def copies(source, target, ssem, rsem):
        out = []
        for k in range(1, n_expert):
            peer = lax.rem(me + k, n_expert)
            out.append(
                pltpu.make_async_remote_copy(
                    source.at[peer], target.at[me], ssem.at[k - 1], rsem.at[k - 1],
                    device_id=make_id(peer), device_id_type=pl.DeviceIdType.MESH,
                )
            )
        return out

    moves = copies(scal_ref, got, send_sem, recv_sem)
    for c in moves:
        c.start()
    got[me] = scal_ref[me]
    for c in moves:
        c.wait()
    slot = [slotrow_ref[i : i + 1, :] for i in range(2)]
    spot = lax.broadcasted_iota(jnp.int32, (cap, tokens), 0)

    def onehot(expert):
        base = spot + expert * cap
        return [jnp.where(base == s, 1.0, 0.0).astype(BF16) for s in slot]

    zero = jnp.zeros((24, tokens), F32)

    def collect(expert, carry):
        values = split_three(got[lax.div(expert, local), lax.rem(expert, local)])
        return tuple(c + mm(values, p) for c, p in zip(carry, onehot(expert)))

    found = lax.fori_loop(0, n_expert * local, collect, (zero, zero))
    found = [join_three(f) for f in found]
    stop, pull, gate0, gate1 = [rowsc_ref[i : i + 1, :] for i in range(4)]
    gates = [gate0, gate1]
    yh = [f[0:1, :] for f in found]
    yg = [f[1:2, :] for f in found]
    halting = jax.nn.sigmoid(stop + gate0 * yh[0] + gate1 * yh[1])
    s = (pull + gate0 * yg[0] + gate1 * yg[1]) * halting * (1.0 - halting)
    u = [halting * g + s * h for g, h in zip(yg, yh)]
    mean = gate0 * u[0] + gate1 * u[1]
    keep = [halting, s, gate0 * (u[0] - mean), gate1 * (u[1] - mean), gate0, gate1]
    sub = lax.broadcasted_iota(jnp.int32, (LANES, tokens), 0)
    table = jnp.zeros((LANES, tokens), F32)
    for i, r in enumerate(keep):
        table = jnp.where(sub == i, r, table)
    cols_ref[...] = jnp.transpose(table)[:, :8]
    sub8 = lax.broadcasted_iota(jnp.int32, (8, tokens), 0)
    ab = [
        split_three(jnp.where(sub8 == 0, g * halting, jnp.where(sub8 == 1, g * s, 0.0))) for g in gates
    ]

    def spread(expert, carry):
        picks = onehot(expert)
        sent[lax.div(expert, local), lax.rem(expert, local)] = join_three(mm_nt(ab[0], picks[0]) + mm_nt(ab[1], picks[1]))
        return carry

    lax.fori_loop(0, n_expert * local, spread, 0)
    moves = copies(sent, got2, send_sem2, recv_sem2)
    for c in moves:
        c.start()
    got2[me] = sent[me]
    for c in moves:
        c.wait()
    ab_ref[...] = got2[...]


def scalar_step(n_expert, scal, rowsc, slotrow):
    vmem = pl.BlockSpec(memory_space=pltpu.VMEM)
    tokens = rowsc.shape[1]
    return pl.pallas_call(
        functools.partial(scalar_kernel, n_expert),
        out_shape=(jax.ShapeDtypeStruct((tokens, 8), F32), jax.ShapeDtypeStruct(scal.shape, F32)),
        in_specs=[vmem] * 3,
        out_specs=[vmem] * 2,
        scratch_shapes=[pltpu.VMEM(scal.shape, F32)] * 3 + [pltpu.SemaphoreType.DMA((n_expert - 1,))] * 4,
        compiler_params=pltpu.CompilerParams(collective_id=0, has_side_effects=True),
        cost_estimate=pl.CostEstimate(flops=10**9, bytes_accessed=1 << 20, transcendentals=tokens),
        name="scalar_step",
    )(scal, rowsc, slotrow)


def result_kernel(has_old, *refs):
    x_ref, mid_ref, ret_ref, cols_ref, slotcol_ref = refs[:5]
    result_ref, hsum_ref = refs[-2:]
    tokens, width = mid_ref.shape
    chunk = 256
    chunks = ret_ref.shape[0] // chunk
    lane = lane_iota(tokens, chunk)
    slot_c = [slotcol_ref[:, i : i + 1] for i in range(2)]

    def gather(k, carry):
        block = ret_ref[pl.ds(pl.multiple_of(k * chunk, chunk), chunk), :]
        base = lane + k * chunk
        return tuple(
            c + mm(jnp.where(base == s, 1.0, 0.0).astype(BF16), block) for c, s in zip(carry, slot_c)
        )

    zero = jnp.zeros((tokens, width), F32)
    picked = lax.fori_loop(0, chunks, gather, (zero, zero))
    halting, s = cols_ref[:, 0:1], cols_ref[:, 1:2]
    x = x_ref[0].astype(F32)
    end = mid_ref[...] + (cols_ref[:, 4:5] * picked[0] + cols_ref[:, 5:6] * picked[1])
    result_ref[0] = (x + halting * (end - x)).astype(BF16)
    sub8 = lax.broadcasted_iota(jnp.int32, (8, width), 0)
    ssum = jnp.broadcast_to(jnp.sum(s, axis=0, keepdims=True), (1, width))
    hsum_ref[...] = jnp.where(sub8 == 0, fold_rows(s * end), jnp.where(sub8 == 1, ssum, 0.0))


def result_step(micro, tokens, mid, ret, cols, slotcol, old):
    _, count, width = tokens.shape
    whole = lambda a: pl.BlockSpec(a.shape, lambda i: (0,) * a.ndim)
    part = pl.BlockSpec((1, count, width), lambda i: (micro, 0, 0))
    return pl.pallas_call(
        functools.partial(result_kernel, bool(old)),
        grid=(1,),
        out_shape=(jax.ShapeDtypeStruct(tokens.shape, BF16), jax.ShapeDtypeStruct((8, width), F32)),
        in_specs=[part] + [whole(a) for a in (mid, ret, cols, slotcol)] + [pl.BlockSpec(memory_space=pl.ANY)] * len(old),
        out_specs=[part, pl.BlockSpec((8, width), lambda i: (0, 0))],
        input_output_aliases={5: 0} if old else {},
        compiler_params=pltpu.CompilerParams(vmem_limit_bytes=VMEM_LIMIT),
        cost_estimate=pl.CostEstimate(
            flops=4 * count * ret.shape[0] * width, bytes_accessed=5 << 20, transcendentals=count
        ),
        name="result_step",
    )(tokens, mid, ret, cols, slotcol, *old)


def attention_backward_kernel(last, n_old, *refs):
    (x_ref, grad_ref, col_ref, vec_ref, qw_ref, kvr_ref, proj_ref, frw_ref,
     mid_ref, n2_ref, normed_ref, mixed_ref, probs_ref, qs_ref, kv_ref, gates_ref, slotcol_ref,
     back_ref, cols_ref) = refs[:19]
    old = refs[19 : 19 + n_old]
    gtok_ref, gq_out, gproj_out, gkvr_out, gfr_out, gvec_out = refs[19 + n_old : 25 + n_old]
    gsum, gq_ref, gproj_ref, gkvr_ref, gfr_ref, gvec_ref = refs[25 + n_old :]
    step = pl.program_id(0)
    rows, width = mid_ref.shape
    lane = lane_iota(rows)
    low = lane < LANES // 2
    col = col_ref[0]
    chunk = 256
    slot_c = [slotcol_ref[:, i : i + 1] for i in range(2)]
    lane_c = lane_iota(rows, chunk)
    accs = (gq_ref, gproj_ref, gkvr_ref, gfr_ref, gvec_ref)

    @pl.when(step == 0)
    def _():
        for k, ref in enumerate(accs):
            ref[...] = old[k][...] if old else jnp.zeros_like(ref)

    gsum[...] = jnp.zeros_like(gsum)

    def gather(k, carry):
        block = back_ref[pl.ds(pl.multiple_of(k * chunk, chunk), chunk), :]
        base = lane_c + k * chunk
        pick = jnp.where((base == slot_c[0]) | (base == slot_c[1]), 1.0, 0.0).astype(BF16)
        gsum[...] += mm(pick, block)
        return carry

    lax.fori_loop(0, back_ref.shape[0] // chunk, gather, 0)
    glog = jnp.zeros((rows, LANES), F32)
    for i in range(2):
        glog = jnp.where(lane == col[:, 4 + i : 5 + i], cols_ref[:, 2 + i : 3 + i], glog)
    glog = glog.astype(BF16)
    n2 = n2_ref[...]
    gfr_ref[...] += mm_tn(n2, glog)
    gn2 = gsum[...] + mm_nt(glog, frw_ref[...])
    hat2, rstd2 = norm_parts(mid_ref[...])
    grad = grad_ref[0].astype(F32)
    halting = cols_ref[:, 0:1]
    gend = halting * grad + cols_ref[:, 1:2] * vec_ref[4:5, :]
    gmid = gend + norm_back(hat2, rstd2, vec_ref[2:3, :], gn2)
    ggain2 = fold_rows(gn2 * hat2)
    gbias2 = fold_rows(gn2)
    gattn = gmid.astype(BF16)
    gproj_ref[...] += mm_tn(mixed_ref[...], gattn)
    gmixed = mm_nt(gattn, proj_ref[...]).astype(BF16).astype(F32)
    pairs = gmixed.shape[1] // LANES
    tiles = [gmixed[:, j * LANES : (j + 1) * LANES] for j in range(pairs)]
    kv = kv_ref[...]
    scale = 0.125
    routes = [col[:, i : i + 1] for i in range(4)]
    gkv = jnp.zeros((rows, LANES), F32)
    ggates = []
    parts = []
    for i in range(4):
        gate = gates_ref[:, i : i + 1]
        sel = pltpu.roll(pick_head(tiles, routes[i], lane), LANES // 2, 1)
        sel = jnp.where(low, 0.0, sel)
        probs = probs_ref[0, i]
        heads = mm(probs, kv)
        ggates.append(jnp.sum(heads * sel, axis=-1, keepdims=True))
        gheads = (gate * sel).astype(BF16)
        gprobs = mm_nt(gheads, kv)
        probs_f = probs.astype(F32)
        inner = jnp.sum(probs_f * gprobs, axis=-1, keepdims=True)
        gscores = (probs_f * (gprobs - inner)).astype(BF16)
        gkv = gkv + mm_tn(probs, gheads) + mm_tn(gscores, qs_ref[0, i]) * scale
        gq = mm(gscores, kv) * scale
        parts.append(jnp.where(low, gq, pltpu.roll(gq, LANES // 2, 1)))
    gtiles = place_heads(parts, routes, pairs, lane)
    gquery = jnp.concatenate([t.astype(BF16) for t in gtiles], axis=1)
    normed = normed_ref[...]
    gq_ref[...] += mm_tn(normed, gquery)
    mean = ggates[0] * gates_ref[:, 0:1]
    for i in range(1, 4):
        mean = mean + ggates[i] * gates_ref[:, i : i + 1]
    alog = jnp.zeros((rows, LANES), F32)
    for i in range(4):
        alog = jnp.where(lane == routes[i], gates_ref[:, i : i + 1] * (ggates[i] - mean), alog)
    gkvr = jnp.concatenate([gkv.astype(BF16), alog.astype(BF16)], axis=1)
    gkvr_ref[...] += mm_tn(normed, gkvr)
    gnormed = mm_nt(gquery, qw_ref[...]) + mm_nt(gkvr, kvr_ref[...])
    hat, rstd = norm_parts(x_ref[0].astype(F32))
    gtok_ref[0] = grad * (1.0 - halting) + gmid + norm_back(hat, rstd, vec_ref[0:1, :], gnormed)
    sub8 = lax.broadcasted_iota(jnp.int32, (8, width), 0)
    gvec = jnp.where(sub8 == 0, fold_rows(gnormed * hat), 0.0)
    gvec = jnp.where(sub8 == 1, fold_rows(gnormed), gvec)
    gvec = jnp.where(sub8 == 2, ggain2, gvec)
    gvec_ref[...] += jnp.where(sub8 == 3, gbias2, gvec)

    @pl.when(step == pl.num_programs(0) - 1)
    def _():
        for ref, out in zip(accs, (gq_out, gproj_out, gkvr_out, gfr_out, gvec_out)):
            out[...] = ref[...].astype(out.dtype)


def attention_backward(micro, last, tokens, grad, col, vec, qw, kvr, proj, frw, saved, back, cols, old):
    mid, n2, normed, mixed, probs, qs, kv, gates, slotcol = saved
    _, count, width = tokens.shape
    steps = count // SEQ
    inner = qw.shape[1]
    whole = lambda a: pl.BlockSpec(a.shape, lambda r: (0,) * a.ndim)
    by_row = lambda c: pl.BlockSpec((SEQ, c), lambda r: (r, 0))
    part = pl.BlockSpec((1, SEQ, width), lambda r: (micro, r, 0))
    kind = BF16 if last else F32
    out_shape = (
        jax.ShapeDtypeStruct(tokens.shape, F32),
        jax.ShapeDtypeStruct(qw.shape, kind),
        jax.ShapeDtypeStruct(proj.shape, kind),
        jax.ShapeDtypeStruct(kvr.shape, kind),
        jax.ShapeDtypeStruct(frw.shape, kind),
        jax.ShapeDtypeStruct((8, width), F32),
    )
    old_in = [old[k] for k in (1, 2, 3, 4, 5)] if old else []
    return pl.pallas_call(
        functools.partial(attention_backward_kernel, last, len(old_in) + (1 if old else 0)),
        grid=(steps,),
        out_shape=out_shape,
        in_specs=[
            part, part,
            pl.BlockSpec((1, SEQ, 8), lambda r: (micro, r, 0)),
            whole(vec), whole(qw), whole(kvr), whole(proj), whole(frw),
            by_row(width), by_row(width), by_row(width), by_row(inner),
            pl.BlockSpec((1, 4, SEQ, SEQ), lambda r: (r, 0, 0, 0)),
            pl.BlockSpec((1, 4, SEQ, LANES), lambda r: (r, 0, 0, 0)),
            by_row(LANES), by_row(8), by_row(8),
            whole(back), by_row(8),
        ] + [whole(o) for o in old_in] + [pl.BlockSpec(memory_space=pl.ANY)] * (1 if old else 0),
        out_specs=[part] + [pl.BlockSpec(o.shape, lambda r: (0, 0)) for o in out_shape[1:]],
        scratch_shapes=[
            pltpu.VMEM((SEQ, width), F32),
            pltpu.VMEM(qw.shape, F32),
            pltpu.VMEM(proj.shape, F32),
            pltpu.VMEM(kvr.shape, F32),
            pltpu.VMEM(frw.shape, F32),
            pltpu.VMEM((8, width), F32),
        ],
        input_output_aliases={24: 0} if old else {},
        compiler_params=pltpu.CompilerParams(vmem_limit_bytes=VMEM_LIMIT),
        cost_estimate=pl.CostEstimate(
            flops=2 * count * width * (4 * inner + 512 + back.shape[0]), bytes_accessed=24 << 20, transcendentals=0
        ),
        name="attention_backward",
    )(tokens, grad, col, vec, qw, kvr, proj, frw, mid, n2, normed, mixed, probs, qs, kv, gates, slotcol, back, cols,
      *old_in, *(old[:1] if old else []))


def sum_kernel(sizes, value_ref, out_ref, got, got2, part, send_sem, recv_sem, send_sem2, recv_sem2):
    n_expert, n_hidden = sizes
    e = lax.axis_index("expert")
    h = lax.axis_index("hidden")
    barrier = pltpu.get_barrier_semaphore()
    for k in range(1, n_expert):
        pl.semaphore_signal(barrier, inc=1, device_id=(lax.rem(e + k, n_expert), h), device_id_type=pl.DeviceIdType.MESH)
    for k in range(1, n_hidden):
        pl.semaphore_signal(barrier, inc=1, device_id=(e, lax.rem(h + k, n_hidden)), device_id_type=pl.DeviceIdType.MESH)
    pl.semaphore_wait(barrier, n_expert + n_hidden - 2)
    moves = []
    for k in range(1, n_expert):
        moves.append(
            pltpu.make_async_remote_copy(
                value_ref, got.at[e], send_sem.at[k - 1], recv_sem.at[k - 1],
                device_id=(lax.rem(e + k, n_expert), h), device_id_type=pl.DeviceIdType.MESH,
            )
        )
    for c in moves:
        c.start()
    got[e] = value_ref[...]
    for c in moves:
        c.wait()
    part[...] = jnp.sum(got[...], axis=0)
    moves = []
    for k in range(1, n_hidden):
        moves.append(
            pltpu.make_async_remote_copy(
                part, got2.at[h], send_sem2.at[k - 1], recv_sem2.at[k - 1],
                device_id=(e, lax.rem(h + k, n_hidden)), device_id_type=pl.DeviceIdType.MESH,
            )
        )
    for c in moves:
        c.start()
    got2[h] = part[...]
    for c in moves:
        c.wait()
    out_ref[...] = jnp.sum(got2[...], axis=0)


def sum_everywhere(sizes, value):
    vmem = pl.BlockSpec(memory_space=pltpu.VMEM)
    return pl.pallas_call(
        functools.partial(sum_kernel, sizes),
        out_shape=jax.ShapeDtypeStruct(value.shape, F32),
        in_specs=[vmem],
        out_specs=vmem,
        scratch_shapes=[
            pltpu.VMEM((sizes[0],) + value.shape, F32),
            pltpu.VMEM((sizes[1],) + value.shape, F32),
            pltpu.VMEM(value.shape, F32),
        ]
        + [pltpu.SemaphoreType.DMA((sizes[0] - 1,))] * 2
        + [pltpu.SemaphoreType.DMA((sizes[1] - 1,))] * 2,
        compiler_params=pltpu.CompilerParams(collective_id=1, has_side_effects=True),
        name="sum_everywhere",
    )(value)


def pad_lanes(a):
    return jnp.pad(a, ((0, 0), (0, LANES - a.shape[1])))


def per_device(
    tokens, grad_out, attn_routes, ffn_routes, segments, pad_mask, norm1_gain, norm1_bias, attn_router,
    query_w, key_w, value_w, attn_proj, norm2_gain, norm2_bias, ffn_router, expert_in, expert_out, halt_w, halt_b,
    *, n_expert, n_hidden,
):
    micros, count, width = tokens.shape
    experts = ffn_router.shape[1]
    capacity = 4 * count // experts
    slots = experts * capacity
    local = experts // n_expert
    first = lax.all_gather(expert_in, "hidden", axis=0, tiled=False)
    second = lax.all_gather(expert_out, "hidden", axis=0, tiled=False)
    seg = segments.reshape(micros, count)
    zeros = jnp.zeros_like(seg)
    col = jnp.concatenate([attn_routes, ffn_routes, seg[:, :, None], pad_mask[:, :, None]], axis=2)
    row = jnp.stack([seg, pad_mask, ffn_routes[:, :, 0], ffn_routes[:, :, 1], zeros, zeros, zeros, zeros], axis=1)
    none = jnp.zeros_like(halt_w)
    vec = jnp.stack([norm1_gain, norm1_bias, norm2_gain, norm2_bias, halt_w, none, none, none])
    kvr = jnp.concatenate([key_w, value_w, pad_lanes(attn_router)], axis=1)
    frw = pad_lanes(ffn_router)
    hb = jnp.broadcast_to(halt_b.reshape(1, 1), (8, LANES))

    def exchange(a):
        return lax.all_to_all(a, "expert", split_axis=0, concat_axis=0, tiled=True)

    def slotted(a):
        return exchange(a.reshape(n_expert, local * capacity, width)).reshape(n_expert, local, capacity, width)

    def returned(a):
        return exchange(a.reshape(n_expert, local * capacity, width)).reshape(slots, width)

    plan = [route_step(m, row, col, grad_out, slots, capacity) for m in range(micros)]
    far_grad = [slotted(p[2]) for p in plan]
    fwd = [
        attention_forward(m, tokens, grad_out, col, row, plan[m][0], vec, hb, query_w, kvr, attn_proj, frw, slots)
        for m in range(micros)
    ]
    arrived = [slotted(f[9]) for f in fwd]
    results = []
    cols = []
    abs_ = []
    for m in range(micros):
        y, scal = expert_forward(arrived[m], far_grad[m], vec, first, second)
        results.append(y)
        c, ab = scalar_step(n_expert, scal, fwd[m][8], plan[m][0])
        cols.append(c)
        abs_.append(ab)
    gback = []
    old = ()
    for m in range(micros):
        gf, gs, rows = expert_backward(arrived[m], far_grad[m], abs_[m], vec, first, second, old)
        gback.append(returned(rows))
        old = (gf, gs)
    gfirst = lax.psum_scatter(old[0], "hidden", scatter_dimension=0, tiled=False).astype(F32)
    gsecond = lax.psum_scatter(old[1], "hidden", scatter_dimension=0, tiled=False).astype(F32)
    out = ()
    for m in range(micros):
        f = fwd[m]
        saved = f[:8] + (plan[m][1],)
        out = attention_backward(
            m, m == micros - 1, tokens, grad_out, col, vec, query_w, kvr, attn_proj, frw, saved, gback[m], cols[m], out
        )
    res = ()
    hsum = None
    for m in range(micros):
        res = result_step(m, tokens, fwd[m][0], returned(results[m]), cols[m], plan[m][1], res[:1])
        hsum = res[1] if hsum is None else hsum + res[1]
    gq, gproj, gkvr, gfr = [a.astype(F32) for a in lax.psum(tuple(out[1:5]), ("expert", "hidden"))]
    small = sum_everywhere((n_expert, n_hidden), jnp.concatenate([out[5], hsum], axis=0))
    head = key_w.shape[1]
    return (
        res[0],
        out[0],
        small[0],
        small[1],
        gkvr[:, LANES : LANES + attn_router.shape[1]],
        gq,
        gkvr[:, :head],
        gkvr[:, head : 2 * head],
        gproj,
        small[2],
        small[3],
        gfr[:, :experts],
        gfirst,
        gsecond,
        small[8],
        small[9, :1],
    )


def solution(mesh):
    rows = P(None, ("expert", "hidden"), None)
    in_specs = (rows,) * 5 + (P(None, ("expert", "hidden")),) + (P(),) * 10 + (
        P("expert", None, "hidden"), P("expert", "hidden", None), P(), P(),
    )
    out_specs = (rows,) * 2 + (P(),) * 10 + (P("expert", None, "hidden"), P("expert", "hidden", None), P(), P())
    return jax.shard_map(
        functools.partial(per_device, n_expert=mesh.shape["expert"], n_hidden=mesh.shape["hidden"]),
        mesh=mesh, in_specs=in_specs, out_specs=out_specs, check_vma=False,
    )
```

```python
import functools
import math

import jax
import jax.numpy as jnp
from jax import lax
from jax.experimental import pallas as pl
from jax.experimental.pallas import tpu as pltpu
from jax.sharding import PartitionSpec as P

SEQ = 256
LANES = 128
F32 = jnp.float32
BF16 = jnp.bfloat16
GELU_C = math.sqrt(2.0 / math.pi)
GELU_A = 0.044715
VMEM_LIMIT = 60 * 1024 * 1024


def mm(left, right):
    return jnp.dot(left, right, preferred_element_type=F32)


def mm_nt(left, right):
    return lax.dot_general(left, right, (((1,), (1,)), ((), ())), preferred_element_type=F32)


def mm_tn(left, right):
    return lax.dot_general(left, right, (((0,), (0,)), ((), ())), preferred_element_type=F32)


def lane_iota(rows, lanes=LANES):
    return lax.broadcasted_iota(jnp.int32, (rows, lanes), 1)


def norm_parts(value):
    center = value - jnp.mean(value, axis=-1, keepdims=True)
    rstd = lax.rsqrt(jnp.mean(center * center, axis=-1, keepdims=True) + 1e-05)
    return center * rstd, rstd


def norm_back(hat, rstd, gain, grad):
    scaled = grad * gain
    first = jnp.mean(scaled, axis=-1, keepdims=True)
    second = jnp.mean(scaled * hat, axis=-1, keepdims=True)
    return rstd * (scaled - first - hat * second)


def fold_rows(value):
    return jnp.sum(value, axis=0, keepdims=True)


def pick_head(tiles, route, lane):
    pair = lax.shift_right_logical(route, 1)
    out = tiles[0]
    for j in range(1, len(tiles)):
        out = jnp.where(pair == j, tiles[j], out)
    odd = (route & 1) == 1
    return jnp.where(odd, pltpu.roll(out, LANES // 2, 1), out)


def place_heads(parts, routes, count, lane):
    half = lax.shift_right_logical(lane, 6)
    kept = [jnp.where(half == (r & 1), p, 0.0) for p, r in zip(parts, routes)]
    pairs = [lax.shift_right_logical(r, 1) for r in routes]
    tiles = []
    for j in range(count):
        total = jnp.where(pairs[0] == j, kept[0], 0.0)
        for k, p in zip(kept[1:], pairs[1:]):
            total = total + jnp.where(p == j, k, 0.0)
        tiles.append(total)
    return tiles


def softmax_cols(cols):
    top = functools.reduce(jnp.maximum, cols)
    expo = [jnp.exp(c - top) for c in cols]
    total = functools.reduce(jnp.add, expo)
    return [e / total for e in expo]


def put_cols(cols, rows, width):
    lane = lane_iota(rows, width)
    out = jnp.zeros((rows, width), cols[0].dtype)
    for i, c in enumerate(cols):
        out = jnp.where(lane == i, c, out)
    return out


def split_three(value):
    high = value.astype(BF16)
    rest = value - high.astype(F32)
    middle = rest.astype(BF16)
    last = (rest - middle.astype(F32)).astype(BF16)
    return jnp.concatenate([high.astype(F32), middle.astype(F32), last.astype(F32)], axis=0).astype(BF16)


def join_three(value):
    n = value.shape[0] // 3
    return value[:n] + value[n : 2 * n] + value[2 * n :]


def row_to_col(row):
    n = row.shape[1]
    place = lax.broadcasted_iota(jnp.int32, (n, n), 0)
    other = lax.broadcasted_iota(jnp.int32, (n, n), 1)
    return jnp.sum(jnp.where(place == other, row, 0.0), axis=-1, keepdims=True)


def dispatch(slot_rows, values, out_ref):
    chunk = 256
    tokens = values[0].shape[0]
    spot = lax.broadcasted_iota(jnp.int32, (chunk, tokens), 0)

    def body(k, carry):
        base = spot + k * chunk
        if len(values) == 1:
            pick = jnp.where((base == slot_rows[0]) | (base == slot_rows[1]), 1.0, 0.0).astype(BF16)
            out = mm(pick, values[0][...])
        else:
            out = mm(jnp.where(base == slot_rows[0], 1.0, 0.0).astype(BF16), values[0][...])
            out = out + mm(jnp.where(base == slot_rows[1], 1.0, 0.0).astype(BF16), values[1][...])
        out_ref[pl.ds(pl.multiple_of(k * chunk, chunk), chunk), :] = out.astype(BF16)
        return carry

    lax.fori_loop(0, out_ref.shape[0] // chunk, body, 0)


def route_kernel(capacity, row_ref, col_ref, grad_ref, slotrow_ref, slotcol_ref, out_ref):
    tokens = grad_ref.shape[1]
    before = lax.broadcasted_iota(jnp.int32, (tokens, tokens), 0)
    after = lax.broadcasted_iota(jnp.int32, (tokens, tokens), 1)
    upper = jnp.where(before < after, 1.0, 0.0).astype(BF16)
    lower = jnp.where(before > after, 1.0, 0.0).astype(BF16)
    sub = lax.broadcasted_iota(jnp.int32, (LANES, tokens), 0)
    row = row_ref[0]
    named = [jnp.where(sub == row[2 + i : 3 + i, :], 1.0, 0.0) for i in range(2)]
    rank = mm((named[0] + named[1]).astype(BF16), upper)
    slots = [
        fold_rows(named[i] * rank).astype(jnp.int32) + row[2 + i : 3 + i, :] * capacity for i in range(2)
    ]
    sub8 = lax.broadcasted_iota(jnp.int32, (8, tokens), 0)
    slotrow_ref[...] = jnp.where(sub8 == 0, slots[0], slots[1])
    lanes = lane_iota(tokens)
    col = col_ref[0]
    named_c = [jnp.where(lanes == col[:, 4 + i : 5 + i], 1.0, 0.0) for i in range(2)]
    rank_c = mm(lower, (named_c[0] + named_c[1]).astype(BF16))
    slots_c = [
        jnp.sum(named_c[i] * rank_c, axis=-1, keepdims=True).astype(jnp.int32) + col[:, 4 + i : 5 + i] * capacity
        for i in range(2)
    ]
    slotcol_ref[...] = put_cols(slots_c, tokens, slotcol_ref.shape[1])
    dispatch(slots, [grad_ref.at[0]], out_ref)


def route_step(micro, row, col, grad, slots, capacity):
    _, count, width = grad.shape
    out_shape = (
        jax.ShapeDtypeStruct((8, count), jnp.int32),
        jax.ShapeDtypeStruct((count, 8), jnp.int32),
        jax.ShapeDtypeStruct((slots, width), BF16),
    )
    return pl.pallas_call(
        functools.partial(route_kernel, capacity),
        grid=(1,),
        out_shape=out_shape,
        in_specs=[
            pl.BlockSpec((1, 8, count), lambda i: (micro, 0, 0)),
            pl.BlockSpec((1, count, 8), lambda i: (micro, 0, 0)),
            pl.BlockSpec((1, count, width), lambda i: (micro, 0, 0)),
        ],
        out_specs=[pl.BlockSpec(o.shape, lambda i: (0, 0)) for o in out_shape],
        compiler_params=pltpu.CompilerParams(vmem_limit_bytes=VMEM_LIMIT),
        cost_estimate=pl.CostEstimate(flops=2 * count * width * slots, bytes_accessed=3 << 20, transcendentals=0),
        name="route_step",
    )(row, col, grad)


def attention_forward_kernel(
    x_ref, grad_ref, col_ref, row_ref, slotrow_ref, vec_ref, hb_ref, qw_ref, kvr_ref, proj_ref, frw_ref,
    mid_ref, n2_ref, normed_ref, mixed_ref, probs_ref, qs_ref, kv_ref, gates_ref, scal_ref, out_ref,
    n2_all,
):
    step = pl.program_id(0)
    rows = x_ref.shape[1]
    top_attn = 4
    lane = lane_iota(rows)
    x = x_ref[0].astype(F32)
    col = col_ref[0]
    row = row_ref[0]
    hat, _ = norm_parts(x)
    normed = (hat * vec_ref[0:1, :] + vec_ref[1:2, :]).astype(BF16)
    normed_ref[...] = normed
    kvr = mm(normed, kvr_ref[...])
    kv = kvr[:, :LANES].astype(BF16)
    kv_ref[...] = kv
    logits = kvr[:, LANES:]
    routes = [col[:, i : i + 1] for i in range(top_attn)]
    picked = [
        jnp.sum(jnp.where(lane == r, logits, 0.0), axis=-1, keepdims=True) for r in routes
    ]
    gates = softmax_cols(picked)
    query = mm(normed, qw_ref[...])
    heads_pairs = query.shape[1] // LANES
    tiles = [query[:, j * LANES : (j + 1) * LANES] for j in range(heads_pairs)]
    low = lane < LANES // 2
    same = col[:, 6:7] == row[0:1, :]
    place = lax.broadcasted_iota(jnp.int32, (rows, rows), 0)
    other = lax.broadcasted_iota(jnp.int32, (rows, rows), 1)
    allowed = same & ((row[1:2, :] == 1) | (place == other))
    scale = 0.125
    shares = []
    for i in range(top_attn):
        sel = jnp.where(low, pick_head(tiles, routes[i], lane), 0.0).astype(BF16)
        qs_ref[0, i] = sel
        scores = mm_nt(sel, kv) * scale
        scores = jnp.where(allowed, scores, -1e30)
        expo = jnp.exp(scores - jnp.max(scores, axis=-1, keepdims=True))
        probs = (expo * (1.0 / jnp.sum(expo, axis=-1, keepdims=True))).astype(BF16)
        probs_ref[0, i] = probs
        heads = mm(probs, kv) * gates[i]
        shares.append(jnp.where(low, pltpu.roll(heads, LANES // 2, 1), heads))
    mixed_tiles = place_heads(shares, routes, heads_pairs, lane)
    mixed = jnp.concatenate([t.astype(BF16) for t in mixed_tiles], axis=1)
    mixed_ref[...] = mixed
    mid = x + mm(mixed, proj_ref[...])
    mid_ref[...] = mid
    hat2, _ = norm_parts(mid)
    n2 = (hat2 * vec_ref[2:3, :] + vec_ref[3:4, :]).astype(BF16)
    n2_ref[...] = n2
    n2_all[pl.ds(pl.multiple_of(step * rows, rows), rows), :] = n2
    logits_ffn = mm(n2, frw_ref[...])
    gates_ffn = softmax_cols(
        [
            jnp.sum(jnp.where(lane == col[:, 4 + i : 5 + i], logits_ffn, 0.0), axis=-1, keepdims=True)
            for i in range(2)
        ]
    )
    gates_ref[...] = put_cols(gates, rows, gates_ref.shape[1])
    stop = jnp.sum(mid * vec_ref[4:5, :], axis=-1, keepdims=True) + hb_ref[0:1, 0:1]
    pull = jnp.sum(grad_ref[0].astype(F32) * (mid - x), axis=-1, keepdims=True)
    scal_ref[...] = jnp.transpose(put_cols([stop, pull] + gates_ffn, rows, LANES))[:8, :]

    @pl.when(step == pl.num_programs(0) - 1)
    def _():
        dispatch([slotrow_ref[0:1, :], slotrow_ref[1:2, :]], [n2_all], out_ref)


def attention_forward(micro, tokens, grad, col, row, slotrow, vec, hb, qw, kvr, proj, frw, slots):
    _, count, width = tokens.shape
    steps = count // SEQ
    inner = qw.shape[1]
    whole = lambda a: pl.BlockSpec(a.shape, lambda r: (0,) * a.ndim)
    out_shape = (
        jax.ShapeDtypeStruct((count, width), F32),
        jax.ShapeDtypeStruct((count, width), BF16),
        jax.ShapeDtypeStruct((count, width), BF16),
        jax.ShapeDtypeStruct((count, inner), BF16),
        jax.ShapeDtypeStruct((steps, 4, SEQ, SEQ), BF16),
        jax.ShapeDtypeStruct((steps, 4, SEQ, LANES), BF16),
        jax.ShapeDtypeStruct((count, LANES), BF16),
        jax.ShapeDtypeStruct((count, 8), F32),
        jax.ShapeDtypeStruct((8, count), F32),
        jax.ShapeDtypeStruct((slots, width), BF16),
    )
    by_row = lambda c: pl.BlockSpec((SEQ, c), lambda r: (r, 0))
    return pl.pallas_call(
        attention_forward_kernel,
        grid=(steps,),
        out_shape=out_shape,
        in_specs=[
            pl.BlockSpec((1, SEQ, width), lambda r: (micro, r, 0)),
            pl.BlockSpec((1, SEQ, width), lambda r: (micro, r, 0)),
            pl.BlockSpec((1, SEQ, 8), lambda r: (micro, r, 0)),
            pl.BlockSpec((1, 8, SEQ), lambda r: (micro, 0, r)),
            whole(slotrow), whole(vec), whole(hb), whole(qw), whole(kvr), whole(proj), whole(frw),
        ],
        out_specs=[
            by_row(width), by_row(width), by_row(width), by_row(inner),
            pl.BlockSpec((1, 4, SEQ, SEQ), lambda r: (r, 0, 0, 0)),
            pl.BlockSpec((1, 4, SEQ, LANES), lambda r: (r, 0, 0, 0)),
            by_row(LANES), by_row(8),
            pl.BlockSpec((8, SEQ), lambda r: (0, r)),
            pl.BlockSpec((slots, width), lambda r: (0, 0)),
        ],
        scratch_shapes=[pltpu.VMEM((count, width), BF16)],
        compiler_params=pltpu.CompilerParams(vmem_limit_bytes=VMEM_LIMIT),
        cost_estimate=pl.CostEstimate(
            flops=2 * count * width * (2 * inner + 256 + slots), bytes_accessed=12 << 20, transcendentals=count * 4 * SEQ
        ),
        name="attention_forward",
    )(tokens, grad, col, row, slotrow, vec, hb, qw, kvr, proj, frw)


def gelu_parts(pre):
    square = pre * pre
    inner = jnp.tanh(GELU_C * pre * (1.0 + GELU_A * square))
    return square, inner


def expert_forward_kernel(rows_ref, grad_ref, vec_ref, first_ref, second_ref, out_ref, scal_ref, total):
    part = pl.program_id(1)
    src, _, cap, width = rows_ref.shape
    rows = rows_ref[...].reshape(src * cap, width)
    pre = mm(rows, first_ref[0, 0])
    _, inner = gelu_parts(pre)
    act = (0.5 * pre * (1.0 + inner)).astype(BF16)
    res = mm(act, second_ref[0, 0])

    @pl.when(part == 0)
    def _():
        total[...] = res

    @pl.when(part > 0)
    def _():
        total[...] += res

    @pl.when(part == pl.num_programs(1) - 1)
    def _():
        halt = split_three(jnp.broadcast_to(vec_ref[4:5, :], (8, width)))
        ones = jnp.ones((8, width), BF16)
        sub8 = lax.broadcasted_iota(jnp.int32, (8, cap), 0)
        for s in range(src):
            low = total[s * cap : (s + 1) * cap, :].astype(BF16)
            out_ref[s, 0] = low
            stop = join_three(mm_nt(halt, low))
            prod = low.astype(F32) * grad_ref[s, 0].astype(F32)
            high = prod.astype(BF16)
            rest = (prod - high.astype(F32)).astype(BF16)
            pull = mm_nt(ones, high) + mm_nt(ones, rest)
            scal_ref[s, 0] = jnp.where(sub8 == 0, stop, pull)


def expert_forward(rows, grad, vec, first, second):
    src, local, cap, width = rows.shape
    parts, _, _, hid = first.shape
    spec_rows = pl.BlockSpec((src, 1, cap, width), lambda e, h: (0, e, 0, 0))
    return pl.pallas_call(
        expert_forward_kernel,
        grid=(local, parts),
        out_shape=(
            jax.ShapeDtypeStruct(rows.shape, BF16),
            jax.ShapeDtypeStruct((src, local, 8, cap), F32),
        ),
        in_specs=[
            spec_rows,
            spec_rows,
            pl.BlockSpec(vec.shape, lambda e, h: (0, 0)),
            pl.BlockSpec((1, 1, width, hid), lambda e, h: (h, e, 0, 0)),
            pl.BlockSpec((1, 1, hid, width), lambda e, h: (h, e, 0, 0)),
        ],
        out_specs=[spec_rows, pl.BlockSpec((src, 1, 8, cap), lambda e, h: (0, e, 0, 0))],
        scratch_shapes=[pltpu.VMEM((src * cap, width), F32)],
        compiler_params=pltpu.CompilerParams(vmem_limit_bytes=VMEM_LIMIT),
        cost_estimate=pl.CostEstimate(
            flops=4 * src * local * cap * width * hid * parts,
            bytes_accessed=6 * src * local * cap * width + 4 * local * parts * width * hid,
            transcendentals=src * local * cap * hid * parts,
        ),
        name="expert_forward",
    )(rows, grad, vec, first, second)


def exchange_copies(n_expert, source, target, send_sem, recv_sem, own_sem):
    me = lax.axis_index("expert")
    other = lax.axis_index("hidden")
    moves = []
    for k in range(1, n_expert):
        peer = lax.rem(me + k, n_expert)
        moves.append(
            pltpu.make_async_remote_copy(
                source.at[peer], target.at[me], send_sem.at[k - 1], recv_sem.at[k - 1],
                device_id=(peer, other), device_id_type=pl.DeviceIdType.MESH,
            )
        )
    return moves, pltpu.make_async_copy(source.at[me], target.at[me], own_sem)


def expert_backward_kernel(n_expert, add_old, *refs):
    rows_ref, grad_ref, ab_ref, vec_ref, first_ref, second_ref, away_ref = refs[:7]
    refs = refs[7:]
    if add_old:
        old_first_ref, old_second_ref = refs[:2]
        refs = refs[2:]
    gfirst_ref, gsecond_ref, out_ref, home_ref, total, gin_all, send_sem, recv_sem, own_sem = refs
    part = pl.program_id(1)
    src, _, cap, width = rows_ref.shape
    moves, own = exchange_copies(n_expert, away_ref, home_ref, send_sem, recv_sem, own_sem)

    @pl.when((pl.program_id(0) == 0) & (part == 0))
    def _():
        other = lax.axis_index("hidden")
        greet("expert", n_expert, lambda e: (e, other))
        for c in moves:
            c.start()
        own.start()

    @pl.when(part == 0)
    def _():
        for s in range(src):
            ab = ab_ref[s, 0]
            scaled = row_to_col(ab[0:1, :]) * grad_ref[s, 0].astype(F32) + row_to_col(ab[1:2, :]) * vec_ref[4:5, :]
            gin_all[s * cap : (s + 1) * cap, :] = scaled.astype(BF16)

    rows = rows_ref[...].reshape(src * cap, width)
    gin = gin_all[...]
    first = first_ref[0, 0]
    second = second_ref[0, 0]
    pre = mm(rows, first)
    gact = mm_nt(gin, second)
    square, inner = gelu_parts(pre)
    half = 0.5 * (1.0 + inner)
    act = (pre * half).astype(BF16)
    slope = half + 0.5 * pre * (1.0 - inner * inner) * (GELU_C + (3.0 * GELU_C * GELU_A) * square)
    gpre = (gact * slope).astype(BF16)
    gsecond = mm_tn(act, gin)
    gfirst = mm_tn(rows, gpre)
    if add_old:
        gsecond = gsecond + old_second_ref[0, 0].astype(F32)
        gfirst = gfirst + old_first_ref[0, 0].astype(F32)
    gsecond_ref[0, 0] = gsecond.astype(BF16)
    gfirst_ref[0, 0] = gfirst.astype(BF16)
    res = mm_nt(gpre, first)

    @pl.when(part == 0)
    def _():
        total[...] = res

    @pl.when(part > 0)
    def _():
        total[...] += res

    @pl.when(part == pl.num_programs(1) - 1)
    def _():
        out_ref[...] = total[...].astype(BF16).reshape(out_ref.shape)

    @pl.when((pl.program_id(0) == pl.num_programs(0) - 1) & (part == pl.num_programs(1) - 1))
    def _():
        for c in moves:
            c.wait()
        own.wait()


def expert_backward(n_expert, rows, grad, ab, vec, first, second, away, old):
    src, local, cap, width = rows.shape
    parts, _, _, hid = first.shape
    spec_rows = pl.BlockSpec((src, 1, cap, width), lambda e, h: (0, e, 0, 0))
    spec_first = pl.BlockSpec((1, 1, width, hid), lambda e, h: (h, e, 0, 0))
    spec_second = pl.BlockSpec((1, 1, hid, width), lambda e, h: (h, e, 0, 0))
    return pl.pallas_call(
        functools.partial(expert_backward_kernel, n_expert, bool(old)),
        grid=(local, parts),
        out_shape=(
            jax.ShapeDtypeStruct(first.shape, BF16),
            jax.ShapeDtypeStruct(second.shape, BF16),
            jax.ShapeDtypeStruct(rows.shape, BF16),
            jax.ShapeDtypeStruct(away.shape, BF16),
        ),
        in_specs=[
            spec_rows, spec_rows,
            pl.BlockSpec((src, 1, 8, cap), lambda e, h: (0, e, 0, 0)),
            pl.BlockSpec(vec.shape, lambda e, h: (0, 0)),
            spec_first, spec_second, pl.BlockSpec(memory_space=pl.ANY),
        ] + [spec_first, spec_second][: len(old)],
        out_specs=[spec_first, spec_second, spec_rows, pl.BlockSpec(memory_space=pl.ANY)],
        scratch_shapes=[
            pltpu.VMEM((src * cap, width), F32),
            pltpu.VMEM((src * cap, width), BF16),
            pltpu.SemaphoreType.DMA((n_expert - 1,)),
            pltpu.SemaphoreType.DMA((n_expert - 1,)),
            pltpu.SemaphoreType.DMA,
        ],
        compiler_params=pltpu.CompilerParams(
            vmem_limit_bytes=VMEM_LIMIT, collective_id=3 if old else 2, has_side_effects=True
        ),
        cost_estimate=pl.CostEstimate(
            flops=10 * src * local * cap * width * hid * parts,
            bytes_accessed=6 * src * local * cap * width + 8 * local * parts * width * hid,
            transcendentals=src * local * cap * hid * parts,
        ),
        name="expert_backward",
    )(rows, grad, ab, vec, first, second, away, *old)


def greet(axis, peers, make_id):
    barrier = pltpu.get_barrier_semaphore()
    me = lax.axis_index(axis)
    for k in range(1, peers):
        pl.semaphore_signal(
            barrier, inc=1, device_id=make_id(lax.rem(me + k, peers)), device_id_type=pl.DeviceIdType.MESH
        )
    pl.semaphore_wait(barrier, peers - 1)
    return me


def scalar_kernel(n_expert, scal_ref, rowsc_ref, slotrow_ref, cols_ref, ab_ref, got, sent, got2, send_sem, recv_sem, send_sem2, recv_sem2):
    local, cap = scal_ref.shape[1], scal_ref.shape[3]
    tokens = rowsc_ref.shape[1]
    other = lax.axis_index("hidden")
    make_id = lambda e: (e, other)
    me = greet("expert", n_expert, make_id)

    def copies(source, target, ssem, rsem):
        out = []
        for k in range(1, n_expert):
            peer = lax.rem(me + k, n_expert)
            out.append(
                pltpu.make_async_remote_copy(
                    source.at[peer], target.at[me], ssem.at[k - 1], rsem.at[k - 1],
                    device_id=make_id(peer), device_id_type=pl.DeviceIdType.MESH,
                )
            )
        return out

    moves = copies(scal_ref, got, send_sem, recv_sem)
    for c in moves:
        c.start()
    got[me] = scal_ref[me]
    for c in moves:
        c.wait()
    slot = [slotrow_ref[i : i + 1, :] for i in range(2)]
    spot = lax.broadcasted_iota(jnp.int32, (cap, tokens), 0)

    def onehot(expert):
        base = spot + expert * cap
        return [jnp.where(base == s, 1.0, 0.0).astype(BF16) for s in slot]

    zero = jnp.zeros((24, tokens), F32)

    def collect(expert, carry):
        values = split_three(got[lax.div(expert, local), lax.rem(expert, local)])
        return tuple(c + mm(values, p) for c, p in zip(carry, onehot(expert)))

    found = lax.fori_loop(0, n_expert * local, collect, (zero, zero))
    found = [join_three(f) for f in found]
    stop, pull, gate0, gate1 = [rowsc_ref[i : i + 1, :] for i in range(4)]
    gates = [gate0, gate1]
    yh = [f[0:1, :] for f in found]
    yg = [f[1:2, :] for f in found]
    halting = jax.nn.sigmoid(stop + gate0 * yh[0] + gate1 * yh[1])
    s = (pull + gate0 * yg[0] + gate1 * yg[1]) * halting * (1.0 - halting)
    u = [halting * g + s * h for g, h in zip(yg, yh)]
    mean = gate0 * u[0] + gate1 * u[1]
    keep = [halting, s, gate0 * (u[0] - mean), gate1 * (u[1] - mean), gate0, gate1]
    sub = lax.broadcasted_iota(jnp.int32, (LANES, tokens), 0)
    table = jnp.zeros((LANES, tokens), F32)
    for i, r in enumerate(keep):
        table = jnp.where(sub == i, r, table)
    cols_ref[...] = jnp.transpose(table)[:, :8]
    sub8 = lax.broadcasted_iota(jnp.int32, (8, tokens), 0)
    ab = [
        split_three(jnp.where(sub8 == 0, g * halting, jnp.where(sub8 == 1, g * s, 0.0))) for g in gates
    ]

    def spread(expert, carry):
        picks = onehot(expert)
        sent[lax.div(expert, local), lax.rem(expert, local)] = join_three(mm_nt(ab[0], picks[0]) + mm_nt(ab[1], picks[1]))
        return carry

    lax.fori_loop(0, n_expert * local, spread, 0)
    moves = copies(sent, got2, send_sem2, recv_sem2)
    for c in moves:
        c.start()
    got2[me] = sent[me]
    for c in moves:
        c.wait()
    ab_ref[...] = got2[...]


def scalar_step(n_expert, scal, rowsc, slotrow):
    vmem = pl.BlockSpec(memory_space=pltpu.VMEM)
    tokens = rowsc.shape[1]
    return pl.pallas_call(
        functools.partial(scalar_kernel, n_expert),
        out_shape=(jax.ShapeDtypeStruct((tokens, 8), F32), jax.ShapeDtypeStruct(scal.shape, F32)),
        in_specs=[vmem] * 3,
        out_specs=[vmem] * 2,
        scratch_shapes=[pltpu.VMEM(scal.shape, F32)] * 3 + [pltpu.SemaphoreType.DMA((n_expert - 1,))] * 4,
        compiler_params=pltpu.CompilerParams(collective_id=0, has_side_effects=True),
        cost_estimate=pl.CostEstimate(flops=10**9, bytes_accessed=1 << 20, transcendentals=tokens),
        name="scalar_step",
    )(scal, rowsc, slotrow)


def result_kernel(has_old, *refs):
    x_ref, mid_ref, ret_ref, cols_ref, slotcol_ref = refs[:5]
    result_ref, hsum_ref = refs[-2:]
    tokens, width = mid_ref.shape
    chunk = 256
    chunks = ret_ref.shape[0] // chunk
    lane = lane_iota(tokens, chunk)
    slot_c = [slotcol_ref[:, i : i + 1] for i in range(2)]

    def gather(k, carry):
        block = ret_ref[pl.ds(pl.multiple_of(k * chunk, chunk), chunk), :]
        base = lane + k * chunk
        return tuple(
            c + mm(jnp.where(base == s, 1.0, 0.0).astype(BF16), block) for c, s in zip(carry, slot_c)
        )

    zero = jnp.zeros((tokens, width), F32)
    picked = lax.fori_loop(0, chunks, gather, (zero, zero))
    halting, s = cols_ref[:, 0:1], cols_ref[:, 1:2]
    x = x_ref[0].astype(F32)
    end = mid_ref[...] + (cols_ref[:, 4:5] * picked[0] + cols_ref[:, 5:6] * picked[1])
    result_ref[0] = (x + halting * (end - x)).astype(BF16)
    sub8 = lax.broadcasted_iota(jnp.int32, (8, width), 0)
    ssum = jnp.broadcast_to(jnp.sum(s, axis=0, keepdims=True), (1, width))
    hsum_ref[...] = jnp.where(sub8 == 0, fold_rows(s * end), jnp.where(sub8 == 1, ssum, 0.0))


def result_step(micro, tokens, mid, ret, cols, slotcol, old):
    _, count, width = tokens.shape
    whole = lambda a: pl.BlockSpec(a.shape, lambda i: (0,) * a.ndim)
    part = pl.BlockSpec((1, count, width), lambda i: (micro, 0, 0))
    return pl.pallas_call(
        functools.partial(result_kernel, bool(old)),
        grid=(1,),
        out_shape=(jax.ShapeDtypeStruct(tokens.shape, BF16), jax.ShapeDtypeStruct((8, width), F32)),
        in_specs=[part] + [whole(a) for a in (mid, ret, cols, slotcol)] + [pl.BlockSpec(memory_space=pl.ANY)] * len(old),
        out_specs=[part, pl.BlockSpec((8, width), lambda i: (0, 0))],
        input_output_aliases={5: 0} if old else {},
        compiler_params=pltpu.CompilerParams(vmem_limit_bytes=VMEM_LIMIT),
        cost_estimate=pl.CostEstimate(
            flops=4 * count * ret.shape[0] * width, bytes_accessed=5 << 20, transcendentals=count
        ),
        name="result_step",
    )(tokens, mid, ret, cols, slotcol, *old)


def attention_backward_kernel(last, n_old, *refs):
    (x_ref, grad_ref, col_ref, vec_ref, qw_ref, kvr_ref, proj_ref, frw_ref,
     mid_ref, n2_ref, normed_ref, mixed_ref, probs_ref, qs_ref, kv_ref, gates_ref, slotcol_ref,
     back_ref, cols_ref) = refs[:19]
    old = refs[19 : 19 + n_old]
    gtok_ref, gq_out, gproj_out, gkvr_out, gfr_out, gvec_out = refs[19 + n_old : 25 + n_old]
    gsum, gq_ref, gproj_ref, gkvr_ref, gfr_ref, gvec_ref = refs[25 + n_old :]
    step = pl.program_id(0)
    rows, width = mid_ref.shape
    lane = lane_iota(rows)
    low = lane < LANES // 2
    col = col_ref[0]
    chunk = 256
    slot_c = [slotcol_ref[:, i : i + 1] for i in range(2)]
    lane_c = lane_iota(rows, chunk)
    accs = (gq_ref, gproj_ref, gkvr_ref, gfr_ref, gvec_ref)

    @pl.when(step == 0)
    def _():
        for k, ref in enumerate(accs):
            ref[...] = old[k][...] if old else jnp.zeros_like(ref)

    gsum[...] = jnp.zeros_like(gsum)

    def gather(k, carry):
        block = back_ref[pl.ds(pl.multiple_of(k * chunk, chunk), chunk), :]
        base = lane_c + k * chunk
        pick = jnp.where((base == slot_c[0]) | (base == slot_c[1]), 1.0, 0.0).astype(BF16)
        gsum[...] += mm(pick, block)
        return carry

    lax.fori_loop(0, back_ref.shape[0] // chunk, gather, 0)
    glog = jnp.zeros((rows, LANES), F32)
    for i in range(2):
        glog = jnp.where(lane == col[:, 4 + i : 5 + i], cols_ref[:, 2 + i : 3 + i], glog)
    glog = glog.astype(BF16)
    n2 = n2_ref[...]
    gfr_ref[...] += mm_tn(n2, glog)
    gn2 = gsum[...] + mm_nt(glog, frw_ref[...])
    hat2, rstd2 = norm_parts(mid_ref[...])
    grad = grad_ref[0].astype(F32)
    halting = cols_ref[:, 0:1]
    gend = halting * grad + cols_ref[:, 1:2] * vec_ref[4:5, :]
    gmid = gend + norm_back(hat2, rstd2, vec_ref[2:3, :], gn2)
    ggain2 = fold_rows(gn2 * hat2)
    gbias2 = fold_rows(gn2)
    gattn = gmid.astype(BF16)
    gproj_ref[...] += mm_tn(mixed_ref[...], gattn)
    gmixed = mm_nt(gattn, proj_ref[...]).astype(BF16).astype(F32)
    pairs = gmixed.shape[1] // LANES
    tiles = [gmixed[:, j * LANES : (j + 1) * LANES] for j in range(pairs)]
    kv = kv_ref[...]
    scale = 0.125
    routes = [col[:, i : i + 1] for i in range(4)]
    gkv = jnp.zeros((rows, LANES), F32)
    ggates = []
    parts = []
    for i in range(4):
        gate = gates_ref[:, i : i + 1]
        sel = pltpu.roll(pick_head(tiles, routes[i], lane), LANES // 2, 1)
        sel = jnp.where(low, 0.0, sel)
        probs = probs_ref[0, i]
        heads = mm(probs, kv)
        ggates.append(jnp.sum(heads * sel, axis=-1, keepdims=True))
        gheads = (gate * sel).astype(BF16)
        gprobs = mm_nt(gheads, kv)
        probs_f = probs.astype(F32)
        inner = jnp.sum(probs_f * gprobs, axis=-1, keepdims=True)
        gscores = (probs_f * (gprobs - inner)).astype(BF16)
        gkv = gkv + mm_tn(probs, gheads) + mm_tn(gscores, qs_ref[0, i]) * scale
        gq = mm(gscores, kv) * scale
        parts.append(jnp.where(low, gq, pltpu.roll(gq, LANES // 2, 1)))
    gtiles = place_heads(parts, routes, pairs, lane)
    gquery = jnp.concatenate([t.astype(BF16) for t in gtiles], axis=1)
    normed = normed_ref[...]
    gq_ref[...] += mm_tn(normed, gquery)
    mean = ggates[0] * gates_ref[:, 0:1]
    for i in range(1, 4):
        mean = mean + ggates[i] * gates_ref[:, i : i + 1]
    alog = jnp.zeros((rows, LANES), F32)
    for i in range(4):
        alog = jnp.where(lane == routes[i], gates_ref[:, i : i + 1] * (ggates[i] - mean), alog)
    gkvr = jnp.concatenate([gkv.astype(BF16), alog.astype(BF16)], axis=1)
    gkvr_ref[...] += mm_tn(normed, gkvr)
    gnormed = mm_nt(gquery, qw_ref[...]) + mm_nt(gkvr, kvr_ref[...])
    hat, rstd = norm_parts(x_ref[0].astype(F32))
    gtok_ref[0] = grad * (1.0 - halting) + gmid + norm_back(hat, rstd, vec_ref[0:1, :], gnormed)
    sub8 = lax.broadcasted_iota(jnp.int32, (8, width), 0)
    gvec = jnp.where(sub8 == 0, fold_rows(gnormed * hat), 0.0)
    gvec = jnp.where(sub8 == 1, fold_rows(gnormed), gvec)
    gvec = jnp.where(sub8 == 2, ggain2, gvec)
    gvec_ref[...] += jnp.where(sub8 == 3, gbias2, gvec)

    @pl.when(step == pl.num_programs(0) - 1)
    def _():
        for ref, out in zip(accs, (gq_out, gproj_out, gkvr_out, gfr_out, gvec_out)):
            out[...] = ref[...].astype(out.dtype)


def attention_backward(micro, last, tokens, grad, col, vec, qw, kvr, proj, frw, saved, back, cols, old):
    mid, n2, normed, mixed, probs, qs, kv, gates, slotcol = saved
    _, count, width = tokens.shape
    steps = count // SEQ
    inner = qw.shape[1]
    whole = lambda a: pl.BlockSpec(a.shape, lambda r: (0,) * a.ndim)
    by_row = lambda c: pl.BlockSpec((SEQ, c), lambda r: (r, 0))
    part = pl.BlockSpec((1, SEQ, width), lambda r: (micro, r, 0))
    kind = BF16 if last else F32
    out_shape = (
        jax.ShapeDtypeStruct(tokens.shape, F32),
        jax.ShapeDtypeStruct(qw.shape, kind),
        jax.ShapeDtypeStruct(proj.shape, kind),
        jax.ShapeDtypeStruct(kvr.shape, kind),
        jax.ShapeDtypeStruct(frw.shape, kind),
        jax.ShapeDtypeStruct((8, width), F32),
    )
    old_in = [old[k] for k in (1, 2, 3, 4, 5)] if old else []
    return pl.pallas_call(
        functools.partial(attention_backward_kernel, last, len(old_in) + (1 if old else 0)),
        grid=(steps,),
        out_shape=out_shape,
        in_specs=[
            part, part,
            pl.BlockSpec((1, SEQ, 8), lambda r: (micro, r, 0)),
            whole(vec), whole(qw), whole(kvr), whole(proj), whole(frw),
            by_row(width), by_row(width), by_row(width), by_row(inner),
            pl.BlockSpec((1, 4, SEQ, SEQ), lambda r: (r, 0, 0, 0)),
            pl.BlockSpec((1, 4, SEQ, LANES), lambda r: (r, 0, 0, 0)),
            by_row(LANES), by_row(8), by_row(8),
            whole(back), by_row(8),
        ] + [whole(o) for o in old_in] + [pl.BlockSpec(memory_space=pl.ANY)] * (1 if old else 0),
        out_specs=[part] + [pl.BlockSpec(o.shape, lambda r: (0, 0)) for o in out_shape[1:]],
        scratch_shapes=[
            pltpu.VMEM((SEQ, width), F32),
            pltpu.VMEM(qw.shape, F32),
            pltpu.VMEM(proj.shape, F32),
            pltpu.VMEM(kvr.shape, F32),
            pltpu.VMEM(frw.shape, F32),
            pltpu.VMEM((8, width), F32),
        ],
        input_output_aliases={24: 0} if old else {},
        compiler_params=pltpu.CompilerParams(vmem_limit_bytes=VMEM_LIMIT),
        cost_estimate=pl.CostEstimate(
            flops=2 * count * width * (4 * inner + 512 + back.shape[0]), bytes_accessed=24 << 20, transcendentals=0
        ),
        name="attention_backward",
    )(tokens, grad, col, vec, qw, kvr, proj, frw, mid, n2, normed, mixed, probs, qs, kv, gates, slotcol, back, cols,
      *old_in, *(old[:1] if old else []))


def sum_kernel(sizes, value_ref, out_ref, got, got2, part, send_sem, recv_sem, send_sem2, recv_sem2):
    n_expert, n_hidden = sizes
    e = lax.axis_index("expert")
    h = lax.axis_index("hidden")
    barrier = pltpu.get_barrier_semaphore()
    for k in range(1, n_expert):
        pl.semaphore_signal(barrier, inc=1, device_id=(lax.rem(e + k, n_expert), h), device_id_type=pl.DeviceIdType.MESH)
    for k in range(1, n_hidden):
        pl.semaphore_signal(barrier, inc=1, device_id=(e, lax.rem(h + k, n_hidden)), device_id_type=pl.DeviceIdType.MESH)
    pl.semaphore_wait(barrier, n_expert + n_hidden - 2)
    moves = []
    for k in range(1, n_expert):
        moves.append(
            pltpu.make_async_remote_copy(
                value_ref, got.at[e], send_sem.at[k - 1], recv_sem.at[k - 1],
                device_id=(lax.rem(e + k, n_expert), h), device_id_type=pl.DeviceIdType.MESH,
            )
        )
    for c in moves:
        c.start()
    got[e] = value_ref[...]
    for c in moves:
        c.wait()
    part[...] = jnp.sum(got[...], axis=0)
    moves = []
    for k in range(1, n_hidden):
        moves.append(
            pltpu.make_async_remote_copy(
                part, got2.at[h], send_sem2.at[k - 1], recv_sem2.at[k - 1],
                device_id=(e, lax.rem(h + k, n_hidden)), device_id_type=pl.DeviceIdType.MESH,
            )
        )
    for c in moves:
        c.start()
    got2[h] = part[...]
    for c in moves:
        c.wait()
    out_ref[...] = jnp.sum(got2[...], axis=0)


def sum_everywhere(sizes, value):
    vmem = pl.BlockSpec(memory_space=pltpu.VMEM)
    return pl.pallas_call(
        functools.partial(sum_kernel, sizes),
        out_shape=jax.ShapeDtypeStruct(value.shape, F32),
        in_specs=[vmem],
        out_specs=vmem,
        scratch_shapes=[
            pltpu.VMEM((sizes[0],) + value.shape, F32),
            pltpu.VMEM((sizes[1],) + value.shape, F32),
            pltpu.VMEM(value.shape, F32),
        ]
        + [pltpu.SemaphoreType.DMA((sizes[0] - 1,))] * 2
        + [pltpu.SemaphoreType.DMA((sizes[1] - 1,))] * 2,
        compiler_params=pltpu.CompilerParams(collective_id=1, has_side_effects=True),
        name="sum_everywhere",
    )(value)


def pad_lanes(a):
    return jnp.pad(a, ((0, 0), (0, LANES - a.shape[1])))


def per_device(
    tokens, grad_out, attn_routes, ffn_routes, segments, pad_mask, norm1_gain, norm1_bias, attn_router,
    query_w, key_w, value_w, attn_proj, norm2_gain, norm2_bias, ffn_router, expert_in, expert_out, halt_w, halt_b,
    *, n_expert, n_hidden,
):
    micros, count, width = tokens.shape
    experts = ffn_router.shape[1]
    capacity = 4 * count // experts
    slots = experts * capacity
    local = experts // n_expert
    first = lax.all_gather(expert_in, "hidden", axis=0, tiled=False)
    second = lax.all_gather(expert_out, "hidden", axis=0, tiled=False)
    seg = segments.reshape(micros, count)
    zeros = jnp.zeros_like(seg)
    col = jnp.concatenate([attn_routes, ffn_routes, seg[:, :, None], pad_mask[:, :, None]], axis=2)
    row = jnp.stack([seg, pad_mask, ffn_routes[:, :, 0], ffn_routes[:, :, 1], zeros, zeros, zeros, zeros], axis=1)
    none = jnp.zeros_like(halt_w)
    vec = jnp.stack([norm1_gain, norm1_bias, norm2_gain, norm2_bias, halt_w, none, none, none])
    kvr = jnp.concatenate([key_w, value_w, pad_lanes(attn_router)], axis=1)
    frw = pad_lanes(ffn_router)
    hb = jnp.broadcast_to(halt_b.reshape(1, 1), (8, LANES))

    def exchange(a):
        return lax.all_to_all(a, "expert", split_axis=0, concat_axis=0, tiled=True)

    def slotted(a):
        return exchange(a.reshape(n_expert, local * capacity, width)).reshape(n_expert, local, capacity, width)

    def returned(a):
        return exchange(a.reshape(n_expert, local * capacity, width)).reshape(slots, width)

    plan = [route_step(m, row, col, grad_out, slots, capacity) for m in range(micros)]
    far_grad = [slotted(p[2]) for p in plan]
    fwd = [
        attention_forward(m, tokens, grad_out, col, row, plan[m][0], vec, hb, query_w, kvr, attn_proj, frw, slots)
        for m in range(micros)
    ]
    arrived = [slotted(f[9]) for f in fwd]
    results = []
    cols = []
    abs_ = []
    for m in range(micros):
        y, scal = expert_forward(arrived[m], far_grad[m], vec, first, second)
        results.append(y)
        c, ab = scalar_step(n_expert, scal, fwd[m][8], plan[m][0])
        cols.append(c)
        abs_.append(ab)
    gback = []
    homes = []
    old = ()
    for m in range(micros):
        gf, gs, rows, home = expert_backward(
            n_expert, arrived[m], far_grad[m], abs_[m], vec, first, second, results[m], old
        )
        homes.append(home.reshape(slots, width))
        gback.append(returned(rows))
        old = (gf, gs)
    gfirst = lax.psum_scatter(old[0], "hidden", scatter_dimension=0, tiled=False).astype(F32)
    gsecond = lax.psum_scatter(old[1], "hidden", scatter_dimension=0, tiled=False).astype(F32)
    out = ()
    for m in range(micros):
        f = fwd[m]
        saved = f[:8] + (plan[m][1],)
        out = attention_backward(
            m, m == micros - 1, tokens, grad_out, col, vec, query_w, kvr, attn_proj, frw, saved, gback[m], cols[m], out
        )
    res = ()
    hsum = None
    for m in range(micros):
        res = result_step(m, tokens, fwd[m][0], homes[m], cols[m], plan[m][1], res[:1])
        hsum = res[1] if hsum is None else hsum + res[1]
    shared, _ = lax.optimization_barrier((tuple(out[1:5]), (gfirst, gsecond)))
    gq, gproj, gkvr, gfr = [a.astype(F32) for a in lax.psum(shared, ("expert", "hidden"))]
    small = sum_everywhere((n_expert, n_hidden), jnp.concatenate([out[5], hsum], axis=0))
    head = key_w.shape[1]
    return (
        res[0],
        out[0],
        small[0],
        small[1],
        gkvr[:, LANES : LANES + attn_router.shape[1]],
        gq,
        gkvr[:, :head],
        gkvr[:, head : 2 * head],
        gproj,
        small[2],
        small[3],
        gfr[:, :experts],
        gfirst,
        gsecond,
        small[8],
        small[9, :1],
    )


def solution(mesh):
    rows = P(None, ("expert", "hidden"), None)
    in_specs = (rows,) * 5 + (P(None, ("expert", "hidden")),) + (P(),) * 10 + (
        P("expert", None, "hidden"), P("expert", "hidden", None), P(), P(),
    )
    out_specs = (rows,) * 2 + (P(),) * 10 + (P("expert", None, "hidden"), P("expert", "hidden", None), P(), P())
    return jax.shard_map(
        functools.partial(per_device, n_expert=mesh.shape["expert"], n_hidden=mesh.shape["hidden"]),
        mesh=mesh, in_specs=in_specs, out_specs=out_specs, check_vma=False,
    )
```

```python
import functools
import math

import jax
import jax.numpy as jnp
from jax import lax
from jax.experimental import pallas as pl
from jax.experimental.pallas import tpu as pltpu
from jax.sharding import PartitionSpec as P

SEQ = 256
LANES = 128
F32 = jnp.float32
BF16 = jnp.bfloat16
GELU_C = math.sqrt(2.0 / math.pi)
GELU_A = 0.044715
VMEM_LIMIT = 60 * 1024 * 1024


def mm(left, right):
    return jnp.dot(left, right, preferred_element_type=F32)


def mm_nt(left, right):
    return lax.dot_general(left, right, (((1,), (1,)), ((), ())), preferred_element_type=F32)


def mm_tn(left, right):
    return lax.dot_general(left, right, (((0,), (0,)), ((), ())), preferred_element_type=F32)


def lane_iota(rows, lanes=LANES):
    return lax.broadcasted_iota(jnp.int32, (rows, lanes), 1)


def norm_parts(value):
    center = value - jnp.mean(value, axis=-1, keepdims=True)
    rstd = lax.rsqrt(jnp.mean(center * center, axis=-1, keepdims=True) + 1e-05)
    return center * rstd, rstd


def norm_back(hat, rstd, gain, grad):
    scaled = grad * gain
    first = jnp.mean(scaled, axis=-1, keepdims=True)
    second = jnp.mean(scaled * hat, axis=-1, keepdims=True)
    return rstd * (scaled - first - hat * second)


def fold_rows(value):
    return jnp.sum(value, axis=0, keepdims=True)


def pick_head(tiles, route, lane):
    pair = lax.shift_right_logical(route, 1)
    out = tiles[0]
    for j in range(1, len(tiles)):
        out = jnp.where(pair == j, tiles[j], out)
    odd = (route & 1) == 1
    return jnp.where(odd, pltpu.roll(out, LANES // 2, 1), out)


def place_heads(parts, routes, count, lane):
    half = lax.shift_right_logical(lane, 6)
    kept = [jnp.where(half == (r & 1), p, 0.0) for p, r in zip(parts, routes)]
    pairs = [lax.shift_right_logical(r, 1) for r in routes]
    tiles = []
    for j in range(count):
        total = jnp.where(pairs[0] == j, kept[0], 0.0)
        for k, p in zip(kept[1:], pairs[1:]):
            total = total + jnp.where(p == j, k, 0.0)
        tiles.append(total)
    return tiles


def softmax_cols(cols):
    top = functools.reduce(jnp.maximum, cols)
    expo = [jnp.exp(c - top) for c in cols]
    total = functools.reduce(jnp.add, expo)
    return [e / total for e in expo]


def put_cols(cols, rows, width):
    lane = lane_iota(rows, width)
    out = jnp.zeros((rows, width), cols[0].dtype)
    for i, c in enumerate(cols):
        out = jnp.where(lane == i, c, out)
    return out


def split_three(value):
    high = value.astype(BF16)
    rest = value - high.astype(F32)
    middle = rest.astype(BF16)
    last = (rest - middle.astype(F32)).astype(BF16)
    return jnp.concatenate([high.astype(F32), middle.astype(F32), last.astype(F32)], axis=0).astype(BF16)


def join_three(value):
    n = value.shape[0] // 3
    return value[:n] + value[n : 2 * n] + value[2 * n :]


def row_to_col(row):
    n = row.shape[1]
    place = lax.broadcasted_iota(jnp.int32, (n, n), 0)
    other = lax.broadcasted_iota(jnp.int32, (n, n), 1)
    return jnp.sum(jnp.where(place == other, row, 0.0), axis=-1, keepdims=True)


def dispatch(slot_rows, values, out_ref):
    chunk = 256
    tokens = values[0].shape[0]
    spot = lax.broadcasted_iota(jnp.int32, (chunk, tokens), 0)

    def body(k, carry):
        base = spot + k * chunk
        if len(values) == 1:
            pick = jnp.where((base == slot_rows[0]) | (base == slot_rows[1]), 1.0, 0.0).astype(BF16)
            out = mm(pick, values[0][...])
        else:
            out = mm(jnp.where(base == slot_rows[0], 1.0, 0.0).astype(BF16), values[0][...])
            out = out + mm(jnp.where(base == slot_rows[1], 1.0, 0.0).astype(BF16), values[1][...])
        out_ref[pl.ds(pl.multiple_of(k * chunk, chunk), chunk), :] = out.astype(BF16)
        return carry

    lax.fori_loop(0, out_ref.shape[0] // chunk, body, 0)


def group_of():
    size = lax.axis_size("expert") // 2
    e = lax.axis_index("expert")
    me = lax.rem(e, size)
    return me, size, e - me


def group_greet():
    me, size, base = group_of()
    other = lax.axis_index("hidden")
    barrier = pltpu.get_barrier_semaphore()
    for k in range(1, size):
        pl.semaphore_signal(
            barrier, inc=1, device_id=(base + lax.rem(me + k, size), other), device_id_type=pl.DeviceIdType.MESH
        )
    pl.semaphore_wait(barrier, size - 1)


def group_copies(source, target, send_sem, recv_sem):
    me, size, base = group_of()
    other = lax.axis_index("hidden")
    moves = []
    for k in range(1, size):
        peer = lax.rem(me + k, size)
        moves.append(
            pltpu.make_async_remote_copy(
                source.at[peer], target.at[me], send_sem.at[k - 1], recv_sem.at[k - 1],
                device_id=(base + peer, other), device_id_type=pl.DeviceIdType.MESH,
            )
        )
    return moves


def at_step(which):
    found = True
    for axis, size in enumerate(which[1]):
        here = pl.program_id(axis) == (0 if which[0] == 0 else size - 1)
        found = here if found is True else found & here
    return found


def run_kernel(kernel, args, in_specs, out_shape, out_specs, scratch, grid, name, cost, moving=(), cid=None, aliases=None):
    n_in, n_out, n_move = len(args), len(out_shape), len(moving)
    peers = lax.axis_size("expert") // 2 - 1
    hbm = pl.BlockSpec(memory_space=pl.ANY)

    def body(*refs):
        ins, sources = refs[:n_in], refs[n_in : n_in + n_move]
        outs = refs[n_in + n_move : n_in + n_move + n_out]
        targets = refs[n_in + n_move + n_out : n_in + 2 * n_move + n_out]
        rest = refs[n_in + 2 * n_move + n_out :]
        sems = rest[len(scratch) :]
        moves, owns = [], []
        me = group_of()[0]
        pairs = []
        for a, b in zip(sources, targets):
            pairs += [(a, b)] if len(a.shape) == 4 else [(a.at[i], b.at[i]) for i in range(a.shape[0])]
        for i, (a, b) in enumerate(pairs):
            moves += group_copies(a, b, sems[3 * i], sems[3 * i + 1])
            owns.append(pltpu.make_async_copy(a.at[me], b.at[me], sems[3 * i + 2]))

        if moving:

            @pl.when(at_step((0, grid)))
            def _():
                group_greet()
                for c in moves + owns:
                    c.start()

        kernel(*ins, *outs, *rest[: len(scratch)])

        if moving:

            @pl.when(at_step((1, grid)))
            def _():
                for c in moves + owns:
                    c.wait()

    sems = []
    for _ in range(sum(1 if a.ndim == 4 else a.shape[0] for a in moving)):
        sems += [pltpu.SemaphoreType.DMA((peers,)), pltpu.SemaphoreType.DMA((peers,)), pltpu.SemaphoreType.DMA]
    more = dict(collective_id=cid, has_side_effects=True) if moving else {}
    return pl.pallas_call(
        body,
        grid=grid,
        out_shape=tuple(out_shape) + tuple(jax.ShapeDtypeStruct(a.shape, a.dtype) for a in moving),
        in_specs=list(in_specs) + [hbm] * n_move,
        out_specs=list(out_specs) + [hbm] * n_move,
        scratch_shapes=list(scratch) + sems,
        input_output_aliases=aliases or {},
        compiler_params=pltpu.CompilerParams(vmem_limit_bytes=VMEM_LIMIT, **more),
        cost_estimate=cost,
        name=name,
    )(*args, *moving)


def route_kernel(row_ref, grad_ref, slotrow_ref, slotcol_ref, out_ref):
    tokens = grad_ref.shape[1]
    before = lax.broadcasted_iota(jnp.int32, (tokens, tokens), 0)
    after = lax.broadcasted_iota(jnp.int32, (tokens, tokens), 1)
    upper = jnp.where(before < after, 1.0, 0.0).astype(BF16)
    sub = lax.broadcasted_iota(jnp.int32, (LANES, tokens), 0)
    row = row_ref[0]
    named = [jnp.where(sub == row[2 + i : 3 + i, :], 1.0, 0.0) for i in range(2)]
    rank = mm((named[0] + named[1]).astype(BF16), upper)
    slots = [fold_rows(named[i] * rank).astype(jnp.int32) + row[4 + i : 5 + i, :] for i in range(2)]
    sub8 = lax.broadcasted_iota(jnp.int32, (8, tokens), 0)
    slotrow_ref[0] = jnp.where(sub8 == 0, slots[0], slots[1])
    table = jnp.where(sub == 0, slots[0].astype(F32), slots[1].astype(F32))
    slotcol_ref[0] = jnp.transpose(table)[:, :8].astype(jnp.int32)
    dispatch(slots, [grad_ref.at[0]], out_ref.at[0])


def route_step(row, grad, slots):
    micros, count, width = grad.shape
    out_shape = (
        jax.ShapeDtypeStruct((micros, 8, count), jnp.int32),
        jax.ShapeDtypeStruct((micros, count, 8), jnp.int32),
        jax.ShapeDtypeStruct((micros, slots, width), BF16),
    )
    spec = lambda a, b: pl.BlockSpec((1, a, b), lambda m: (m, 0, 0))
    return run_kernel(
        route_kernel, (row, grad), [spec(8, count), spec(count, width)], out_shape,
        [spec(8, count), spec(count, 8), spec(slots, width)], (), (micros,), "route_step",
        pl.CostEstimate(flops=4 * count * width * slots, bytes_accessed=6 << 20, transcendentals=0),
    )


def attention_forward_kernel(
    x_ref, grad_ref, col_ref, row_ref, slotrow_ref, vec_ref, hb_ref, qw_ref, kvr_ref, proj_ref, frw_ref,
    mid_ref, n2_ref, normed_ref, mixed_ref, probs_ref, qs_ref, kv_ref, gates_ref, scal_ref, out_ref,
    n2_all,
):
    step = pl.program_id(0)
    rows = x_ref.shape[1]
    top_attn = 4
    lane = lane_iota(rows)
    x = x_ref[0].astype(F32)
    col = col_ref[0]
    row = row_ref[0]
    hat, _ = norm_parts(x)
    normed = (hat * vec_ref[0:1, :] + vec_ref[1:2, :]).astype(BF16)
    normed_ref[...] = normed
    kvr = mm(normed, kvr_ref[...])
    kv = kvr[:, :LANES].astype(BF16)
    kv_ref[...] = kv
    logits = kvr[:, LANES:]
    routes = [col[:, i : i + 1] for i in range(top_attn)]
    picked = [
        jnp.sum(jnp.where(lane == r, logits, 0.0), axis=-1, keepdims=True) for r in routes
    ]
    gates = softmax_cols(picked)
    query = mm(normed, qw_ref[...])
    heads_pairs = query.shape[1] // LANES
    tiles = [query[:, j * LANES : (j + 1) * LANES] for j in range(heads_pairs)]
    low = lane < LANES // 2
    same = col[:, 6:7] == row[0:1, :]
    place = lax.broadcasted_iota(jnp.int32, (rows, rows), 0)
    other = lax.broadcasted_iota(jnp.int32, (rows, rows), 1)
    allowed = same & ((row[1:2, :] == 1) | (place == other))
    scale = 0.125
    shares = []
    for i in range(top_attn):
        sel = jnp.where(low, pick_head(tiles, routes[i], lane), 0.0).astype(BF16)
        qs_ref[0, i] = sel
        scores = mm_nt(sel, kv) * scale
        scores = jnp.where(allowed, scores, -1e30)
        expo = jnp.exp(scores - jnp.max(scores, axis=-1, keepdims=True))
        probs = (expo * (1.0 / jnp.sum(expo, axis=-1, keepdims=True))).astype(BF16)
        probs_ref[0, i] = probs
        heads = mm(probs, kv) * gates[i]
        shares.append(jnp.where(low, pltpu.roll(heads, LANES // 2, 1), heads))
    mixed_tiles = place_heads(shares, routes, heads_pairs, lane)
    mixed = jnp.concatenate([t.astype(BF16) for t in mixed_tiles], axis=1)
    mixed_ref[...] = mixed
    mid = x + mm(mixed, proj_ref[...])
    mid_ref[...] = mid
    hat2, _ = norm_parts(mid)
    n2 = (hat2 * vec_ref[2:3, :] + vec_ref[3:4, :]).astype(BF16)
    n2_ref[...] = n2
    n2_all[pl.ds(pl.multiple_of(step * rows, rows), rows), :] = n2
    logits_ffn = mm(n2, frw_ref[...])
    gates_ffn = softmax_cols(
        [
            jnp.sum(jnp.where(lane == col[:, 4 + i : 5 + i], logits_ffn, 0.0), axis=-1, keepdims=True)
            for i in range(2)
        ]
    )
    gates_ref[...] = put_cols(gates, rows, gates_ref.shape[1])
    stop = jnp.sum(mid * vec_ref[4:5, :], axis=-1, keepdims=True) + hb_ref[0:1, 0:1]
    pull = jnp.sum(grad_ref[0].astype(F32) * (mid - x), axis=-1, keepdims=True)
    scal_ref[...] = jnp.transpose(put_cols([stop, pull] + gates_ffn, rows, LANES))[:8, :]

    @pl.when(step == pl.num_programs(0) - 1)
    def _():
        dispatch([slotrow_ref[0, 0:1, :], slotrow_ref[0, 1:2, :]], [n2_all], out_ref)


def attention_forward(micro, tokens, grad, col, row, slotrow, vec, hb, qw, kvr, proj, frw, slots, moving, cid):
    _, count, width = tokens.shape
    steps = count // SEQ
    inner = qw.shape[1]
    whole = lambda a: pl.BlockSpec(a.shape, lambda r: (0,) * a.ndim)
    out_shape = (
        jax.ShapeDtypeStruct((count, width), F32),
        jax.ShapeDtypeStruct((count, width), BF16),
        jax.ShapeDtypeStruct((count, width), BF16),
        jax.ShapeDtypeStruct((count, inner), BF16),
        jax.ShapeDtypeStruct((steps, 4, SEQ, SEQ), BF16),
        jax.ShapeDtypeStruct((steps, 4, SEQ, LANES), BF16),
        jax.ShapeDtypeStruct((count, LANES), BF16),
        jax.ShapeDtypeStruct((count, 8), F32),
        jax.ShapeDtypeStruct((8, count), F32),
        jax.ShapeDtypeStruct((slots, width), BF16),
    )
    by_row = lambda c: pl.BlockSpec((SEQ, c), lambda r: (r, 0))
    in_specs = [
        pl.BlockSpec((1, SEQ, width), lambda r: (micro, r, 0)),
        pl.BlockSpec((1, SEQ, width), lambda r: (micro, r, 0)),
        pl.BlockSpec((1, SEQ, 8), lambda r: (micro, r, 0)),
        pl.BlockSpec((1, 8, SEQ), lambda r: (micro, 0, r)),
        pl.BlockSpec((1, 8, count), lambda r: (micro, 0, 0)),
        whole(vec), whole(hb), whole(qw), whole(kvr), whole(proj), whole(frw),
    ]
    out_specs = [
        by_row(width), by_row(width), by_row(width), by_row(inner),
        pl.BlockSpec((1, 4, SEQ, SEQ), lambda r: (r, 0, 0, 0)),
        pl.BlockSpec((1, 4, SEQ, LANES), lambda r: (r, 0, 0, 0)),
        by_row(LANES), by_row(8),
        pl.BlockSpec((8, SEQ), lambda r: (0, r)),
        pl.BlockSpec((slots, width), lambda r: (0, 0)),
    ]
    return run_kernel(
        attention_forward_kernel, (tokens, grad, col, row, slotrow, vec, hb, qw, kvr, proj, frw), in_specs,
        out_shape, out_specs, [pltpu.VMEM((count, width), BF16)], (steps,), "attention_forward",
        pl.CostEstimate(
            flops=2 * count * width * (2 * inner + 256 + slots), bytes_accessed=12 << 20, transcendentals=count * 4 * SEQ
        ),
        moving, cid,
    )


def gelu_parts(pre):
    square = pre * pre
    inner = jnp.tanh(GELU_C * pre * (1.0 + GELU_A * square))
    return square, inner


def expert_forward_kernel(rows0_ref, rows1_ref, first_ref, second_ref, out0_ref, out1_ref, total):
    part = pl.program_id(1)
    _, src, _, cap, width = rows0_ref.shape
    half = src * cap
    rows = jnp.concatenate([r[...].reshape(half, width) for r in (rows0_ref, rows1_ref)], axis=0)
    pre = mm(rows, first_ref[0, 0])
    _, inner = gelu_parts(pre)
    act = (0.5 * pre * (1.0 + inner)).astype(BF16)
    res = mm(act, second_ref[0, 0])

    @pl.when(part == 0)
    def _():
        total[...] = res

    @pl.when(part > 0)
    def _():
        total[...] += res

    @pl.when(part == pl.num_programs(1) - 1)
    def _():
        out0_ref[...] = total[:half, :].astype(BF16).reshape(out0_ref.shape)
        out1_ref[...] = total[half:, :].astype(BF16).reshape(out1_ref.shape)


def expert_forward(kind, rows, first, second, moving, cid):
    _, src, local, cap, width = rows[0].shape
    parts, _, _, hid = first.shape
    spec_in = pl.BlockSpec((1, src, 1, cap, width), lambda e, h: (kind, 0, e, 0, 0))
    spec_rows = pl.BlockSpec((src, 1, cap, width), lambda e, h: (0, e, 0, 0))
    work = 2 * src * local * cap * width * hid * parts
    return run_kernel(
        expert_forward_kernel, (*rows, first, second),
        [
            spec_in, spec_in,
            pl.BlockSpec((1, 1, width, hid), lambda e, h: (h, e, 0, 0)),
            pl.BlockSpec((1, 1, hid, width), lambda e, h: (h, e, 0, 0)),
        ],
        [jax.ShapeDtypeStruct(r.shape[1:], BF16) for r in rows], [spec_rows] * 2,
        [pltpu.VMEM((2 * src * cap, width), F32)], (local, parts), "expert_forward",
        pl.CostEstimate(flops=4 * work, bytes_accessed=24 << 20, transcendentals=work // width), moving, cid,
    )


def reading_kernel(*refs):
    outs, grads = refs[:4], refs[4:8]
    vec_ref, scal_ref = refs[8:]
    src, _, cap, width = outs[0].shape
    halt = split_three(jnp.broadcast_to(vec_ref[4:5, :], (8, width)))
    ones = jnp.ones((8, width), BF16)
    sub8 = lax.broadcasted_iota(jnp.int32, (8, cap), 0)
    for kind in range(2):
        for m in range(2):
            for s in range(src):
                low = outs[2 * kind + m][s, 0]
                stop = join_three(mm_nt(halt, low))
                prod = low.astype(F32) * grads[2 * kind + m][0, s, 0].astype(F32)
                high = prod.astype(BF16)
                rest = (prod - high.astype(F32)).astype(BF16)
                pull = mm_nt(ones, high) + mm_nt(ones, rest)
                scal_ref[s, m, kind, 0] = jnp.where(sub8 == 0, stop, pull)


def reading_step(outs, grads, vec):
    src, local, cap, width = outs[0].shape
    spec_rows = pl.BlockSpec((src, 1, cap, width), lambda e: (0, e, 0, 0))
    spec_grad = lambda kind: pl.BlockSpec((1, src, 1, cap, width), lambda e: (kind, 0, e, 0, 0))
    return run_kernel(
        reading_kernel, (*outs, *grads, *grads, vec),
        [spec_rows] * 4 + [spec_grad(0)] * 2 + [spec_grad(1)] * 2 + [pl.BlockSpec(vec.shape, lambda e: (0, 0))],
        [jax.ShapeDtypeStruct((src, 2, 2, local, 8, cap), F32)],
        [pl.BlockSpec((src, 2, 2, 1, 8, cap), lambda e: (0, 0, 0, e, 0, 0))], (), (local,), "reading_step",
        pl.CostEstimate(flops=10**9, bytes_accessed=8 << 20, transcendentals=0),
    )[0].reshape(src, 2, 2 * local, 8, cap)


def expert_backward_kernel(
    rows0_ref, rows1_ref, grad0_ref, grad1_ref, ab_ref, vec_ref, first_ref, second_ref,
    gfirst_ref, gsecond_ref, out0_ref, out1_ref, total, gin_all,
):
    part = pl.program_id(1)
    _, src, _, cap, width = rows0_ref.shape
    half = src * cap

    @pl.when(part == 0)
    def _():
        for m, grad_ref in enumerate((grad0_ref, grad1_ref)):
            for s in range(src):
                ab = ab_ref[s, m, 0]
                scaled = row_to_col(ab[0:1, :]) * grad_ref[0, s, 0].astype(F32) + row_to_col(ab[1:2, :]) * vec_ref[4:5, :]
                gin_all[m * half + s * cap : m * half + (s + 1) * cap, :] = scaled.astype(BF16)

    rows = jnp.concatenate([r[...].reshape(half, width) for r in (rows0_ref, rows1_ref)], axis=0)
    gin = gin_all[...]
    first = first_ref[0, 0]
    second = second_ref[0, 0]
    pre = mm(rows, first)
    gact = mm_nt(gin, second)
    square, inner = gelu_parts(pre)
    part_one = 0.5 * (1.0 + inner)
    act = (pre * part_one).astype(BF16)
    slope = part_one + 0.5 * pre * (1.0 - inner * inner) * (GELU_C + (3.0 * GELU_C * GELU_A) * square)
    gpre = (gact * slope).astype(BF16)
    gsecond_ref[0, 0] = mm_tn(act, gin).astype(BF16)
    gfirst_ref[0, 0] = mm_tn(rows, gpre).astype(BF16)
    res = mm_nt(gpre, first)

    @pl.when(part == 0)
    def _():
        total[...] = res

    @pl.when(part > 0)
    def _():
        total[...] += res

    @pl.when(part == pl.num_programs(1) - 1)
    def _():
        out0_ref[...] = total[:half, :].astype(BF16).reshape(out0_ref.shape)
        out1_ref[...] = total[half:, :].astype(BF16).reshape(out1_ref.shape)


def expert_backward(kind, rows, grads, ab, vec, first, second, moving, cid):
    _, src, local, cap, width = rows[0].shape
    parts, _, _, hid = first.shape
    spec_in = pl.BlockSpec((1, src, 1, cap, width), lambda e, h: (kind, 0, e, 0, 0))
    spec_rows = pl.BlockSpec((src, 1, cap, width), lambda e, h: (0, e, 0, 0))
    spec_first = pl.BlockSpec((1, 1, width, hid), lambda e, h: (h, e, 0, 0))
    spec_second = pl.BlockSpec((1, 1, hid, width), lambda e, h: (h, e, 0, 0))
    work = 2 * src * local * cap * width * hid * parts
    return run_kernel(
        expert_backward_kernel, (*rows, *grads, ab, vec, first, second),
        [spec_in] * 4
        + [pl.BlockSpec((src, 2, 1, 8, cap), lambda e, h: (0, 0, kind * local + e, 0, 0)), pl.BlockSpec(vec.shape, lambda e, h: (0, 0))]
        + [spec_first, spec_second],
        [jax.ShapeDtypeStruct(first.shape, BF16), jax.ShapeDtypeStruct(second.shape, BF16)]
        + [jax.ShapeDtypeStruct(r.shape[1:], BF16) for r in rows],
        [spec_first, spec_second, spec_rows, spec_rows],
        [pltpu.VMEM((2 * src * cap, width), F32), pltpu.VMEM((2 * src * cap, width), BF16)],
        (local, parts), "expert_backward",
        pl.CostEstimate(flops=10 * work, bytes_accessed=48 << 20, transcendentals=work // width), moving, cid,
    )


def scalar_kernel(scal_ref, rowsc0_ref, rowsc1_ref, slotrow_ref, cols_ref, ab_ref, got, sent, got2, send_sem, recv_sem, send_sem2, recv_sem2):
    src, micros, local, _, cap = scal_ref.shape
    tokens = rowsc0_ref.shape[1]
    me = group_of()[0]
    group_greet()
    moves = group_copies(scal_ref, got, send_sem, recv_sem)
    for c in moves:
        c.start()
    got[me] = scal_ref[me]
    for c in moves:
        c.wait()
    spot = lax.broadcasted_iota(jnp.int32, (cap, tokens), 0)
    sub = lax.broadcasted_iota(jnp.int32, (LANES, tokens), 0)
    sub8 = lax.broadcasted_iota(jnp.int32, (8, tokens), 0)
    for m, rowsc_ref in enumerate((rowsc0_ref, rowsc1_ref)):
        slot = [slotrow_ref[m, i : i + 1, :] for i in range(2)]

        def onehot(expert):
            per = local // 2
            which = lax.rem(expert, local)
            base = lax.div(which, per) * (src * per) + lax.div(expert, local) * per + lax.rem(which, per)
            base = spot + base * cap
            return [jnp.where(base == s, 1.0, 0.0).astype(BF16) for s in slot]

        zero = jnp.zeros((24, tokens), F32)

        def collect(expert, carry):
            values = split_three(got[lax.div(expert, local), m, lax.rem(expert, local)])
            return tuple(c + mm(values, p) for c, p in zip(carry, onehot(expert)))

        found = lax.fori_loop(0, src * local, collect, (zero, zero))
        found = [join_three(f) for f in found]
        stop, pull, gate0, gate1 = [rowsc_ref[i : i + 1, :] for i in range(4)]
        gates = [gate0, gate1]
        yh = [f[0:1, :] for f in found]
        yg = [f[1:2, :] for f in found]
        halting = jax.nn.sigmoid(stop + gate0 * yh[0] + gate1 * yh[1])
        s = (pull + gate0 * yg[0] + gate1 * yg[1]) * halting * (1.0 - halting)
        u = [halting * g + s * h for g, h in zip(yg, yh)]
        mean = gate0 * u[0] + gate1 * u[1]
        keep = [halting, s, gate0 * (u[0] - mean), gate1 * (u[1] - mean), gate0, gate1]
        table = jnp.zeros((LANES, tokens), F32)
        for i, r in enumerate(keep):
            table = jnp.where(sub == i, r, table)
        cols_ref[m] = jnp.transpose(table)[:, :8]
        ab = [split_three(jnp.where(sub8 == 0, g * halting, jnp.where(sub8 == 1, g * s, 0.0))) for g in gates]

        def spread(expert, carry):
            picks = onehot(expert)
            sent[lax.div(expert, local), m, lax.rem(expert, local)] = join_three(
                mm_nt(ab[0], picks[0]) + mm_nt(ab[1], picks[1])
            )
            return carry

        lax.fori_loop(0, src * local, spread, 0)
    moves = group_copies(sent, got2, send_sem2, recv_sem2)
    for c in moves:
        c.start()
    got2[me] = sent[me]
    for c in moves:
        c.wait()
    ab_ref[...] = got2[...]


def scalar_step(scal, rowsc, slotrow):
    vmem = pl.BlockSpec(memory_space=pltpu.VMEM)
    tokens = rowsc[0].shape[1]
    peers = scal.shape[0] - 1
    return pl.pallas_call(
        scalar_kernel,
        out_shape=(jax.ShapeDtypeStruct((2, tokens, 8), F32), jax.ShapeDtypeStruct(scal.shape, F32)),
        in_specs=[vmem] * 4,
        out_specs=[vmem] * 2,
        scratch_shapes=[pltpu.VMEM(scal.shape, F32)] * 3 + [pltpu.SemaphoreType.DMA((peers,))] * 4,
        compiler_params=pltpu.CompilerParams(collective_id=0, has_side_effects=True),
        cost_estimate=pl.CostEstimate(flops=10**9, bytes_accessed=1 << 20, transcendentals=tokens),
        name="scalar_step",
    )(scal, *rowsc, slotrow)


def result_kernel(has_old, *refs):
    x_ref, mid_ref, near_ref, far_ref, cols_ref, slotcol_ref = refs[:6]
    result_ref, hsum_ref = refs[-2:]
    tokens, width = mid_ref.shape
    chunk = 256
    chunks = near_ref.shape[0] // chunk
    lane = lane_iota(tokens, chunk)
    slot_c = [slotcol_ref[0, :, i : i + 1] for i in range(2)]

    def gather(k, carry):
        for kind, ref in enumerate((near_ref, far_ref)):
            block = ref[pl.ds(pl.multiple_of(k * chunk, chunk), chunk), :]
            base = lane + (k + kind * chunks) * chunk
            carry = tuple(
                c + mm(jnp.where(base == s, 1.0, 0.0).astype(BF16), block) for c, s in zip(carry, slot_c)
            )
        return carry

    zero = jnp.zeros((tokens, width), F32)
    picked = lax.fori_loop(0, chunks, gather, (zero, zero))
    cols = cols_ref[0]
    halting, s = cols[:, 0:1], cols[:, 1:2]
    x = x_ref[0].astype(F32)
    end = mid_ref[...] + (cols[:, 4:5] * picked[0] + cols[:, 5:6] * picked[1])
    result_ref[0] = (x + halting * (end - x)).astype(BF16)
    sub8 = lax.broadcasted_iota(jnp.int32, (8, width), 0)
    ssum = jnp.broadcast_to(jnp.sum(s, axis=0, keepdims=True), (1, width))
    hsum_ref[...] = jnp.where(sub8 == 0, fold_rows(s * end), jnp.where(sub8 == 1, ssum, 0.0))


def result_step(micro, tokens, mid, near, far, cols, slotcol, old, moving, cid):
    _, count, width = tokens.shape
    whole = lambda a: pl.BlockSpec(a.shape, lambda i: (0,) * a.ndim)
    part = pl.BlockSpec((1, count, width), lambda i: (micro, 0, 0))
    cols_spec = pl.BlockSpec((1, count, 8), lambda i: (micro, 0, 0))
    return run_kernel(
        functools.partial(result_kernel, bool(old)), (tokens, mid, near, far, cols, slotcol, *old),
        [part, whole(mid), whole(near), whole(far), cols_spec, cols_spec] + [pl.BlockSpec(memory_space=pl.ANY)] * len(old),
        (jax.ShapeDtypeStruct(tokens.shape, BF16), jax.ShapeDtypeStruct((8, width), F32)),
        [part, pl.BlockSpec((8, width), lambda i: (0, 0))], (), (1,), "result_step",
        pl.CostEstimate(
            flops=8 * count * near.shape[0] * width, bytes_accessed=5 << 20, transcendentals=count
        ),
        moving, cid, {6: 0} if old else None,
    )


def attention_backward_kernel(last, n_old, *refs):
    (x_ref, grad_ref, col_ref, vec_ref, qw_ref, kvr_ref, proj_ref, frw_ref,
     mid_ref, n2_ref, normed_ref, mixed_ref, probs_ref, qs_ref, kv_ref, gates_ref, slotcol_ref,
     near_ref, far_ref, cols_ref) = refs[:20]
    old = refs[20 : 20 + n_old]
    gtok_ref = refs[20 + n_old]
    outs = refs[21 + n_old : -6]
    gsum, gq_ref, gproj_ref, gkvr_ref, gfr_ref, gvec_ref = refs[-6:]
    step = pl.program_id(0)
    rows, width = mid_ref.shape
    lane = lane_iota(rows)
    low = lane < LANES // 2
    col = col_ref[0]
    chunk = 256
    cols = cols_ref[0]
    slot_c = [slotcol_ref[0, :, i : i + 1] for i in range(2)]
    lane_c = lane_iota(rows, chunk)
    accs = (gq_ref, gproj_ref, gkvr_ref, gfr_ref, gvec_ref)

    @pl.when(step == 0)
    def _():
        for k, ref in enumerate(accs):
            ref[...] = old[k][...] if old else jnp.zeros_like(ref)

    gsum[...] = jnp.zeros_like(gsum)

    chunks = near_ref.shape[0] // chunk

    def gather(k, carry):
        for kind, ref in enumerate((near_ref, far_ref)):
            block = ref[pl.ds(pl.multiple_of(k * chunk, chunk), chunk), :]
            base = lane_c + (k + kind * chunks) * chunk
            pick = jnp.where((base == slot_c[0]) | (base == slot_c[1]), 1.0, 0.0).astype(BF16)
            gsum[...] += mm(pick, block)
        return carry

    lax.fori_loop(0, chunks, gather, 0)
    glog = jnp.zeros((rows, LANES), F32)
    for i in range(2):
        glog = jnp.where(lane == col[:, 4 + i : 5 + i], cols[:, 2 + i : 3 + i], glog)
    glog = glog.astype(BF16)
    n2 = n2_ref[...]
    gfr_ref[...] += mm_tn(n2, glog)
    gn2 = gsum[...] + mm_nt(glog, frw_ref[...])
    hat2, rstd2 = norm_parts(mid_ref[...])
    grad = grad_ref[0].astype(F32)
    halting = cols[:, 0:1]
    gend = halting * grad + cols[:, 1:2] * vec_ref[4:5, :]
    gmid = gend + norm_back(hat2, rstd2, vec_ref[2:3, :], gn2)
    ggain2 = fold_rows(gn2 * hat2)
    gbias2 = fold_rows(gn2)
    gattn = gmid.astype(BF16)
    gproj_ref[...] += mm_tn(mixed_ref[...], gattn)
    gmixed = mm_nt(gattn, proj_ref[...]).astype(BF16).astype(F32)
    pairs = gmixed.shape[1] // LANES
    tiles = [gmixed[:, j * LANES : (j + 1) * LANES] for j in range(pairs)]
    kv = kv_ref[...]
    scale = 0.125
    routes = [col[:, i : i + 1] for i in range(4)]
    gkv = jnp.zeros((rows, LANES), F32)
    ggates = []
    parts = []
    for i in range(4):
        gate = gates_ref[:, i : i + 1]
        sel = pltpu.roll(pick_head(tiles, routes[i], lane), LANES // 2, 1)
        sel = jnp.where(low, 0.0, sel)
        probs = probs_ref[0, i]
        heads = mm(probs, kv)
        ggates.append(jnp.sum(heads * sel, axis=-1, keepdims=True))
        gheads = (gate * sel).astype(BF16)
        gprobs = mm_nt(gheads, kv)
        probs_f = probs.astype(F32)
        inner = jnp.sum(probs_f * gprobs, axis=-1, keepdims=True)
        gscores = (probs_f * (gprobs - inner)).astype(BF16)
        gkv = gkv + mm_tn(probs, gheads) + mm_tn(gscores, qs_ref[0, i]) * scale
        gq = mm(gscores, kv) * scale
        parts.append(jnp.where(low, gq, pltpu.roll(gq, LANES // 2, 1)))
    gtiles = place_heads(parts, routes, pairs, lane)
    gquery = jnp.concatenate([t.astype(BF16) for t in gtiles], axis=1)
    normed = normed_ref[...]
    gq_ref[...] += mm_tn(normed, gquery)
    mean = ggates[0] * gates_ref[:, 0:1]
    for i in range(1, 4):
        mean = mean + ggates[i] * gates_ref[:, i : i + 1]
    alog = jnp.zeros((rows, LANES), F32)
    for i in range(4):
        alog = jnp.where(lane == routes[i], gates_ref[:, i : i + 1] * (ggates[i] - mean), alog)
    gkvr = jnp.concatenate([gkv.astype(BF16), alog.astype(BF16)], axis=1)
    gkvr_ref[...] += mm_tn(normed, gkvr)
    gnormed = mm_nt(gquery, qw_ref[...]) + mm_nt(gkvr, kvr_ref[...])
    hat, rstd = norm_parts(x_ref[0].astype(F32))
    gtok_ref[0] = grad * (1.0 - halting) + gmid + norm_back(hat, rstd, vec_ref[0:1, :], gnormed)
    sub8 = lax.broadcasted_iota(jnp.int32, (8, width), 0)
    gvec = jnp.where(sub8 == 0, fold_rows(gnormed * hat), 0.0)
    gvec = jnp.where(sub8 == 1, fold_rows(gnormed), gvec)
    gvec = jnp.where(sub8 == 2, ggain2, gvec)
    gvec_ref[...] += jnp.where(sub8 == 3, gbias2, gvec)

    @pl.when(step == pl.num_programs(0) - 1)
    def _():
        if not last:
            for ref, out in zip(accs, outs):
                out[...] = ref[...]
            return
        pack, gvec_out = outs
        gvec_out[...] = gvec_ref[...]
        blocks = gq_ref.shape[1] // width
        for j in range(blocks):
            pack[j * width : (j + 1) * width, :] = gq_ref[:, j * width : (j + 1) * width].astype(BF16)
        place = blocks * width
        pack[place : place + gproj_ref.shape[0], :] = gproj_ref[...].astype(BF16)
        place = place + gproj_ref.shape[0]
        wide = gkvr_ref.shape[1]
        pack[place : place + width, :wide] = gkvr_ref[...].astype(BF16)
        pack[place : place + width, wide : wide + LANES] = gfr_ref[...].astype(BF16)
        pack[place : place + width, wide + LANES :] = jnp.zeros((width, width - wide - LANES), BF16)
        if pack.shape[0] > place + width:
            pack[place + width :, :] = jnp.zeros((pack.shape[0] - place - width, width), BF16)


def attention_backward(micro, last, packed_rows, tokens, grad, col, vec, qw, kvr, proj, frw, saved, near, far, cols, old, moving, cid):
    mid, n2, normed, mixed, probs, qs, kv, gates, slotcol = saved
    _, count, width = tokens.shape
    steps = count // SEQ
    inner = qw.shape[1]
    whole = lambda a: pl.BlockSpec(a.shape, lambda r: (0,) * a.ndim)
    by_row = lambda c: pl.BlockSpec((SEQ, c), lambda r: (r, 0))
    part = pl.BlockSpec((1, SEQ, width), lambda r: (micro, r, 0))
    out_shape = [jax.ShapeDtypeStruct(tokens.shape, F32)]
    if last:
        out_shape += [jax.ShapeDtypeStruct((packed_rows, width), BF16)]
    else:
        out_shape += [jax.ShapeDtypeStruct(a.shape, F32) for a in (qw, proj, kvr, frw)]
    out_shape += [jax.ShapeDtypeStruct((8, width), F32)]
    old_in = [old[k] for k in (1, 2, 3, 4, 5)] if old else []
    hbm = pl.BlockSpec(memory_space=pl.ANY)
    cols_spec = pl.BlockSpec((1, SEQ, 8), lambda r: (micro, r, 0))
    in_specs = [
        part, part, cols_spec,
        whole(vec), whole(qw), whole(kvr), whole(proj), whole(frw),
        by_row(width), by_row(width), by_row(width), by_row(inner),
        pl.BlockSpec((1, 4, SEQ, SEQ), lambda r: (r, 0, 0, 0)),
        pl.BlockSpec((1, 4, SEQ, LANES), lambda r: (r, 0, 0, 0)),
        by_row(LANES), by_row(8), cols_spec,
        whole(near), whole(far), cols_spec,
    ] + [whole(o) for o in old_in] + [hbm] * (1 if old else 0)
    args = (
        tokens, grad, col, vec, qw, kvr, proj, frw, mid, n2, normed, mixed, probs, qs, kv, gates, slotcol, near, far, cols,
        *old_in, *(old[:1] if old else []),
    )
    return run_kernel(
        functools.partial(attention_backward_kernel, last, len(old_in) + (1 if old else 0)), args, in_specs,
        out_shape, [part] + [pl.BlockSpec(o.shape, lambda r: (0, 0)) for o in out_shape[1:]],
        [
            pltpu.VMEM((SEQ, width), F32),
            pltpu.VMEM(qw.shape, F32),
            pltpu.VMEM(proj.shape, F32),
            pltpu.VMEM(kvr.shape, F32),
            pltpu.VMEM(frw.shape, F32),
            pltpu.VMEM((8, width), F32),
        ],
        (steps,), "attention_backward",
        pl.CostEstimate(
            flops=2 * count * width * (4 * inner + 512 + 2 * near.shape[0]), bytes_accessed=24 << 20, transcendentals=0
        ),
        moving, cid, {25: 0} if old else None,
    )


def total_plan(n_expert, n_hidden, rows):
    ny = nx = n_hidden // 2
    nz = n_expert // nx
    unit = 16 * ny * nx * nz
    units = -(-rows // (2 * unit))
    first = (units + 1) // 2
    return (nz, nx, ny), (first * unit, (units - first) * unit)


def total_kernel(
    sizes, parts, pack_ref, small_ref, gq_ref, gproj_ref, gkvr_ref, gfr_ref, sum_ref,
    buf, done, core_in, land_a, land_b, small_got, small_part, small_got2, sems, small_sems,
):
    nz, nx, ny = sizes
    e, h = lax.axis_index("expert"), lax.axis_index("hidden")
    n_expert, n_hidden = nz * nx, ny * 2
    z, x = lax.div(e, nx), lax.rem(e, nx)
    y, c = lax.div(h, 2), lax.rem(h, 2)
    half = sum(parts)
    width = pack_ref.shape[1]
    mesh_id = pl.DeviceIdType.MESH
    barrier = pltpu.get_barrier_semaphore()
    for k in range(1, n_expert):
        pl.semaphore_signal(barrier, inc=1, device_id=(lax.rem(e + k, n_expert), h), device_id_type=mesh_id)
    for k in range(1, n_hidden):
        pl.semaphore_signal(barrier, inc=1, device_id=(e, lax.rem(h + k, n_hidden)), device_id_type=mesh_id)
    pl.semaphore_wait(barrier, n_expert + n_hidden - 2)

    counter = [0]

    def copy(source, target, device, pool=sems):
        i = counter[0] if pool is sems else counter[1]
        if pool is sems:
            counter[0] += 1
        else:
            counter[1] += 1
        return pltpu.make_async_remote_copy(
            source, target, pool.at[0, i], pool.at[1, i], device_id=device, device_id_type=mesh_id
        )

    counter.append(0)

    def rows_at(ref, start, count):
        return ref.at[pl.ds(pl.multiple_of(start, 16), count)]

    def add_rows(start, count, pieces):
        step = 112 if count % 112 == 0 else 64 if count % 64 == 0 else 16

        def body(i, carry):
            place = pl.ds(pl.multiple_of(start + i * step, 16), step)
            total = buf[place, :].astype(F32)
            for ref in pieces:
                total = total + ref[pl.ds(pl.multiple_of(i * step, 16), step), :].astype(F32)
            buf[place, :] = total.astype(BF16)
            return carry

        lax.fori_loop(0, count // step, body, 0)

    axes = {
        "y": (ny, y, lambda p: (e, p * 2 + c)),
        "x": (nx, x, lambda p: (z * nx + p, h)),
        "z": (nz, z, lambda p: (p * nx + x, h)),
    }
    orders = ("yxz", "xyz")
    lands = (land_a, land_b)
    starts = [c * half, c * half + parts[0]]
    spans = list(parts)
    todo = [i for i in range(2) if parts[i]]

    small = [
        copy(small_ref, small_got.at[e], (lax.rem(e + k, n_expert), h), small_sems) for k in range(1, n_expert)
    ]
    for m in small:
        m.start()
    swap = copy(rows_at(pack_ref, (1 - c) * half, half), core_in, (e, h + 1 - 2 * c))
    swap.start()
    small_got[e] = small_ref[...]
    buf[pl.ds(pl.multiple_of(c * half, 16), half), :] = pack_ref[pl.ds(pl.multiple_of(c * half, 16), half), :]
    swap.wait()
    add_rows(c * half, half, [core_in])
    trail = []
    offset = [0, 0]
    for stage in range(3):
        running = []
        for i in todo:
            size, me, device = axes[orders[i][stage]]
            chunk = spans[i] // size
            moves = []
            pieces = []
            for k in range(1, size):
                peer = lax.rem(me + k, size)
                piece = lands[i].at[pl.ds(offset[i], chunk)]
                offset[i] += chunk
                moves.append(copy(rows_at(buf, starts[i] + peer * chunk, chunk), piece, device(peer)))
                pieces.append(piece)
            for m in moves:
                m.start()
            running.append((i, size, me, device, chunk, moves, pieces))
        for i, size, me, device, chunk, moves, pieces in running:
            for m in moves:
                m.wait()
            trail.append((stage, i, starts[i], chunk, size, me, device))
            starts[i] = starts[i] + me * chunk
            spans[i] = chunk
            add_rows(starts[i], chunk, pieces)
        if stage == 0:
            for m in small:
                m.wait()
            small_part[...] = jnp.sum(small_got[...], axis=0)
            small = [
                copy(small_part, small_got2.at[h], (e, lax.rem(h + k, n_hidden)), small_sems) for k in range(1, n_hidden)
            ]
            for m in small:
                m.start()
            small_got2[h] = small_part[...]
    for i in todo:
        here = pl.ds(pl.multiple_of(starts[i], 16), spans[i])
        done[here, :] = buf[here, :]
    for stage in (2, 1, 0):
        moves = []
        for s, i, start, chunk, size, me, device in trail:
            if s == stage:
                place = rows_at(done, start + me * chunk, chunk)
                moves += [copy(place, place, device(lax.rem(me + k, size))) for k in range(1, size)]
        for m in moves:
            m.start()
        for m in moves:
            m.wait()
    place = rows_at(done, c * half, half)
    swap = copy(place, place, (e, h + 1 - 2 * c))
    swap.start()
    for m in small:
        m.wait()
    sum_ref[...] = jnp.sum(small_got2[...], axis=0)
    swap.wait()
    blocks = gq_ref.shape[1] // width

    def widen(target, lanes, base, count, span):
        def body(i, carry):
            here = pl.multiple_of(i * 64, 64)
            target[pl.ds(here, 64), lanes] = done[pl.ds(base + here, 64), span].astype(F32)
            return carry

        lax.fori_loop(0, count // 64, body, 0)

    for j in range(blocks):
        widen(gq_ref, slice(j * width, (j + 1) * width), j * width, width, slice(0, width))
    base = blocks * width
    widen(gproj_ref, slice(0, width), base, gproj_ref.shape[0], slice(0, width))
    base = base + gproj_ref.shape[0]
    wide = gkvr_ref.shape[1]
    widen(gkvr_ref, slice(0, wide), base, width, slice(0, wide))
    widen(gfr_ref, slice(0, LANES), base, width, slice(wide, wide + LANES))


def total_step(n_expert, n_hidden, rows, pack, small, qw, proj, kvr, frw):
    sizes, parts = total_plan(n_expert, n_hidden, rows)
    nz, nx, ny = sizes
    width = pack.shape[1]
    half = sum(parts)
    vmem = pl.BlockSpec(memory_space=pltpu.VMEM)
    lands = []
    for part, order in zip(parts, ((ny, nx, nz), (nx, ny, nz))):
        total = 0
        for size in order:
            part = part // size
            total += part * (size - 1)
        lands.append(pltpu.VMEM((max(total, 16), width), BF16))
    steps = 2 + 4 * ((ny - 1) + (nx - 1) + (nz - 1))
    return pl.pallas_call(
        functools.partial(total_kernel, sizes, parts),
        out_shape=tuple(jax.ShapeDtypeStruct(a.shape, F32) for a in (qw, proj, kvr, frw, small)),
        in_specs=[vmem] * 2,
        out_specs=[vmem] * 5,
        scratch_shapes=[
            pltpu.VMEM((2 * half, width), BF16),
            pltpu.VMEM((2 * half, width), BF16),
            pltpu.VMEM((half, width), BF16),
            *lands,
            pltpu.VMEM((n_expert,) + small.shape, F32),
            pltpu.VMEM(small.shape, F32),
            pltpu.VMEM((n_hidden,) + small.shape, F32),
            pltpu.SemaphoreType.DMA((2, steps)),
            pltpu.SemaphoreType.DMA((2, n_expert + n_hidden)),
        ],
        compiler_params=pltpu.CompilerParams(collective_id=8, has_side_effects=True, vmem_limit_bytes=VMEM_LIMIT),
        name="total_step",
    )(pack, small)


def move_only(moving, cid):
    return run_kernel(
        lambda *refs: None, (), [], (), [], (), (1,), "move_only",
        pl.CostEstimate(flops=0, bytes_accessed=4 << 20, transcendentals=0), moving, cid,
    )


def pad_lanes(a):
    return jnp.pad(a, ((0, 0), (0, LANES - a.shape[1])))


def per_device(
    tokens, grad_out, attn_routes, ffn_routes, segments, pad_mask, norm1_gain, norm1_bias, attn_router,
    query_w, key_w, value_w, attn_proj, norm2_gain, norm2_bias, ffn_router, expert_in, expert_out, halt_w, halt_b,
    *, n_expert, n_hidden,
):
    micros, count, width = tokens.shape
    experts = ffn_router.shape[1]
    capacity = 4 * count // experts
    slots = experts * capacity
    per = experts // n_expert
    group = n_expert // 2
    across = [(i, (i + group) % n_expert) for i in range(n_expert)]

    def gathered(a):
        return lax.all_gather(a, "hidden", axis=0, tiled=False)

    crossed = [lax.ppermute(a, "expert", across) for a in (expert_in, expert_out)]
    near_first, near_second = gathered(expert_in), gathered(expert_out)
    seg = segments.reshape(micros, count)
    zeros = jnp.zeros_like(seg)
    mine = lax.axis_index("expert") // group
    kind = (ffn_routes // (experts // 2) != mine).astype(jnp.int32)
    base = (kind * (experts // 2) + ffn_routes % (experts // 2)) * capacity
    col = jnp.concatenate([attn_routes, ffn_routes, seg[:, :, None], pad_mask[:, :, None]], axis=2)
    row = jnp.stack(
        [seg, pad_mask, ffn_routes[:, :, 0], ffn_routes[:, :, 1], base[:, :, 0], base[:, :, 1], zeros, zeros], axis=1
    )
    none = jnp.zeros_like(halt_w)
    vec = jnp.stack([norm1_gain, norm1_bias, norm2_gain, norm2_bias, halt_w, none, none, none])
    kvr = jnp.concatenate([key_w, value_w, pad_lanes(attn_router)], axis=1)
    frw = pad_lanes(ffn_router)
    hb = jnp.broadcast_to(halt_b.reshape(1, 1), (8, LANES))
    shape = (2, group, per, capacity, width)
    packed = query_w.size // width + attn_proj.shape[0] + width
    packed_rows = 2 * sum(total_plan(n_expert, n_hidden, packed)[1])

    slotrow, slotcol, gslots = route_step(row, grad_out, slots)
    weights = (vec, hb, query_w, kvr, attn_proj, frw)
    f0 = attention_forward(0, tokens, grad_out, col, row, slotrow, *weights, slots, (), None)
    crossed[0], n0_out = lax.optimization_barrier((crossed[0], f0[9]))
    far_first = gathered(crossed[0])
    *f1, n0 = attention_forward(1, tokens, grad_out, col, row, slotrow, *weights, slots, [n0_out.reshape(shape)], 2)
    crossed[1], n1_out = lax.optimization_barrier((crossed[1], f1[9]))
    far_second = gathered(crossed[1])
    (n1,) = move_only([n1_out.reshape(shape)], 3)
    rows = (n0, n1)
    y0, y1, g1 = expert_forward(0, rows, near_first, near_second, [gslots[1].reshape(shape)], 4)
    far0, far1, g0 = expert_forward(1, rows, far_first, far_second, [gslots[0].reshape(shape)], 1)
    grads = (g0, g1)
    scal = reading_step((y0, y1, far0, far1), grads, vec)
    cols, ab = scalar_step(scal, (f0[8], f1[8]), slotrow)
    gf_far, gs_far, bf0, bf1, r0, rf0 = expert_backward(1, rows, grads, ab, vec, far_first, far_second, [y0, far0], 5)
    gf_near, gs_near, bn0, bn1, qf0, qf1 = expert_backward(
        0, rows, grads, ab, vec, near_first, near_second, [bf0, bf1], 6
    )

    flat = lambda a: a.reshape(slots // 2, width)

    def reduced(a):
        return lax.psum_scatter(a, "hidden", scatter_dimension=0, tiled=False)

    far_grads = [lax.ppermute(reduced(a), "expert", across) for a in (gf_far, gs_far)]
    near_grads = [reduced(a) for a in (gf_near, gs_near)]
    *res0, qn0 = result_step(0, tokens, f0[0], flat(r0), flat(rf0), cols, slotcol, (), [bn0], 7)
    common = (tokens, grad_out, col, vec, query_w, kvr, attn_proj, frw)
    *out, qn1, r1 = attention_backward(
        0, False, packed_rows, *common, list(f0[:8]) + [slotcol], flat(qn0), flat(qf0), cols, (), [bn1, y1], 9
    )
    *out, rf1 = attention_backward(
        1, True, packed_rows, *common, list(f1[:8]) + [slotcol], flat(qn1), flat(qf1), cols, tuple(out), [far1], 10
    )
    res1 = result_step(1, tokens, f1[0], flat(r1), flat(rf1), cols, slotcol, tuple(res0[:1]), (), None)
    gfirst, gsecond = [a.astype(F32) + b.astype(F32) for a, b in zip(near_grads, far_grads)]
    small = jnp.concatenate([out[2], res0[1] + res1[1]], axis=0)
    gq, gproj, gkvr, gfr, small = total_step(
        n_expert, n_hidden, packed, out[1], small, query_w, attn_proj, kvr, frw
    )
    head = key_w.shape[1]
    return (
        res1[0],
        out[0],
        small[0],
        small[1],
        gkvr[:, LANES : LANES + attn_router.shape[1]],
        gq,
        gkvr[:, :head],
        gkvr[:, head : 2 * head],
        gproj,
        small[2],
        small[3],
        gfr[:, :experts],
        gfirst,
        gsecond,
        small[8],
        small[9, :1],
    )


def solution(mesh):
    rows = P(None, ("expert", "hidden"), None)
    in_specs = (rows,) * 5 + (P(None, ("expert", "hidden")),) + (P(),) * 10 + (
        P("expert", None, "hidden"), P("expert", "hidden", None), P(), P(),
    )
    out_specs = (rows,) * 2 + (P(),) * 10 + (P("expert", None, "hidden"), P("expert", "hidden", None), P(), P())
    return jax.shard_map(
        functools.partial(per_device, n_expert=mesh.shape["expert"], n_hidden=mesh.shape["hidden"]),
        mesh=mesh, in_specs=in_specs, out_specs=out_specs, check_vma=False,
    )
```

```python
import functools
import math

import jax
import jax.numpy as jnp
from jax import lax
from jax.experimental import pallas as pl
from jax.experimental.pallas import tpu as pltpu
from jax.sharding import PartitionSpec as P

SEQ = 256
LANES = 128
F32 = jnp.float32
BF16 = jnp.bfloat16
GELU_C = math.sqrt(2.0 / math.pi)
GELU_A = 0.044715
VMEM_LIMIT = 60 * 1024 * 1024
STREAMS = 4


def mm(left, right):
    return jnp.dot(left, right, preferred_element_type=F32)


def mm_nt(left, right):
    return lax.dot_general(left, right, (((1,), (1,)), ((), ())), preferred_element_type=F32)


def mm_tn(left, right):
    return lax.dot_general(left, right, (((0,), (0,)), ((), ())), preferred_element_type=F32)


def lane_iota(rows, lanes=LANES):
    return lax.broadcasted_iota(jnp.int32, (rows, lanes), 1)


def norm_parts(value):
    center = value - jnp.mean(value, axis=-1, keepdims=True)
    rstd = lax.rsqrt(jnp.mean(center * center, axis=-1, keepdims=True) + 1e-05)
    return center * rstd, rstd


def norm_back(hat, rstd, gain, grad):
    scaled = grad * gain
    first = jnp.mean(scaled, axis=-1, keepdims=True)
    second = jnp.mean(scaled * hat, axis=-1, keepdims=True)
    return rstd * (scaled - first - hat * second)


def fold_rows(value):
    return jnp.sum(value, axis=0, keepdims=True)


def pick_head(tiles, route, lane):
    pair = lax.shift_right_logical(route, 1)
    out = tiles[0]
    for j in range(1, len(tiles)):
        out = jnp.where(pair == j, tiles[j], out)
    odd = (route & 1) == 1
    return jnp.where(odd, pltpu.roll(out, LANES // 2, 1), out)


def place_heads(parts, routes, count, lane):
    half = lax.shift_right_logical(lane, 6)
    kept = [jnp.where(half == (r & 1), p, 0.0) for p, r in zip(parts, routes)]
    pairs = [lax.shift_right_logical(r, 1) for r in routes]
    tiles = []
    for j in range(count):
        total = jnp.where(pairs[0] == j, kept[0], 0.0)
        for k, p in zip(kept[1:], pairs[1:]):
            total = total + jnp.where(p == j, k, 0.0)
        tiles.append(total)
    return tiles


def softmax_cols(cols):
    top = functools.reduce(jnp.maximum, cols)
    expo = [jnp.exp(c - top) for c in cols]
    total = functools.reduce(jnp.add, expo)
    return [e / total for e in expo]


def put_cols(cols, rows, width):
    lane = lane_iota(rows, width)
    out = jnp.zeros((rows, width), cols[0].dtype)
    for i, c in enumerate(cols):
        out = jnp.where(lane == i, c, out)
    return out


def split_three(value):
    high = value.astype(BF16)
    rest = value - high.astype(F32)
    middle = rest.astype(BF16)
    last = (rest - middle.astype(F32)).astype(BF16)
    return jnp.concatenate([high.astype(F32), middle.astype(F32), last.astype(F32)], axis=0).astype(BF16)


def join_three(value):
    n = value.shape[0] // 3
    return value[:n] + value[n : 2 * n] + value[2 * n :]


def row_to_col(row):
    n = row.shape[1]
    place = lax.broadcasted_iota(jnp.int32, (n, n), 0)
    other = lax.broadcasted_iota(jnp.int32, (n, n), 1)
    return jnp.sum(jnp.where(place == other, row, 0.0), axis=-1, keepdims=True)


def dispatch(slot_rows, values, out_ref):
    chunk = 256
    tokens = values[0].shape[0]
    spot = lax.broadcasted_iota(jnp.int32, (chunk, tokens), 0)

    def body(k, carry):
        base = spot + k * chunk
        if len(values) == 1:
            pick = jnp.where((base == slot_rows[0]) | (base == slot_rows[1]), 1.0, 0.0).astype(BF16)
            out = mm(pick, values[0][...])
        else:
            out = mm(jnp.where(base == slot_rows[0], 1.0, 0.0).astype(BF16), values[0][...])
            out = out + mm(jnp.where(base == slot_rows[1], 1.0, 0.0).astype(BF16), values[1][...])
        out_ref[pl.ds(pl.multiple_of(k * chunk, chunk), chunk), :] = out.astype(BF16)
        return carry

    lax.fori_loop(0, out_ref.shape[0] // chunk, body, 0)


def group_of():
    size = lax.axis_size("expert") // 2
    e = lax.axis_index("expert")
    me = lax.rem(e, size)
    return me, size, e - me


def group_greet():
    me, size, base = group_of()
    other = lax.axis_index("hidden")
    barrier = pltpu.get_barrier_semaphore()
    for k in range(1, size):
        pl.semaphore_signal(
            barrier, inc=1, device_id=(base + lax.rem(me + k, size), other), device_id_type=pl.DeviceIdType.MESH
        )
    pl.semaphore_wait(barrier, size - 1)


def group_copies(source, target, send_sem, recv_sem):
    me, size, base = group_of()
    other = lax.axis_index("hidden")
    moves = []
    for k in range(1, size):
        peer = lax.rem(me + k, size)
        moves.append(
            pltpu.make_async_remote_copy(
                source.at[peer], target.at[me], send_sem.at[k - 1], recv_sem.at[k - 1],
                device_id=(base + peer, other), device_id_type=pl.DeviceIdType.MESH,
            )
        )
    return moves


def at_step(which):
    found = True
    for axis, size in enumerate(which[1]):
        here = pl.program_id(axis) == (0 if which[0] == 0 else size - 1)
        found = here if found is True else found & here
    return found


def run_kernel(kernel, args, in_specs, out_shape, out_specs, scratch, grid, name, cost, moving=(), cid=None, aliases=None):
    n_in, n_out, n_move = len(args), len(out_shape), len(moving)
    peers = lax.axis_size("expert") // 2 - 1
    hbm = pl.BlockSpec(memory_space=pl.ANY)

    def body(*refs):
        ins, sources = refs[:n_in], refs[n_in : n_in + n_move]
        outs = refs[n_in + n_move : n_in + n_move + n_out]
        targets = refs[n_in + n_move + n_out : n_in + 2 * n_move + n_out]
        rest = refs[n_in + 2 * n_move + n_out :]
        sems = rest[len(scratch) :]
        moves, owns = [], []
        me = group_of()[0]
        pairs = []
        for a, b in zip(sources, targets):
            pairs += [(a, b)] if len(a.shape) == 4 else [(a.at[i], b.at[i]) for i in range(a.shape[0])]
        for i, (a, b) in enumerate(pairs):
            moves += group_copies(a, b, sems[3 * i], sems[3 * i + 1])
            owns.append(pltpu.make_async_copy(a.at[me], b.at[me], sems[3 * i + 2]))

        if moving:

            @pl.when(at_step((0, grid)))
            def _():
                group_greet()
                for c in moves + owns:
                    c.start()

        kernel(*ins, *outs, *rest[: len(scratch)])

        if moving:

            @pl.when(at_step((1, grid)))
            def _():
                for c in moves + owns:
                    c.wait()

    sems = []
    for _ in range(sum(1 if a.ndim == 4 else a.shape[0] for a in moving)):
        sems += [pltpu.SemaphoreType.DMA((peers,)), pltpu.SemaphoreType.DMA((peers,)), pltpu.SemaphoreType.DMA]
    more = dict(collective_id=cid, has_side_effects=True) if moving else {}
    return pl.pallas_call(
        body,
        grid=grid,
        out_shape=tuple(out_shape) + tuple(jax.ShapeDtypeStruct(a.shape, a.dtype) for a in moving),
        in_specs=list(in_specs) + [hbm] * n_move,
        out_specs=list(out_specs) + [hbm] * n_move,
        scratch_shapes=list(scratch) + sems,
        input_output_aliases=aliases or {},
        compiler_params=pltpu.CompilerParams(vmem_limit_bytes=VMEM_LIMIT, **more),
        cost_estimate=cost,
        name=name,
    )(*args, *moving)


def route_kernel(row_ref, slotrow_ref, slotcol_ref):
    tokens = row_ref.shape[2]
    before = lax.broadcasted_iota(jnp.int32, (tokens, tokens), 0)
    after = lax.broadcasted_iota(jnp.int32, (tokens, tokens), 1)
    upper = jnp.where(before < after, 1.0, 0.0).astype(BF16)
    sub = lax.broadcasted_iota(jnp.int32, (LANES, tokens), 0)
    sub8 = lax.broadcasted_iota(jnp.int32, (8, tokens), 0)
    for m in range(row_ref.shape[0]):
        row = row_ref[m]
        named = [jnp.where(sub == row[2 + i : 3 + i, :], 1.0, 0.0) for i in range(2)]
        rank = mm((named[0] + named[1]).astype(BF16), upper)
        slots = [fold_rows(named[i] * rank).astype(jnp.int32) + row[4 + i : 5 + i, :] for i in range(2)]
        slotrow_ref[m] = jnp.where(sub8 == 0, slots[0], slots[1])
        table = jnp.where(sub == 0, slots[0].astype(F32), slots[1].astype(F32))
        slotcol_ref[m] = jnp.transpose(table)[:, :8].astype(jnp.int32)


def route_step(row):
    micros, _, count = row.shape
    out_shape = (
        jax.ShapeDtypeStruct((micros, 8, count), jnp.int32),
        jax.ShapeDtypeStruct((micros, count, 8), jnp.int32),
    )
    whole = lambda s: pl.BlockSpec(s, lambda i: (0,) * len(s))
    return run_kernel(
        route_kernel, (row,), [whole(row.shape)], out_shape, [whole(o.shape) for o in out_shape], (), (1,), "route_step",
        pl.CostEstimate(flops=10**8, bytes_accessed=1 << 20, transcendentals=0),
    )


def spread_kernel(slotrow_ref, grad_ref, out0_ref, out1_ref):
    for m, out_ref in enumerate((out0_ref, out1_ref)):
        dispatch([slotrow_ref[m, 0:1, :], slotrow_ref[m, 1:2, :]], [grad_ref.at[m]], out_ref)


def spread_step(slotrow, grad, slots, moving, cid):
    width = grad.shape[2]
    whole = lambda s: pl.BlockSpec(s, lambda i: (0,) * len(s))
    return run_kernel(
        spread_kernel, (slotrow, grad), [whole(slotrow.shape), whole(grad.shape)],
        [jax.ShapeDtypeStruct((slots, width), BF16)] * 2, [whole((slots, width))] * 2, (), (1,), "spread_step",
        pl.CostEstimate(flops=8 * slots * width * grad.shape[1], bytes_accessed=6 << 20, transcendentals=0), moving, cid,
    )


def attention_forward_kernel(
    x_ref, grad_ref, col_ref, row_ref, slotrow_ref, vec_ref, hb_ref, qw_ref, kvr_ref, proj_ref, frw_ref,
    mid_ref, n2_ref, normed_ref, mixed_ref, probs_ref, qs_ref, kv_ref, gates_ref, scal_ref, out_ref,
    n2_all,
):
    step = pl.program_id(0)
    rows = x_ref.shape[1]
    top_attn = 4
    lane = lane_iota(rows)
    x = x_ref[0].astype(F32)
    col = col_ref[0]
    row = row_ref[0]
    hat, _ = norm_parts(x)
    normed = (hat * vec_ref[0:1, :] + vec_ref[1:2, :]).astype(BF16)
    normed_ref[...] = normed
    kvr = mm(normed, kvr_ref[...])
    kv = kvr[:, :LANES].astype(BF16)
    kv_ref[...] = kv
    logits = kvr[:, LANES:]
    routes = [col[:, i : i + 1] for i in range(top_attn)]
    picked = [
        jnp.sum(jnp.where(lane == r, logits, 0.0), axis=-1, keepdims=True) for r in routes
    ]
    gates = softmax_cols(picked)
    query = mm(normed, qw_ref[...])
    heads_pairs = query.shape[1] // LANES
    tiles = [query[:, j * LANES : (j + 1) * LANES] for j in range(heads_pairs)]
    low = lane < LANES // 2
    same = col[:, 6:7] == row[0:1, :]
    place = lax.broadcasted_iota(jnp.int32, (rows, rows), 0)
    other = lax.broadcasted_iota(jnp.int32, (rows, rows), 1)
    allowed = same & ((row[1:2, :] == 1) | (place == other))
    scale = 0.125
    shares = []
    for i in range(top_attn):
        sel = jnp.where(low, pick_head(tiles, routes[i], lane), 0.0).astype(BF16)
        qs_ref[0, i] = sel
        scores = mm_nt(sel, kv) * scale
        scores = jnp.where(allowed, scores, -1e30)
        expo = jnp.exp(scores - jnp.max(scores, axis=-1, keepdims=True))
        probs = (expo * (1.0 / jnp.sum(expo, axis=-1, keepdims=True))).astype(BF16)
        probs_ref[0, i] = probs
        heads = mm(probs, kv) * gates[i]
        shares.append(jnp.where(low, pltpu.roll(heads, LANES // 2, 1), heads))
    mixed_tiles = place_heads(shares, routes, heads_pairs, lane)
    mixed = jnp.concatenate([t.astype(BF16) for t in mixed_tiles], axis=1)
    mixed_ref[...] = mixed
    mid = x + mm(mixed, proj_ref[...])
    mid_ref[...] = mid
    hat2, _ = norm_parts(mid)
    n2 = (hat2 * vec_ref[2:3, :] + vec_ref[3:4, :]).astype(BF16)
    n2_ref[...] = n2
    n2_all[pl.ds(pl.multiple_of(step * rows, rows), rows), :] = n2
    logits_ffn = mm(n2, frw_ref[...])
    gates_ffn = softmax_cols(
        [
            jnp.sum(jnp.where(lane == col[:, 4 + i : 5 + i], logits_ffn, 0.0), axis=-1, keepdims=True)
            for i in range(2)
        ]
    )
    gates_ref[...] = put_cols(gates, rows, gates_ref.shape[1])
    stop = jnp.sum(mid * vec_ref[4:5, :], axis=-1, keepdims=True) + hb_ref[0:1, 0:1]
    pull = jnp.sum(grad_ref[0].astype(F32) * (mid - x), axis=-1, keepdims=True)
    scal_ref[...] = jnp.transpose(put_cols([stop, pull] + gates_ffn, rows, LANES))[:8, :]

    @pl.when(step == pl.num_programs(0) - 1)
    def _():
        dispatch([slotrow_ref[0, 0:1, :], slotrow_ref[0, 1:2, :]], [n2_all], out_ref)


def attention_forward(micro, tokens, grad, col, row, slotrow, vec, hb, qw, kvr, proj, frw, slots, moving, cid):
    _, count, width = tokens.shape
    steps = count // SEQ
    inner = qw.shape[1]
    whole = lambda a: pl.BlockSpec(a.shape, lambda r: (0,) * a.ndim)
    out_shape = (
        jax.ShapeDtypeStruct((count, width), F32),
        jax.ShapeDtypeStruct((count, width), BF16),
        jax.ShapeDtypeStruct((count, width), BF16),
        jax.ShapeDtypeStruct((count, inner), BF16),
        jax.ShapeDtypeStruct((steps, 4, SEQ, SEQ), BF16),
        jax.ShapeDtypeStruct((steps, 4, SEQ, LANES), BF16),
        jax.ShapeDtypeStruct((count, LANES), BF16),
        jax.ShapeDtypeStruct((count, 8), F32),
        jax.ShapeDtypeStruct((8, count), F32),
        jax.ShapeDtypeStruct((slots, width), BF16),
    )
    by_row = lambda c: pl.BlockSpec((SEQ, c), lambda r: (r, 0))
    in_specs = [
        pl.BlockSpec((1, SEQ, width), lambda r: (micro, r, 0)),
        pl.BlockSpec((1, SEQ, width), lambda r: (micro, r, 0)),
        pl.BlockSpec((1, SEQ, 8), lambda r: (micro, r, 0)),
        pl.BlockSpec((1, 8, SEQ), lambda r: (micro, 0, r)),
        pl.BlockSpec((1, 8, count), lambda r: (micro, 0, 0)),
        whole(vec), whole(hb), whole(qw), whole(kvr), whole(proj), whole(frw),
    ]
    out_specs = [
        by_row(width), by_row(width), by_row(width), by_row(inner),
        pl.BlockSpec((1, 4, SEQ, SEQ), lambda r: (r, 0, 0, 0)),
        pl.BlockSpec((1, 4, SEQ, LANES), lambda r: (r, 0, 0, 0)),
        by_row(LANES), by_row(8),
        pl.BlockSpec((8, SEQ), lambda r: (0, r)),
        pl.BlockSpec((slots, width), lambda r: (0, 0)),
    ]
    return run_kernel(
        attention_forward_kernel, (tokens, grad, col, row, slotrow, vec, hb, qw, kvr, proj, frw), in_specs,
        out_shape, out_specs, [pltpu.VMEM((count, width), BF16)], (steps,), "attention_forward",
        pl.CostEstimate(
            flops=2 * count * width * (2 * inner + 256 + slots), bytes_accessed=12 << 20, transcendentals=count * 4 * SEQ
        ),
        moving, cid,
    )


def gelu_parts(pre):
    square = pre * pre
    inner = jnp.tanh(GELU_C * pre * (1.0 + GELU_A * square))
    return square, inner


def expert_forward_kernel(rows0_ref, rows1_ref, first_ref, second_ref, out0_ref, out1_ref, total):
    part = pl.program_id(1)
    _, src, _, cap, width = rows0_ref.shape
    half = src * cap
    rows = jnp.concatenate([r[...].reshape(half, width) for r in (rows0_ref, rows1_ref)], axis=0)
    pre = mm(rows, first_ref[0, 0])
    _, inner = gelu_parts(pre)
    act = (0.5 * pre * (1.0 + inner)).astype(BF16)
    res = mm(act, second_ref[0, 0])

    @pl.when(part == 0)
    def _():
        total[...] = res

    @pl.when(part > 0)
    def _():
        total[...] += res

    @pl.when(part == pl.num_programs(1) - 1)
    def _():
        out0_ref[...] = total[:half, :].astype(BF16).reshape(out0_ref.shape)
        out1_ref[...] = total[half:, :].astype(BF16).reshape(out1_ref.shape)


def expert_forward(kind, rows, first, second, moving, cid):
    _, src, local, cap, width = rows[0].shape
    parts, _, _, hid = first.shape
    spec_in = pl.BlockSpec((1, src, 1, cap, width), lambda e, h: (kind, 0, e, 0, 0))
    spec_rows = pl.BlockSpec((src, 1, cap, width), lambda e, h: (0, e, 0, 0))
    work = 2 * src * local * cap * width * hid * parts
    return run_kernel(
        expert_forward_kernel, (*rows, first, second),
        [
            spec_in, spec_in,
            pl.BlockSpec((1, 1, width, hid), lambda e, h: (h, e, 0, 0)),
            pl.BlockSpec((1, 1, hid, width), lambda e, h: (h, e, 0, 0)),
        ],
        [jax.ShapeDtypeStruct(r.shape[1:], BF16) for r in rows], [spec_rows] * 2,
        [pltpu.VMEM((2 * src * cap, width), F32)], (local, parts), "expert_forward",
        pl.CostEstimate(flops=4 * work, bytes_accessed=24 << 20, transcendentals=work // width), moving, cid,
    )


def reading_kernel(*refs):
    outs, grads = refs[:4], refs[4:8]
    vec_ref, scal_ref = refs[8:]
    src, _, cap, width = outs[0].shape
    halt = split_three(jnp.broadcast_to(vec_ref[4:5, :], (8, width)))
    ones = jnp.ones((8, width), BF16)
    sub8 = lax.broadcasted_iota(jnp.int32, (8, cap), 0)
    for kind in range(2):
        for m in range(2):
            for s in range(src):
                low = outs[2 * kind + m][s, 0]
                stop = join_three(mm_nt(halt, low))
                prod = low.astype(F32) * grads[2 * kind + m][0, s, 0].astype(F32)
                high = prod.astype(BF16)
                rest = (prod - high.astype(F32)).astype(BF16)
                pull = mm_nt(ones, high) + mm_nt(ones, rest)
                scal_ref[s, m, kind, 0] = jnp.where(sub8 == 0, stop, pull)


def reading_step(outs, grads, vec):
    src, local, cap, width = outs[0].shape
    spec_rows = pl.BlockSpec((src, 1, cap, width), lambda e: (0, e, 0, 0))
    spec_grad = lambda kind: pl.BlockSpec((1, src, 1, cap, width), lambda e: (kind, 0, e, 0, 0))
    return run_kernel(
        reading_kernel, (*outs, *grads, *grads, vec),
        [spec_rows] * 4 + [spec_grad(0)] * 2 + [spec_grad(1)] * 2 + [pl.BlockSpec(vec.shape, lambda e: (0, 0))],
        [jax.ShapeDtypeStruct((src, 2, 2, local, 8, cap), F32)],
        [pl.BlockSpec((src, 2, 2, 1, 8, cap), lambda e: (0, 0, 0, e, 0, 0))], (), (local,), "reading_step",
        pl.CostEstimate(flops=10**9, bytes_accessed=8 << 20, transcendentals=0),
    )[0].reshape(src, 2, 2 * local, 8, cap)


def expert_backward_kernel(
    rows0_ref, rows1_ref, grad0_ref, grad1_ref, ab_ref, vec_ref, first_ref, second_ref,
    gfirst_ref, gsecond_ref, out0_ref, out1_ref, total, gin_all,
):
    part = pl.program_id(1)
    _, src, _, cap, width = rows0_ref.shape
    half = src * cap

    @pl.when(part == 0)
    def _():
        for m, grad_ref in enumerate((grad0_ref, grad1_ref)):
            for s in range(src):
                ab = ab_ref[s, m, 0]
                scaled = row_to_col(ab[0:1, :]) * grad_ref[0, s, 0].astype(F32) + row_to_col(ab[1:2, :]) * vec_ref[4:5, :]
                gin_all[m * half + s * cap : m * half + (s + 1) * cap, :] = scaled.astype(BF16)

    rows = jnp.concatenate([r[...].reshape(half, width) for r in (rows0_ref, rows1_ref)], axis=0)
    gin = gin_all[...]
    first = first_ref[0, 0]
    second = second_ref[0, 0]
    pre = mm(rows, first)
    gact = mm_nt(gin, second)
    square, inner = gelu_parts(pre)
    part_one = 0.5 * (1.0 + inner)
    act = (pre * part_one).astype(BF16)
    slope = part_one + 0.5 * pre * (1.0 - inner * inner) * (GELU_C + (3.0 * GELU_C * GELU_A) * square)
    gpre = (gact * slope).astype(BF16)
    gsecond_ref[0, 0] = mm_tn(act, gin).astype(BF16)
    gfirst_ref[0, 0] = mm_tn(rows, gpre).astype(BF16)
    res = mm_nt(gpre, first)

    @pl.when(part == 0)
    def _():
        total[...] = res

    @pl.when(part > 0)
    def _():
        total[...] += res

    @pl.when(part == pl.num_programs(1) - 1)
    def _():
        out0_ref[...] = total[:half, :].astype(BF16).reshape(out0_ref.shape)
        out1_ref[...] = total[half:, :].astype(BF16).reshape(out1_ref.shape)


def expert_backward(kind, rows, grads, ab, vec, first, second, moving, cid):
    _, src, local, cap, width = rows[0].shape
    parts, _, _, hid = first.shape
    spec_in = pl.BlockSpec((1, src, 1, cap, width), lambda e, h: (kind, 0, e, 0, 0))
    spec_rows = pl.BlockSpec((src, 1, cap, width), lambda e, h: (0, e, 0, 0))
    spec_first = pl.BlockSpec((1, 1, width, hid), lambda e, h: (h, e, 0, 0))
    spec_second = pl.BlockSpec((1, 1, hid, width), lambda e, h: (h, e, 0, 0))
    work = 2 * src * local * cap * width * hid * parts
    return run_kernel(
        expert_backward_kernel, (*rows, *grads, ab, vec, first, second),
        [spec_in] * 4
        + [pl.BlockSpec((src, 2, 1, 8, cap), lambda e, h: (0, 0, kind * local + e, 0, 0)), pl.BlockSpec(vec.shape, lambda e, h: (0, 0))]
        + [spec_first, spec_second],
        [jax.ShapeDtypeStruct(first.shape, BF16), jax.ShapeDtypeStruct(second.shape, BF16)]
        + [jax.ShapeDtypeStruct(r.shape[1:], BF16) for r in rows],
        [spec_first, spec_second, spec_rows, spec_rows],
        [pltpu.VMEM((2 * src * cap, width), F32), pltpu.VMEM((2 * src * cap, width), BF16)],
        (local, parts), "expert_backward",
        pl.CostEstimate(flops=10 * work, bytes_accessed=48 << 20, transcendentals=work // width), moving, cid,
    )


def scalar_kernel(scal_ref, rowsc0_ref, rowsc1_ref, slotrow_ref, cols_ref, ab_ref, got, sent, got2, send_sem, recv_sem, send_sem2, recv_sem2):
    src, micros, local, _, cap = scal_ref.shape
    tokens = rowsc0_ref.shape[1]
    me = group_of()[0]
    group_greet()
    moves = group_copies(scal_ref, got, send_sem, recv_sem)
    for c in moves:
        c.start()
    got[me] = scal_ref[me]
    for c in moves:
        c.wait()
    spot = lax.broadcasted_iota(jnp.int32, (cap, tokens), 0)
    sub = lax.broadcasted_iota(jnp.int32, (LANES, tokens), 0)
    sub8 = lax.broadcasted_iota(jnp.int32, (8, tokens), 0)
    for m, rowsc_ref in enumerate((rowsc0_ref, rowsc1_ref)):
        slot = [slotrow_ref[m, i : i + 1, :] for i in range(2)]

        def onehot(expert):
            per = local // 2
            which = lax.rem(expert, local)
            base = lax.div(which, per) * (src * per) + lax.div(expert, local) * per + lax.rem(which, per)
            base = spot + base * cap
            return [jnp.where(base == s, 1.0, 0.0).astype(BF16) for s in slot]

        zero = jnp.zeros((24, tokens), F32)

        def collect(expert, carry):
            values = split_three(got[lax.div(expert, local), m, lax.rem(expert, local)])
            return tuple(c + mm(values, p) for c, p in zip(carry, onehot(expert)))

        found = lax.fori_loop(0, src * local, collect, (zero, zero))
        found = [join_three(f) for f in found]
        stop, pull, gate0, gate1 = [rowsc_ref[i : i + 1, :] for i in range(4)]
        gates = [gate0, gate1]
        yh = [f[0:1, :] for f in found]
        yg = [f[1:2, :] for f in found]
        halting = jax.nn.sigmoid(stop + gate0 * yh[0] + gate1 * yh[1])
        s = (pull + gate0 * yg[0] + gate1 * yg[1]) * halting * (1.0 - halting)
        u = [halting * g + s * h for g, h in zip(yg, yh)]
        mean = gate0 * u[0] + gate1 * u[1]
        keep = [halting, s, gate0 * (u[0] - mean), gate1 * (u[1] - mean), gate0, gate1]
        table = jnp.zeros((LANES, tokens), F32)
        for i, r in enumerate(keep):
            table = jnp.where(sub == i, r, table)
        cols_ref[m] = jnp.transpose(table)[:, :8]
        ab = [split_three(jnp.where(sub8 == 0, g * halting, jnp.where(sub8 == 1, g * s, 0.0))) for g in gates]

        def spread(expert, carry):
            picks = onehot(expert)
            sent[lax.div(expert, local), m, lax.rem(expert, local)] = join_three(
                mm_nt(ab[0], picks[0]) + mm_nt(ab[1], picks[1])
            )
            return carry

        lax.fori_loop(0, src * local, spread, 0)
    moves = group_copies(sent, got2, send_sem2, recv_sem2)
    for c in moves:
        c.start()
    got2[me] = sent[me]
    for c in moves:
        c.wait()
    ab_ref[...] = got2[...]


def scalar_step(scal, rowsc, slotrow):
    vmem = pl.BlockSpec(memory_space=pltpu.VMEM)
    tokens = rowsc[0].shape[1]
    peers = scal.shape[0] - 1
    return pl.pallas_call(
        scalar_kernel,
        out_shape=(jax.ShapeDtypeStruct((2, tokens, 8), F32), jax.ShapeDtypeStruct(scal.shape, F32)),
        in_specs=[vmem] * 4,
        out_specs=[vmem] * 2,
        scratch_shapes=[pltpu.VMEM(scal.shape, F32)] * 3 + [pltpu.SemaphoreType.DMA((peers,))] * 4,
        compiler_params=pltpu.CompilerParams(collective_id=0, has_side_effects=True),
        cost_estimate=pl.CostEstimate(flops=10**9, bytes_accessed=1 << 20, transcendentals=tokens),
        name="scalar_step",
    )(scal, *rowsc, slotrow)


def result_kernel(has_old, *refs):
    x_ref, mid_ref, near_ref, far_ref, cols_ref, slotcol_ref = refs[:6]
    result_ref, hsum_ref = refs[-2:]
    tokens, width = mid_ref.shape
    chunk = 256
    chunks = near_ref.shape[0] // chunk
    lane = lane_iota(tokens, chunk)
    slot_c = [slotcol_ref[0, :, i : i + 1] for i in range(2)]

    def gather(k, carry):
        for kind, ref in enumerate((near_ref, far_ref)):
            block = ref[pl.ds(pl.multiple_of(k * chunk, chunk), chunk), :]
            base = lane + (k + kind * chunks) * chunk
            carry = tuple(
                c + mm(jnp.where(base == s, 1.0, 0.0).astype(BF16), block) for c, s in zip(carry, slot_c)
            )
        return carry

    zero = jnp.zeros((tokens, width), F32)
    picked = lax.fori_loop(0, chunks, gather, (zero, zero))
    cols = cols_ref[0]
    halting, s = cols[:, 0:1], cols[:, 1:2]
    x = x_ref[0].astype(F32)
    end = mid_ref[...] + (cols[:, 4:5] * picked[0] + cols[:, 5:6] * picked[1])
    result_ref[0] = (x + halting * (end - x)).astype(BF16)
    sub8 = lax.broadcasted_iota(jnp.int32, (8, width), 0)
    ssum = jnp.broadcast_to(jnp.sum(s, axis=0, keepdims=True), (1, width))
    hsum_ref[...] = jnp.where(sub8 == 0, fold_rows(s * end), jnp.where(sub8 == 1, ssum, 0.0))


def result_step(micro, tokens, mid, near, far, cols, slotcol, old, moving, cid):
    _, count, width = tokens.shape
    whole = lambda a: pl.BlockSpec(a.shape, lambda i: (0,) * a.ndim)
    part = pl.BlockSpec((1, count, width), lambda i: (micro, 0, 0))
    cols_spec = pl.BlockSpec((1, count, 8), lambda i: (micro, 0, 0))
    return run_kernel(
        functools.partial(result_kernel, bool(old)), (tokens, mid, near, far, cols, slotcol, *old),
        [part, whole(mid), whole(near), whole(far), cols_spec, cols_spec] + [pl.BlockSpec(memory_space=pl.ANY)] * len(old),
        (jax.ShapeDtypeStruct(tokens.shape, BF16), jax.ShapeDtypeStruct((8, width), F32)),
        [part, pl.BlockSpec((8, width), lambda i: (0, 0))], (), (1,), "result_step",
        pl.CostEstimate(
            flops=8 * count * near.shape[0] * width, bytes_accessed=5 << 20, transcendentals=count
        ),
        moving, cid, {6: 0} if old else None,
    )


def attention_backward_kernel(last, n_old, *refs):
    (x_ref, grad_ref, col_ref, vec_ref, qw_ref, kvr_ref, proj_ref, frw_ref,
     mid_ref, n2_ref, normed_ref, mixed_ref, probs_ref, qs_ref, kv_ref, gates_ref, slotcol_ref,
     near_ref, far_ref, cols_ref) = refs[:20]
    old = refs[20 : 20 + n_old]
    gtok_ref = refs[20 + n_old]
    outs = refs[21 + n_old : -6]
    gsum, gq_ref, gproj_ref, gkvr_ref, gfr_ref, gvec_ref = refs[-6:]
    step = pl.program_id(0)
    rows, width = mid_ref.shape
    lane = lane_iota(rows)
    low = lane < LANES // 2
    col = col_ref[0]
    chunk = 256
    cols = cols_ref[0]
    slot_c = [slotcol_ref[0, :, i : i + 1] for i in range(2)]
    lane_c = lane_iota(rows, chunk)
    accs = (gq_ref, gproj_ref, gkvr_ref, gfr_ref, gvec_ref)

    @pl.when(step == 0)
    def _():
        for k, ref in enumerate(accs):
            ref[...] = old[k][...] if old else jnp.zeros_like(ref)

    gsum[...] = jnp.zeros_like(gsum)

    chunks = near_ref.shape[0] // chunk

    def gather(k, carry):
        for kind, ref in enumerate((near_ref, far_ref)):
            block = ref[pl.ds(pl.multiple_of(k * chunk, chunk), chunk), :]
            base = lane_c + (k + kind * chunks) * chunk
            pick = jnp.where((base == slot_c[0]) | (base == slot_c[1]), 1.0, 0.0).astype(BF16)
            gsum[...] += mm(pick, block)
        return carry

    lax.fori_loop(0, chunks, gather, 0)
    glog = jnp.zeros((rows, LANES), F32)
    for i in range(2):
        glog = jnp.where(lane == col[:, 4 + i : 5 + i], cols[:, 2 + i : 3 + i], glog)
    glog = glog.astype(BF16)
    n2 = n2_ref[...]
    gfr_ref[...] += mm_tn(n2, glog)
    gn2 = gsum[...] + mm_nt(glog, frw_ref[...])
    hat2, rstd2 = norm_parts(mid_ref[...])
    grad = grad_ref[0].astype(F32)
    halting = cols[:, 0:1]
    gend = halting * grad + cols[:, 1:2] * vec_ref[4:5, :]
    gmid = gend + norm_back(hat2, rstd2, vec_ref[2:3, :], gn2)
    ggain2 = fold_rows(gn2 * hat2)
    gbias2 = fold_rows(gn2)
    gattn = gmid.astype(BF16)
    gproj_ref[...] += mm_tn(mixed_ref[...], gattn)
    gmixed = mm_nt(gattn, proj_ref[...]).astype(BF16).astype(F32)
    pairs = gmixed.shape[1] // LANES
    tiles = [gmixed[:, j * LANES : (j + 1) * LANES] for j in range(pairs)]
    kv = kv_ref[...]
    scale = 0.125
    routes = [col[:, i : i + 1] for i in range(4)]
    gkv = jnp.zeros((rows, LANES), F32)
    ggates = []
    parts = []
    for i in range(4):
        gate = gates_ref[:, i : i + 1]
        sel = pltpu.roll(pick_head(tiles, routes[i], lane), LANES // 2, 1)
        sel = jnp.where(low, 0.0, sel)
        probs = probs_ref[0, i]
        heads = mm(probs, kv)
        ggates.append(jnp.sum(heads * sel, axis=-1, keepdims=True))
        gheads = (gate * sel).astype(BF16)
        gprobs = mm_nt(gheads, kv)
        probs_f = probs.astype(F32)
        inner = jnp.sum(probs_f * gprobs, axis=-1, keepdims=True)
        gscores = (probs_f * (gprobs - inner)).astype(BF16)
        gkv = gkv + mm_tn(probs, gheads) + mm_tn(gscores, qs_ref[0, i]) * scale
        gq = mm(gscores, kv) * scale
        parts.append(jnp.where(low, gq, pltpu.roll(gq, LANES // 2, 1)))
    gtiles = place_heads(parts, routes, pairs, lane)
    gquery = jnp.concatenate([t.astype(BF16) for t in gtiles], axis=1)
    normed = normed_ref[...]
    gq_ref[...] += mm_tn(normed, gquery)
    mean = ggates[0] * gates_ref[:, 0:1]
    for i in range(1, 4):
        mean = mean + ggates[i] * gates_ref[:, i : i + 1]
    alog = jnp.zeros((rows, LANES), F32)
    for i in range(4):
        alog = jnp.where(lane == routes[i], gates_ref[:, i : i + 1] * (ggates[i] - mean), alog)
    gkvr = jnp.concatenate([gkv.astype(BF16), alog.astype(BF16)], axis=1)
    gkvr_ref[...] += mm_tn(normed, gkvr)
    gnormed = mm_nt(gquery, qw_ref[...]) + mm_nt(gkvr, kvr_ref[...])
    hat, rstd = norm_parts(x_ref[0].astype(F32))
    gtok_ref[0] = grad * (1.0 - halting) + gmid + norm_back(hat, rstd, vec_ref[0:1, :], gnormed)
    sub8 = lax.broadcasted_iota(jnp.int32, (8, width), 0)
    gvec = jnp.where(sub8 == 0, fold_rows(gnormed * hat), 0.0)
    gvec = jnp.where(sub8 == 1, fold_rows(gnormed), gvec)
    gvec = jnp.where(sub8 == 2, ggain2, gvec)
    gvec_ref[...] += jnp.where(sub8 == 3, gbias2, gvec)

    @pl.when(step == pl.num_programs(0) - 1)
    def _():
        if not last:
            for ref, out in zip(accs, outs):
                out[...] = ref[...]
            return
        pack, gvec_out = outs
        gvec_out[...] = gvec_ref[...]
        blocks = gq_ref.shape[1] // width
        for j in range(blocks):
            pack[j * width : (j + 1) * width, :] = gq_ref[:, j * width : (j + 1) * width].astype(BF16)
        place = blocks * width
        pack[place : place + gproj_ref.shape[0], :] = gproj_ref[...].astype(BF16)
        place = place + gproj_ref.shape[0]
        wide = gkvr_ref.shape[1]
        pack[place : place + width, :wide] = gkvr_ref[...].astype(BF16)
        pack[place : place + width, wide : wide + LANES] = gfr_ref[...].astype(BF16)
        pack[place : place + width, wide + LANES :] = jnp.zeros((width, width - wide - LANES), BF16)
        if pack.shape[0] > place + width:
            pack[place + width :, :] = jnp.zeros((pack.shape[0] - place - width, width), BF16)


def attention_backward(micro, last, packed_rows, tokens, grad, col, vec, qw, kvr, proj, frw, saved, near, far, cols, old, moving, cid):
    mid, n2, normed, mixed, probs, qs, kv, gates, slotcol = saved
    _, count, width = tokens.shape
    steps = count // SEQ
    inner = qw.shape[1]
    whole = lambda a: pl.BlockSpec(a.shape, lambda r: (0,) * a.ndim)
    by_row = lambda c: pl.BlockSpec((SEQ, c), lambda r: (r, 0))
    part = pl.BlockSpec((1, SEQ, width), lambda r: (micro, r, 0))
    out_shape = [jax.ShapeDtypeStruct(tokens.shape, F32)]
    if last:
        out_shape += [jax.ShapeDtypeStruct((packed_rows, width), BF16)]
    else:
        out_shape += [jax.ShapeDtypeStruct(a.shape, F32) for a in (qw, proj, kvr, frw)]
    out_shape += [jax.ShapeDtypeStruct((8, width), F32)]
    old_in = [old[k] for k in (1, 2, 3, 4, 5)] if old else []
    hbm = pl.BlockSpec(memory_space=pl.ANY)
    cols_spec = pl.BlockSpec((1, SEQ, 8), lambda r: (micro, r, 0))
    in_specs = [
        part, part, cols_spec,
        whole(vec), whole(qw), whole(kvr), whole(proj), whole(frw),
        by_row(width), by_row(width), by_row(width), by_row(inner),
        pl.BlockSpec((1, 4, SEQ, SEQ), lambda r: (r, 0, 0, 0)),
        pl.BlockSpec((1, 4, SEQ, LANES), lambda r: (r, 0, 0, 0)),
        by_row(LANES), by_row(8), cols_spec,
        whole(near), whole(far), cols_spec,
    ] + [whole(o) for o in old_in] + [hbm] * (1 if old else 0)
    args = (
        tokens, grad, col, vec, qw, kvr, proj, frw, mid, n2, normed, mixed, probs, qs, kv, gates, slotcol, near, far, cols,
        *old_in, *(old[:1] if old else []),
    )
    return run_kernel(
        functools.partial(attention_backward_kernel, last, len(old_in) + (1 if old else 0)), args, in_specs,
        out_shape, [part] + [pl.BlockSpec(o.shape, lambda r: (0, 0)) for o in out_shape[1:]],
        [
            pltpu.VMEM((SEQ, width), F32),
            pltpu.VMEM(qw.shape, F32),
            pltpu.VMEM(proj.shape, F32),
            pltpu.VMEM(kvr.shape, F32),
            pltpu.VMEM(frw.shape, F32),
            pltpu.VMEM((8, width), F32),
        ],
        (steps,), "attention_backward",
        pl.CostEstimate(
            flops=2 * count * width * (4 * inner + 512 + 2 * near.shape[0]), bytes_accessed=24 << 20, transcendentals=0
        ),
        moving, cid, {25: 0} if old else None,
    )


def total_plan(n_expert, n_hidden, rows):
    ny = nx = n_hidden // 2
    nz = n_expert // nx
    unit = 16 * ny * nx * nz
    units = -(-rows // (2 * unit))
    count = min(units, STREAMS)
    streams = tuple((units // count + (i < units % count)) * unit for i in range(count))
    return (nz, nx, ny), streams


def total_kernel(
    sizes, streams, pack_ref, small_ref, gq_ref, gproj_ref, gkvr_ref, gfr_ref, sum_ref,
    buf, done, core_in, land, small_got, small_part, small_got2, sems, small_sems,
):
    nz, nx, ny = sizes
    e, h = lax.axis_index("expert"), lax.axis_index("hidden")
    n_expert, n_hidden = nz * nx, ny * 2
    z, x = lax.div(e, nx), lax.rem(e, nx)
    y, c = lax.div(h, 2), lax.rem(h, 2)
    half = sum(streams)
    width = pack_ref.shape[1]
    mesh_id = pl.DeviceIdType.MESH
    barrier = pltpu.get_barrier_semaphore()
    for k in range(1, n_expert):
        pl.semaphore_signal(barrier, inc=1, device_id=(lax.rem(e + k, n_expert), h), device_id_type=mesh_id)
    for k in range(1, n_hidden):
        pl.semaphore_signal(barrier, inc=1, device_id=(e, lax.rem(h + k, n_hidden)), device_id_type=mesh_id)
    pl.semaphore_wait(barrier, n_expert + n_hidden - 2)
    used = {}

    def copy(source, target, device, pool=sems):
        i = used.get(id(pool), 0)
        used[id(pool)] = i + 1
        return pltpu.make_async_remote_copy(
            source, target, pool.at[0, i], pool.at[1, i], device_id=device, device_id_type=mesh_id
        )

    def rows_at(ref, start, count):
        return ref.at[pl.ds(pl.multiple_of(start, 16), count)]

    def add_rows(start, count, base, pieces):
        step = 64 if count % 64 == 0 else 16

        def body(i, carry):
            place = pl.ds(pl.multiple_of(start + i * step, 16), step)
            total = base[place, :].astype(F32)
            for ref in pieces:
                total = total + ref[pl.ds(pl.multiple_of(i * step, 16), step), :].astype(F32)
            buf[place, :] = total.astype(BF16)
            return carry

        lax.fori_loop(0, count // step, body, 0)

    axes = {
        "c": (2, c, lambda p: (e, y * 2 + p)),
        "y": (ny, y, lambda p: (e, p * 2 + c)),
        "x": (nx, x, lambda p: (z * nx + p, h)),
        "z": (nz, z, lambda p: (p * nx + x, h)),
    }
    landed = [0]

    def travel(first, count, order):
        moves = [copy(rows_at(pack_ref, (1 - c) * half + first, count), rows_at(core_in, first, count), axes["c"][2](1 - c))]
        for m in moves:
            m.start()
        yield
        for m in moves:
            m.wait()
        start, span = c * half + first, count
        add_rows(start, span, pack_ref, [core_in.at[pl.ds(first, count)]])
        trail = []
        for name in order:
            size, me, device = axes[name]
            chunk = span // size
            moves, pieces = [], []
            for k in range(1, size):
                peer = lax.rem(me + k, size)
                pieces.append(land.at[pl.ds(landed[0], chunk)])
                landed[0] += chunk
                moves.append(copy(rows_at(buf, start + peer * chunk, chunk), pieces[-1], device(peer)))
            for m in moves:
                m.start()
            yield
            for m in moves:
                m.wait()
            start, span = start + me * chunk, chunk
            trail.append((start, chunk, size, me, device))
            add_rows(start, span, buf, pieces)
        here = pl.ds(pl.multiple_of(start, 16), span)
        done[here, :] = buf[here, :]
        for begin, chunk, size, me, device in reversed(trail):
            place = rows_at(done, begin, chunk)
            moves = [copy(place, place, device(lax.rem(me + k, size))) for k in range(1, size)]
            for m in moves:
                m.start()
            yield
            for m in moves:
                m.wait()
        place = rows_at(done, c * half + first, count)
        moves = [copy(place, place, axes["c"][2](1 - c))]
        for m in moves:
            m.start()
        yield
        for m in moves:
            m.wait()

    def travel_small():
        moves = [
            copy(small_ref, small_got.at[e], (lax.rem(e + k, n_expert), h), small_sems) for k in range(1, n_expert)
        ]
        for m in moves:
            m.start()
        small_got[e] = small_ref[...]
        yield
        yield
        for m in moves:
            m.wait()
        small_part[...] = jnp.sum(small_got[...], axis=0)
        moves = [
            copy(small_part, small_got2.at[h], (e, lax.rem(h + k, n_hidden)), small_sems) for k in range(1, n_hidden)
        ]
        for m in moves:
            m.start()
        small_got2[h] = small_part[...]
        yield
        yield
        for m in moves:
            m.wait()
        sum_ref[...] = jnp.sum(small_got2[...], axis=0)

    going, first = [], 0
    for i, count in enumerate(streams):
        going.append(travel(first, count, ("yxz", "xyz")[i % 2]))
        first += count
    going.append(travel_small())
    while going:
        going = [g for g in going if next(g, StopIteration) is not StopIteration]
    blocks = gq_ref.shape[1] // width

    def widen(target, lanes, base, count, span):
        def body(i, carry):
            here = pl.multiple_of(i * 64, 64)
            target[pl.ds(here, 64), lanes] = done[pl.ds(base + here, 64), span].astype(F32)
            return carry

        lax.fori_loop(0, count // 64, body, 0)

    for j in range(blocks):
        widen(gq_ref, slice(j * width, (j + 1) * width), j * width, width, slice(0, width))
    base = blocks * width
    widen(gproj_ref, slice(0, width), base, gproj_ref.shape[0], slice(0, width))
    base = base + gproj_ref.shape[0]
    wide = gkvr_ref.shape[1]
    widen(gkvr_ref, slice(0, wide), base, width, slice(0, wide))
    widen(gfr_ref, slice(0, LANES), base, width, slice(wide, wide + LANES))


def total_step(n_expert, n_hidden, rows, pack, small, qw, proj, kvr, frw):
    sizes, streams = total_plan(n_expert, n_hidden, rows)
    nz, nx, ny = sizes
    width = pack.shape[1]
    half = sum(streams)
    vmem = pl.BlockSpec(memory_space=pltpu.VMEM)
    landing = 0
    for i, span in enumerate(streams):
        for size in ((ny, nx, nz), (nx, ny, nz))[i % 2]:
            span = span // size
            landing += span * (size - 1)
    steps = len(streams) * (2 + 2 * ((ny - 1) + (nx - 1) + (nz - 1)))
    return pl.pallas_call(
        functools.partial(total_kernel, sizes, streams),
        out_shape=tuple(jax.ShapeDtypeStruct(a.shape, F32) for a in (qw, proj, kvr, frw, small)),
        in_specs=[vmem] * 2,
        out_specs=[vmem] * 5,
        scratch_shapes=[
            pltpu.VMEM((2 * half, width), BF16),
            pltpu.VMEM((2 * half, width), BF16),
            pltpu.VMEM((half, width), BF16),
            pltpu.VMEM((landing, width), BF16),
            pltpu.VMEM((n_expert,) + small.shape, F32),
            pltpu.VMEM(small.shape, F32),
            pltpu.VMEM((n_hidden,) + small.shape, F32),
            pltpu.SemaphoreType.DMA((2, steps)),
            pltpu.SemaphoreType.DMA((2, n_expert + n_hidden)),
        ],
        compiler_params=pltpu.CompilerParams(collective_id=8, has_side_effects=True, vmem_limit_bytes=VMEM_LIMIT),
        name="total_step",
    )(pack, small)


def pad_lanes(a):
    return jnp.pad(a, ((0, 0), (0, LANES - a.shape[1])))


def per_device(
    tokens, grad_out, attn_routes, ffn_routes, segments, pad_mask, norm1_gain, norm1_bias, attn_router,
    query_w, key_w, value_w, attn_proj, norm2_gain, norm2_bias, ffn_router, expert_in, expert_out, halt_w, halt_b,
    *, n_expert, n_hidden,
):
    micros, count, width = tokens.shape
    experts = ffn_router.shape[1]
    capacity = 4 * count // experts
    slots = experts * capacity
    per = experts // n_expert
    group = n_expert // 2
    across = [(i, (i + group) % n_expert) for i in range(n_expert)]

    def gathered(a):
        return lax.all_gather(a, "hidden", axis=0, tiled=False)

    crossed = [lax.ppermute(a, "expert", across) for a in (expert_in, expert_out)]
    near_first, near_second = gathered(expert_in), gathered(expert_out)
    seg = segments.reshape(micros, count)
    zeros = jnp.zeros_like(seg)
    mine = lax.axis_index("expert") // group
    kind = (ffn_routes // (experts // 2) != mine).astype(jnp.int32)
    base = (kind * (experts // 2) + ffn_routes % (experts // 2)) * capacity
    col = jnp.concatenate([attn_routes, ffn_routes, seg[:, :, None], pad_mask[:, :, None]], axis=2)
    row = jnp.stack(
        [seg, pad_mask, ffn_routes[:, :, 0], ffn_routes[:, :, 1], base[:, :, 0], base[:, :, 1], zeros, zeros], axis=1
    )
    none = jnp.zeros_like(halt_w)
    vec = jnp.stack([norm1_gain, norm1_bias, norm2_gain, norm2_bias, halt_w, none, none, none])
    kvr = jnp.concatenate([key_w, value_w, pad_lanes(attn_router)], axis=1)
    frw = pad_lanes(ffn_router)
    hb = jnp.broadcast_to(halt_b.reshape(1, 1), (8, LANES))
    shape = (2, group, per, capacity, width)
    packed = query_w.size // width + attn_proj.shape[0] + width
    packed_rows = 2 * sum(total_plan(n_expert, n_hidden, packed)[1])

    slotrow, slotcol = route_step(row)
    weights = (vec, hb, query_w, kvr, attn_proj, frw)
    f0 = attention_forward(0, tokens, grad_out, col, row, slotrow, *weights, slots, (), None)
    crossed[0], n0_out = lax.optimization_barrier((crossed[0], f0[9]))
    far_first = gathered(crossed[0])
    *f1, n0 = attention_forward(1, tokens, grad_out, col, row, slotrow, *weights, slots, [n0_out.reshape(shape)], 2)
    crossed[1], n1_out = lax.optimization_barrier((crossed[1], f1[9]))
    far_second = gathered(crossed[1])
    gs0, gs1, n1 = spread_step(slotrow, grad_out, slots, [n1_out.reshape(shape)], 3)
    rows = (n0, n1)
    y0, y1, g1 = expert_forward(0, rows, near_first, near_second, [gs1.reshape(shape)], 4)
    far0, far1, g0 = expert_forward(1, rows, far_first, far_second, [gs0.reshape(shape)], 1)
    grads = (g0, g1)
    scal = reading_step((y0, y1, far0, far1), grads, vec)
    cols, ab = scalar_step(scal, (f0[8], f1[8]), slotrow)
    gf_far, gs_far, bf0, bf1, r0, rf0, r1 = expert_backward(
        1, rows, grads, ab, vec, far_first, far_second, [y0, far0, y1], 9
    )
    gf_near, gs_near, bn0, bn1, qf0, qf1, rf1 = expert_backward(
        0, rows, grads, ab, vec, near_first, near_second, [bf0, bf1, far1], 10
    )

    flat = lambda a: a.reshape(slots // 2, width)

    def reduced(a):
        return lax.psum_scatter(a, "hidden", scatter_dimension=0, tiled=False)

    far_grads = [reduced(a) for a in (gf_far, gs_far)]
    near_grads = [reduced(a) for a in (gf_near, gs_near)]
    *res0, qn0, qn1 = result_step(0, tokens, f0[0], flat(r0), flat(rf0), cols, slotcol, (), [bn0, bn1], 11)
    common = (tokens, grad_out, col, vec, query_w, kvr, attn_proj, frw)
    far_grads[0], qn0 = lax.optimization_barrier((far_grads[0], qn0))
    far_grads[0] = lax.ppermute(far_grads[0], "expert", across)
    out = attention_backward(
        0, False, packed_rows, *common, list(f0[:8]) + [slotcol], flat(qn0), flat(qf0), cols, (), (), None
    )
    res1 = result_step(1, tokens, f1[0], flat(r1), flat(rf1), cols, slotcol, tuple(res0[:1]), (), None)
    out, far_grads, res1 = lax.optimization_barrier((tuple(out), far_grads, tuple(res1)))
    far_grads[1] = lax.ppermute(far_grads[1], "expert", across)
    out = attention_backward(
        1, True, packed_rows, *common, list(f1[:8]) + [slotcol], flat(qn1), flat(qf1), cols, tuple(out), (), None
    )
    packs = out[1]
    gfirst, gsecond = [a.astype(F32) + b.astype(F32) for a, b in zip(near_grads, far_grads)]
    small = jnp.concatenate([out[2], res0[1] + res1[1]], axis=0)
    gq, gproj, gkvr, gfr, small = total_step(
        n_expert, n_hidden, packed, packs, small, query_w, attn_proj, kvr, frw
    )
    head = key_w.shape[1]
    return (
        res1[0],
        out[0],
        small[0],
        small[1],
        gkvr[:, LANES : LANES + attn_router.shape[1]],
        gq,
        gkvr[:, :head],
        gkvr[:, head : 2 * head],
        gproj,
        small[2],
        small[3],
        gfr[:, :experts],
        gfirst,
        gsecond,
        small[8],
        small[9, :1],
    )


def solution(mesh):
    rows = P(None, ("expert", "hidden"), None)
    in_specs = (rows,) * 5 + (P(None, ("expert", "hidden")),) + (P(),) * 10 + (
        P("expert", None, "hidden"), P("expert", "hidden", None), P(), P(),
    )
    out_specs = (rows,) * 2 + (P(),) * 10 + (P("expert", None, "hidden"), P("expert", "hidden", None), P(), P())
    return jax.shard_map(
        functools.partial(per_device, n_expert=mesh.shape["expert"], n_hidden=mesh.shape["hidden"]),
        mesh=mesh, in_specs=in_specs, out_specs=out_specs, check_vma=False,
    )
```

```python
import functools
import math

import jax
import jax.numpy as jnp
from jax import lax
from jax.experimental import pallas as pl
from jax.experimental.pallas import tpu as pltpu
from jax.sharding import PartitionSpec as P

SEQ = 256
LANES = 128
F32 = jnp.float32
BF16 = jnp.bfloat16
GELU_C = math.sqrt(2.0 / math.pi)
GELU_A = 0.044715
VMEM_LIMIT = 60 * 1024 * 1024
STREAMS = 7


def mm(left, right):
    return jnp.dot(left, right, preferred_element_type=F32)


def mm_nt(left, right):
    return lax.dot_general(left, right, (((1,), (1,)), ((), ())), preferred_element_type=F32)


def mm_tn(left, right):
    return lax.dot_general(left, right, (((0,), (0,)), ((), ())), preferred_element_type=F32)


def lane_iota(rows, lanes=LANES):
    return lax.broadcasted_iota(jnp.int32, (rows, lanes), 1)


def norm_parts(value):
    center = value - jnp.mean(value, axis=-1, keepdims=True)
    rstd = lax.rsqrt(jnp.mean(center * center, axis=-1, keepdims=True) + 1e-05)
    return center * rstd, rstd


def norm_back(hat, rstd, gain, grad):
    scaled = grad * gain
    first = jnp.mean(scaled, axis=-1, keepdims=True)
    second = jnp.mean(scaled * hat, axis=-1, keepdims=True)
    return rstd * (scaled - first - hat * second)


def fold_rows(value):
    return jnp.sum(value, axis=0, keepdims=True)


def pick_head(tiles, route, lane):
    route = jnp.broadcast_to(route, lane.shape)
    pair = lax.shift_right_logical(route, 1)
    out = tiles[0]
    for j in range(1, len(tiles)):
        out = jnp.where(pair == j, tiles[j], out)
    odd = (route & 1) == 1
    return jnp.where(odd, pltpu.roll(out, LANES // 2, 1), out)


def place_heads(parts, routes, count, lane):
    half = lax.shift_right_logical(lane, 6)
    routes = [jnp.broadcast_to(r, lane.shape) for r in routes]
    kept = [jnp.where(half == (r & 1), p, 0.0) for p, r in zip(parts, routes)]
    pairs = [lax.shift_right_logical(r, 1) for r in routes]
    tiles = []
    for j in range(count):
        total = jnp.where(pairs[0] == j, kept[0], 0.0)
        for k, p in zip(kept[1:], pairs[1:]):
            total = total + jnp.where(p == j, k, 0.0)
        tiles.append(total)
    return tiles


def softmax_cols(cols):
    top = functools.reduce(jnp.maximum, cols)
    expo = [jnp.exp(c - top) for c in cols]
    total = functools.reduce(jnp.add, expo)
    return [e / total for e in expo]


def put_cols(cols, rows, width):
    lane = lane_iota(rows, width)
    out = jnp.zeros((rows, width), cols[0].dtype)
    for i, c in enumerate(cols):
        out = jnp.where(lane == i, c, out)
    return out


def split_three(value):
    high = value.astype(BF16)
    rest = value - high.astype(F32)
    middle = rest.astype(BF16)
    last = (rest - middle.astype(F32)).astype(BF16)
    return jnp.concatenate([high.astype(F32), middle.astype(F32), last.astype(F32)], axis=0).astype(BF16)


def join_three(value):
    n = value.shape[0] // 3
    return value[:n] + value[n : 2 * n] + value[2 * n :]


def row_to_col(row):
    n = row.shape[1]
    place = lax.broadcasted_iota(jnp.int32, (n, n), 0)
    other = lax.broadcasted_iota(jnp.int32, (n, n), 1)
    return jnp.sum(jnp.where(place == other, row, 0.0), axis=-1, keepdims=True)


def dispatch(slot_rows, values, out_ref):
    chunk = 256
    tokens = values[0].shape[0]
    spot = lax.broadcasted_iota(jnp.int32, (chunk, tokens), 0)

    def body(k, carry):
        base = spot + k * chunk
        if len(values) == 1:
            pick = jnp.where((base == slot_rows[0]) | (base == slot_rows[1]), 1.0, 0.0).astype(BF16)
            out = mm(pick, values[0][...])
        else:
            out = mm(jnp.where(base == slot_rows[0], 1.0, 0.0).astype(BF16), values[0][...])
            out = out + mm(jnp.where(base == slot_rows[1], 1.0, 0.0).astype(BF16), values[1][...])
        out_ref[pl.ds(pl.multiple_of(k * chunk, chunk), chunk), :] = out.astype(BF16)
        return carry

    lax.fori_loop(0, out_ref.shape[0] // chunk, body, 0)


def group_of():
    size = lax.axis_size("expert") // 2
    e = lax.axis_index("expert")
    me = lax.rem(e, size)
    return me, size, e - me


def group_greet():
    me, size, base = group_of()
    other = lax.axis_index("hidden")
    barrier = pltpu.get_barrier_semaphore()
    for k in range(1, size):
        pl.semaphore_signal(
            barrier, inc=1, device_id=(base + lax.rem(me + k, size), other), device_id_type=pl.DeviceIdType.MESH
        )
    pl.semaphore_wait(barrier, size - 1)


def group_copies(source, target, send_sem, recv_sem):
    me, size, base = group_of()
    other = lax.axis_index("hidden")
    moves = []
    for k in range(1, size):
        peer = lax.rem(me + k, size)
        moves.append(
            pltpu.make_async_remote_copy(
                source.at[peer], target.at[me], send_sem.at[k - 1], recv_sem.at[k - 1],
                device_id=(base + peer, other), device_id_type=pl.DeviceIdType.MESH,
            )
        )
    return moves


def at_step(which):
    found = True
    for axis, size in enumerate(which[1]):
        here = pl.program_id(axis) == (0 if which[0] == 0 else size - 1)
        found = here if found is True else found & here
    return found


def run_kernel(kernel, args, in_specs, out_shape, out_specs, scratch, grid, name, cost, moving=(), cid=None, aliases=None):
    n_in, n_out, n_move = len(args), len(out_shape), len(moving)
    peers = lax.axis_size("expert") // 2 - 1
    hbm = pl.BlockSpec(memory_space=pl.ANY)

    def body(*refs):
        ins, sources = refs[:n_in], refs[n_in : n_in + n_move]
        outs = refs[n_in + n_move : n_in + n_move + n_out]
        targets = refs[n_in + n_move + n_out : n_in + 2 * n_move + n_out]
        rest = refs[n_in + 2 * n_move + n_out :]
        sems = rest[len(scratch) :]
        moves, owns = [], []
        me = group_of()[0]
        pairs = []
        for a, b in zip(sources, targets):
            pairs += [(a, b)] if len(a.shape) == 4 else [(a.at[i], b.at[i]) for i in range(a.shape[0])]
        for i, (a, b) in enumerate(pairs):
            moves += group_copies(a, b, sems[3 * i], sems[3 * i + 1])
            owns.append(pltpu.make_async_copy(a.at[me], b.at[me], sems[3 * i + 2]))

        if moving:

            @pl.when(at_step((0, grid)))
            def _():
                group_greet()
                for c in moves + owns:
                    c.start()

        kernel(*ins, *outs, *rest[: len(scratch)])

        if moving:

            @pl.when(at_step((1, grid)))
            def _():
                for c in moves + owns:
                    c.wait()

    sems = []
    for _ in range(sum(1 if a.ndim == 4 else a.shape[0] for a in moving)):
        sems += [pltpu.SemaphoreType.DMA((peers,)), pltpu.SemaphoreType.DMA((peers,)), pltpu.SemaphoreType.DMA]
    more = dict(collective_id=cid, has_side_effects=True) if moving else {}
    return pl.pallas_call(
        body,
        grid=grid,
        out_shape=tuple(out_shape) + tuple(jax.ShapeDtypeStruct(a.shape, a.dtype) for a in moving),
        in_specs=list(in_specs) + [hbm] * n_move,
        out_specs=list(out_specs) + [hbm] * n_move,
        scratch_shapes=list(scratch) + sems,
        input_output_aliases=aliases or {},
        compiler_params=pltpu.CompilerParams(vmem_limit_bytes=VMEM_LIMIT, **more),
        cost_estimate=cost,
        name=name,
    )(*args, *moving)


def route_kernel(row_ref, slotrow_ref, slotcol_ref):
    tokens = row_ref.shape[2]
    before = lax.broadcasted_iota(jnp.int32, (tokens, tokens), 0)
    after = lax.broadcasted_iota(jnp.int32, (tokens, tokens), 1)
    upper = jnp.where(before < after, 1.0, 0.0).astype(BF16)
    sub = lax.broadcasted_iota(jnp.int32, (LANES, tokens), 0)
    sub8 = lax.broadcasted_iota(jnp.int32, (8, tokens), 0)
    for m in range(row_ref.shape[0]):
        row = row_ref[m]
        named = [jnp.where(sub == row[2 + i : 3 + i, :], 1.0, 0.0) for i in range(2)]
        rank = mm((named[0] + named[1]).astype(BF16), upper)
        slots = [fold_rows(named[i] * rank).astype(jnp.int32) + row[4 + i : 5 + i, :] for i in range(2)]
        slotrow_ref[m] = jnp.where(sub8 == 0, slots[0], slots[1])
        table = jnp.where(sub == 0, slots[0].astype(F32), slots[1].astype(F32))
        slotcol_ref[m] = jnp.transpose(table)[:, :8].astype(jnp.int32)


def route_step(row):
    micros, _, count = row.shape
    out_shape = (
        jax.ShapeDtypeStruct((micros, 8, count), jnp.int32),
        jax.ShapeDtypeStruct((micros, count, 8), jnp.int32),
    )
    whole = lambda s: pl.BlockSpec(s, lambda i: (0,) * len(s))
    return run_kernel(
        route_kernel, (row,), [whole(row.shape)], out_shape, [whole(o.shape) for o in out_shape], (), (1,), "route_step",
        pl.CostEstimate(flops=10**8, bytes_accessed=1 << 20, transcendentals=0),
    )


def spread_kernel(slotrow_ref, grad_ref, out0_ref, out1_ref):
    for m, out_ref in enumerate((out0_ref, out1_ref)):
        dispatch([slotrow_ref[m, 0:1, :], slotrow_ref[m, 1:2, :]], [grad_ref.at[m]], out_ref)


def spread_step(slotrow, grad, slots, moving, cid):
    width = grad.shape[2]
    whole = lambda s: pl.BlockSpec(s, lambda i: (0,) * len(s))
    return run_kernel(
        spread_kernel, (slotrow, grad), [whole(slotrow.shape), whole(grad.shape)],
        [jax.ShapeDtypeStruct((slots, width), BF16)] * 2, [whole((slots, width))] * 2, (), (1,), "spread_step",
        pl.CostEstimate(flops=8 * slots * width * grad.shape[1], bytes_accessed=6 << 20, transcendentals=0), moving, cid,
    )


def attention_forward_kernel(
    x_ref, grad_ref, col_ref, row_ref, slotrow_ref, vec_ref, hb_ref, qw_ref, kvr_ref, proj_ref, frw_ref,
    mid_ref, n2_ref, normed_ref, mixed_ref, probs_ref, qs_ref, kv_ref, gates_ref, scal_ref, out_ref,
    n2_all,
):
    step = pl.program_id(0)
    rows = x_ref.shape[1]
    top_attn = 4
    lane = lane_iota(rows)
    x = x_ref[0].astype(F32)
    col = col_ref[0]
    row = row_ref[0]
    hat, _ = norm_parts(x)
    normed = (hat * vec_ref[0:1, :] + vec_ref[1:2, :]).astype(BF16)
    normed_ref[...] = normed
    kvr = mm(normed, kvr_ref[...])
    kv = kvr[:, :LANES].astype(BF16)
    kv_ref[...] = kv
    logits = kvr[:, LANES:]
    routes = [col[:, i : i + 1] for i in range(top_attn)]
    picked = [
        jnp.sum(jnp.where(lane == r, logits, 0.0), axis=-1, keepdims=True) for r in routes
    ]
    gates = softmax_cols(picked)
    query = mm(normed, qw_ref[...])
    heads_pairs = query.shape[1] // LANES
    tiles = [query[:, j * LANES : (j + 1) * LANES] for j in range(heads_pairs)]
    low = lane < LANES // 2
    same = col[:, 6:7] == row[0:1, :]
    place = lax.broadcasted_iota(jnp.int32, (rows, rows), 0)
    other = lax.broadcasted_iota(jnp.int32, (rows, rows), 1)
    allowed = same & ((row[1:2, :] == 1) | (place == other))
    scale = 0.125
    shares = []
    for i in range(top_attn):
        sel = jnp.where(low, pick_head(tiles, routes[i], lane), 0.0).astype(BF16)
        qs_ref[0, i] = sel
        scores = mm_nt(sel, kv) * scale
        scores = jnp.where(allowed, scores, -1e30)
        expo = jnp.exp(scores - jnp.max(scores, axis=-1, keepdims=True))
        probs = (expo * (1.0 / jnp.sum(expo, axis=-1, keepdims=True))).astype(BF16)
        probs_ref[0, i] = probs
        heads = mm(probs, kv) * gates[i]
        shares.append(jnp.where(low, pltpu.roll(heads, LANES // 2, 1), heads))
    mixed_tiles = place_heads(shares, routes, heads_pairs, lane)
    mixed = jnp.concatenate([t.astype(BF16) for t in mixed_tiles], axis=1)
    mixed_ref[...] = mixed
    mid = x + mm(mixed, proj_ref[...])
    mid_ref[...] = mid
    hat2, _ = norm_parts(mid)
    n2 = (hat2 * vec_ref[2:3, :] + vec_ref[3:4, :]).astype(BF16)
    n2_ref[...] = n2
    n2_all[pl.ds(pl.multiple_of(step * rows, rows), rows), :] = n2
    logits_ffn = mm(n2, frw_ref[...])
    gates_ffn = softmax_cols(
        [
            jnp.sum(jnp.where(lane == col[:, 4 + i : 5 + i], logits_ffn, 0.0), axis=-1, keepdims=True)
            for i in range(2)
        ]
    )
    gates_ref[...] = put_cols(gates, rows, gates_ref.shape[1])
    stop = jnp.sum(mid * vec_ref[4:5, :], axis=-1, keepdims=True) + hb_ref[0:1, 0:1]
    pull = jnp.sum(grad_ref[0].astype(F32) * (mid - x), axis=-1, keepdims=True)
    scal_ref[...] = jnp.transpose(put_cols([stop, pull] + gates_ffn, rows, LANES))[:8, :]

    @pl.when(step == pl.num_programs(0) - 1)
    def _():
        dispatch([slotrow_ref[0, 0:1, :], slotrow_ref[0, 1:2, :]], [n2_all], out_ref)


def attention_forward(micro, tokens, grad, col, row, slotrow, vec, hb, qw, kvr, proj, frw, slots, moving, cid):
    _, count, width = tokens.shape
    steps = count // SEQ
    inner = qw.shape[1]
    whole = lambda a: pl.BlockSpec(a.shape, lambda r: (0,) * a.ndim)
    out_shape = (
        jax.ShapeDtypeStruct((count, width), F32),
        jax.ShapeDtypeStruct((count, width), BF16),
        jax.ShapeDtypeStruct((count, width), BF16),
        jax.ShapeDtypeStruct((count, inner), BF16),
        jax.ShapeDtypeStruct((steps, 4, SEQ, SEQ), BF16),
        jax.ShapeDtypeStruct((steps, 4, SEQ, LANES), BF16),
        jax.ShapeDtypeStruct((count, LANES), BF16),
        jax.ShapeDtypeStruct((count, 8), F32),
        jax.ShapeDtypeStruct((8, count), F32),
        jax.ShapeDtypeStruct((slots, width), BF16),
    )
    by_row = lambda c: pl.BlockSpec((SEQ, c), lambda r: (r, 0))
    in_specs = [
        pl.BlockSpec((1, SEQ, width), lambda r: (micro, r, 0)),
        pl.BlockSpec((1, SEQ, width), lambda r: (micro, r, 0)),
        pl.BlockSpec((1, SEQ, 8), lambda r: (micro, r, 0)),
        pl.BlockSpec((1, 8, SEQ), lambda r: (micro, 0, r)),
        pl.BlockSpec((1, 8, count), lambda r: (micro, 0, 0)),
        whole(vec), whole(hb), whole(qw), whole(kvr), whole(proj), whole(frw),
    ]
    out_specs = [
        by_row(width), by_row(width), by_row(width), by_row(inner),
        pl.BlockSpec((1, 4, SEQ, SEQ), lambda r: (r, 0, 0, 0)),
        pl.BlockSpec((1, 4, SEQ, LANES), lambda r: (r, 0, 0, 0)),
        by_row(LANES), by_row(8),
        pl.BlockSpec((8, SEQ), lambda r: (0, r)),
        pl.BlockSpec((slots, width), lambda r: (0, 0)),
    ]
    return run_kernel(
        attention_forward_kernel, (tokens, grad, col, row, slotrow, vec, hb, qw, kvr, proj, frw), in_specs,
        out_shape, out_specs, [pltpu.VMEM((count, width), BF16)], (steps,), "attention_forward",
        pl.CostEstimate(
            flops=2 * count * width * (2 * inner + 256 + slots), bytes_accessed=12 << 20, transcendentals=count * 4 * SEQ
        ),
        moving, cid,
    )


def gelu_parts(pre):
    square = pre * pre
    inner = jnp.tanh(GELU_C * pre * (1.0 + GELU_A * square))
    return square, inner


def expert_forward_kernel(rows0_ref, rows1_ref, first_ref, second_ref, out0_ref, out1_ref, total):
    part = pl.program_id(1)
    _, src, _, cap, width = rows0_ref.shape
    half = src * cap
    rows = jnp.concatenate([r[...].reshape(half, width) for r in (rows0_ref, rows1_ref)], axis=0)
    pre = mm(rows, first_ref[0, 0])
    _, inner = gelu_parts(pre)
    act = (0.5 * pre * (1.0 + inner)).astype(BF16)
    res = mm(act, second_ref[0, 0])

    @pl.when(part == 0)
    def _():
        total[...] = res

    @pl.when(part > 0)
    def _():
        total[...] += res

    @pl.when(part == pl.num_programs(1) - 1)
    def _():
        out0_ref[...] = total[:half, :].astype(BF16).reshape(out0_ref.shape)
        out1_ref[...] = total[half:, :].astype(BF16).reshape(out1_ref.shape)


def expert_forward(kind, rows, first, second, moving, cid):
    _, src, local, cap, width = rows[0].shape
    parts, _, _, hid = first.shape
    spec_in = pl.BlockSpec((1, src, 1, cap, width), lambda e, h: (kind, 0, e, 0, 0))
    spec_rows = pl.BlockSpec((src, 1, cap, width), lambda e, h: (0, e, 0, 0))
    work = 2 * src * local * cap * width * hid * parts
    return run_kernel(
        expert_forward_kernel, (*rows, first, second),
        [
            spec_in, spec_in,
            pl.BlockSpec((1, 1, width, hid), lambda e, h: (h, e, 0, 0)),
            pl.BlockSpec((1, 1, hid, width), lambda e, h: (h, e, 0, 0)),
        ],
        [jax.ShapeDtypeStruct(r.shape[1:], BF16) for r in rows], [spec_rows] * 2,
        [pltpu.VMEM((2 * src * cap, width), F32)], (local, parts), "expert_forward",
        pl.CostEstimate(flops=4 * work, bytes_accessed=24 << 20, transcendentals=work // width), moving, cid,
    )


def reading_kernel(*refs):
    outs, grads = refs[:4], refs[4:8]
    vec_ref, scal_ref = refs[8:]
    src, _, cap, width = outs[0].shape
    halt = split_three(jnp.broadcast_to(vec_ref[4:5, :], (8, width)))
    ones = jnp.ones((8, width), BF16)
    sub8 = lax.broadcasted_iota(jnp.int32, (8, cap), 0)
    for kind in range(2):
        for m in range(2):
            for s in range(src):
                low = outs[2 * kind + m][s, 0]
                stop = join_three(mm_nt(halt, low))
                prod = low.astype(F32) * grads[2 * kind + m][0, s, 0].astype(F32)
                high = prod.astype(BF16)
                rest = (prod - high.astype(F32)).astype(BF16)
                pull = mm_nt(ones, high) + mm_nt(ones, rest)
                scal_ref[s, m, kind, 0] = jnp.where(sub8 == 0, stop, pull)


def reading_step(outs, grads, vec):
    src, local, cap, width = outs[0].shape
    spec_rows = pl.BlockSpec((src, 1, cap, width), lambda e: (0, e, 0, 0))
    spec_grad = lambda kind: pl.BlockSpec((1, src, 1, cap, width), lambda e: (kind, 0, e, 0, 0))
    return run_kernel(
        reading_kernel, (*outs, *grads, *grads, vec),
        [spec_rows] * 4 + [spec_grad(0)] * 2 + [spec_grad(1)] * 2 + [pl.BlockSpec(vec.shape, lambda e: (0, 0))],
        [jax.ShapeDtypeStruct((src, 2, 2, local, 8, cap), F32)],
        [pl.BlockSpec((src, 2, 2, 1, 8, cap), lambda e: (0, 0, 0, e, 0, 0))], (), (local,), "reading_step",
        pl.CostEstimate(flops=10**9, bytes_accessed=8 << 20, transcendentals=0),
    )[0].reshape(src, 2, 2 * local, 8, cap)


def expert_backward_kernel(
    rows0_ref, rows1_ref, grad0_ref, grad1_ref, ab_ref, vec_ref, first_ref, second_ref,
    gfirst_ref, gsecond_ref, out0_ref, out1_ref, total, gin_all,
):
    part = pl.program_id(1)
    _, src, _, cap, width = rows0_ref.shape
    half = src * cap

    @pl.when(part == 0)
    def _():
        for m, grad_ref in enumerate((grad0_ref, grad1_ref)):
            for s in range(src):
                ab = ab_ref[s, m, 0]
                scaled = row_to_col(ab[0:1, :]) * grad_ref[0, s, 0].astype(F32) + row_to_col(ab[1:2, :]) * vec_ref[4:5, :]
                gin_all[m * half + s * cap : m * half + (s + 1) * cap, :] = scaled.astype(BF16)

    rows = jnp.concatenate([r[...].reshape(half, width) for r in (rows0_ref, rows1_ref)], axis=0)
    gin = gin_all[...]
    first = first_ref[0, 0]
    second = second_ref[0, 0]
    pre = mm(rows, first)
    gact = mm_nt(gin, second)
    square, inner = gelu_parts(pre)
    part_one = 0.5 * (1.0 + inner)
    act = (pre * part_one).astype(BF16)
    slope = part_one + 0.5 * pre * (1.0 - inner * inner) * (GELU_C + (3.0 * GELU_C * GELU_A) * square)
    gpre = (gact * slope).astype(BF16)
    gsecond_ref[0, 0] = mm_tn(act, gin).astype(BF16)
    gfirst_ref[0, 0] = mm_tn(rows, gpre).astype(BF16)
    res = mm_nt(gpre, first)

    @pl.when(part == 0)
    def _():
        total[...] = res

    @pl.when(part > 0)
    def _():
        total[...] += res

    @pl.when(part == pl.num_programs(1) - 1)
    def _():
        out0_ref[...] = total[:half, :].astype(BF16).reshape(out0_ref.shape)
        out1_ref[...] = total[half:, :].astype(BF16).reshape(out1_ref.shape)


def expert_backward(kind, rows, grads, ab, vec, first, second, moving, cid):
    _, src, local, cap, width = rows[0].shape
    parts, _, _, hid = first.shape
    spec_in = pl.BlockSpec((1, src, 1, cap, width), lambda e, h: (kind, 0, e, 0, 0))
    spec_rows = pl.BlockSpec((src, 1, cap, width), lambda e, h: (0, e, 0, 0))
    spec_first = pl.BlockSpec((1, 1, width, hid), lambda e, h: (h, e, 0, 0))
    spec_second = pl.BlockSpec((1, 1, hid, width), lambda e, h: (h, e, 0, 0))
    work = 2 * src * local * cap * width * hid * parts
    return run_kernel(
        expert_backward_kernel, (*rows, *grads, ab, vec, first, second),
        [spec_in] * 4
        + [pl.BlockSpec((src, 2, 1, 8, cap), lambda e, h: (0, 0, kind * local + e, 0, 0)), pl.BlockSpec(vec.shape, lambda e, h: (0, 0))]
        + [spec_first, spec_second],
        [jax.ShapeDtypeStruct(first.shape, BF16), jax.ShapeDtypeStruct(second.shape, BF16)]
        + [jax.ShapeDtypeStruct(r.shape[1:], BF16) for r in rows],
        [spec_first, spec_second, spec_rows, spec_rows],
        [pltpu.VMEM((2 * src * cap, width), F32), pltpu.VMEM((2 * src * cap, width), BF16)],
        (local, parts), "expert_backward",
        pl.CostEstimate(flops=10 * work, bytes_accessed=48 << 20, transcendentals=work // width), moving, cid,
    )


def scalar_kernel(scal_ref, rowsc0_ref, rowsc1_ref, slotrow_ref, cols_ref, ab_ref, got, sent, got2, send_sem, recv_sem, send_sem2, recv_sem2):
    src, micros, local, _, cap = scal_ref.shape
    tokens = rowsc0_ref.shape[1]
    me = group_of()[0]
    group_greet()
    moves = group_copies(scal_ref, got, send_sem, recv_sem)
    for c in moves:
        c.start()
    got[me] = scal_ref[me]
    for c in moves:
        c.wait()
    spot = lax.broadcasted_iota(jnp.int32, (cap, tokens), 0)
    sub = lax.broadcasted_iota(jnp.int32, (LANES, tokens), 0)
    sub8 = lax.broadcasted_iota(jnp.int32, (8, tokens), 0)
    slots = [[slotrow_ref[m, i : i + 1, :] for i in range(2)] for m in range(micros)]

    def onehot(m, s, which):
        per = local // 2
        base = (which // per) * (src * per) + s * per + which % per
        base = spot + base * cap
        return [jnp.where(base == t, 1.0, 0.0).astype(BF16) for t in slots[m]]

    zero = jnp.zeros((24, tokens), F32)

    def collect(s, carry):
        carry = list(carry)
        for which in range(local):
            for m in range(micros):
                values = split_three(got[s, m, which])
                for i, p in enumerate(onehot(m, s, which)):
                    carry[2 * m + i] = carry[2 * m + i] + mm(values, p)
        return tuple(carry)

    found_all = [join_three(f) for f in lax.fori_loop(0, src, collect, (zero,) * (2 * micros))]
    shares = []
    for m, rowsc_ref in enumerate((rowsc0_ref, rowsc1_ref)):
        found = found_all[2 * m : 2 * m + 2]
        stop, pull, gate0, gate1 = [rowsc_ref[i : i + 1, :] for i in range(4)]
        gates = [gate0, gate1]
        yh = [f[0:1, :] for f in found]
        yg = [f[1:2, :] for f in found]
        halting = jax.nn.sigmoid(stop + gate0 * yh[0] + gate1 * yh[1])
        s = (pull + gate0 * yg[0] + gate1 * yg[1]) * halting * (1.0 - halting)
        u = [halting * g + s * h for g, h in zip(yg, yh)]
        mean = gate0 * u[0] + gate1 * u[1]
        keep = [halting, s, gate0 * (u[0] - mean), gate1 * (u[1] - mean), gate0, gate1]
        table = jnp.zeros((LANES, tokens), F32)
        for i, r in enumerate(keep):
            table = jnp.where(sub == i, r, table)
        cols_ref[m] = jnp.transpose(table)[:, :8]
        shares.append(
            [split_three(jnp.where(sub8 == 0, g * halting, jnp.where(sub8 == 1, g * s, 0.0))) for g in gates]
        )

    def spread(s, carry):
        for which in range(local):
            for m in range(micros):
                picks = onehot(m, s, which)
                sent[s, m, which] = join_three(mm_nt(shares[m][0], picks[0]) + mm_nt(shares[m][1], picks[1]))
        return carry

    lax.fori_loop(0, src, spread, 0)
    moves = group_copies(sent, got2, send_sem2, recv_sem2)
    for c in moves:
        c.start()
    got2[me] = sent[me]
    for c in moves:
        c.wait()
    ab_ref[...] = got2[...]


def scalar_step(scal, rowsc, slotrow):
    vmem = pl.BlockSpec(memory_space=pltpu.VMEM)
    tokens = rowsc[0].shape[1]
    peers = scal.shape[0] - 1
    return pl.pallas_call(
        scalar_kernel,
        out_shape=(jax.ShapeDtypeStruct((2, tokens, 8), F32), jax.ShapeDtypeStruct(scal.shape, F32)),
        in_specs=[vmem] * 4,
        out_specs=[vmem] * 2,
        scratch_shapes=[pltpu.VMEM(scal.shape, F32)] * 3 + [pltpu.SemaphoreType.DMA((peers,))] * 4,
        compiler_params=pltpu.CompilerParams(collective_id=0, has_side_effects=True),
        cost_estimate=pl.CostEstimate(flops=10**9, bytes_accessed=1 << 20, transcendentals=tokens),
        name="scalar_step",
    )(scal, *rowsc, slotrow)


def result_kernel(has_old, *refs):
    x_ref, mid_ref, near_ref, far_ref, cols_ref, slotcol_ref = refs[:6]
    result_ref, hsum_ref = refs[-2:]
    tokens, width = mid_ref.shape
    chunk = 256
    chunks = near_ref.shape[0] // chunk
    lane = lane_iota(tokens, chunk)
    slot_c = [slotcol_ref[0, :, i : i + 1] for i in range(2)]

    def gather(k, carry):
        for kind, ref in enumerate((near_ref, far_ref)):
            block = ref[pl.ds(pl.multiple_of(k * chunk, chunk), chunk), :]
            base = lane + (k + kind * chunks) * chunk
            carry = tuple(
                c + mm(jnp.where(base == s, 1.0, 0.0).astype(BF16), block) for c, s in zip(carry, slot_c)
            )
        return carry

    zero = jnp.zeros((tokens, width), F32)
    picked = lax.fori_loop(0, chunks, gather, (zero, zero))
    cols = cols_ref[0]
    halting, s = cols[:, 0:1], cols[:, 1:2]
    x = x_ref[0].astype(F32)
    end = mid_ref[...] + (cols[:, 4:5] * picked[0] + cols[:, 5:6] * picked[1])
    result_ref[0] = (x + halting * (end - x)).astype(BF16)
    sub8 = lax.broadcasted_iota(jnp.int32, (8, width), 0)
    ssum = jnp.broadcast_to(jnp.sum(s, axis=0, keepdims=True), (1, width))
    hsum_ref[...] = jnp.where(sub8 == 0, fold_rows(s * end), jnp.where(sub8 == 1, ssum, 0.0))


def result_step(micro, tokens, mid, near, far, cols, slotcol, old, moving, cid):
    _, count, width = tokens.shape
    whole = lambda a: pl.BlockSpec(a.shape, lambda i: (0,) * a.ndim)
    part = pl.BlockSpec((1, count, width), lambda i: (micro, 0, 0))
    cols_spec = pl.BlockSpec((1, count, 8), lambda i: (micro, 0, 0))
    return run_kernel(
        functools.partial(result_kernel, bool(old)), (tokens, mid, near, far, cols, slotcol, *old),
        [part, whole(mid), whole(near), whole(far), cols_spec, cols_spec] + [pl.BlockSpec(memory_space=pl.ANY)] * len(old),
        (jax.ShapeDtypeStruct(tokens.shape, BF16), jax.ShapeDtypeStruct((8, width), F32)),
        [part, pl.BlockSpec((8, width), lambda i: (0, 0))], (), (1,), "result_step",
        pl.CostEstimate(
            flops=8 * count * near.shape[0] * width, bytes_accessed=5 << 20, transcendentals=count
        ),
        moving, cid, {6: 0} if old else None,
    )


def attention_backward_kernel(last, n_old, *refs):
    (x_ref, grad_ref, col_ref, vec_ref, qw_ref, kvr_ref, proj_ref, frw_ref,
     mid_ref, n2_ref, normed_ref, mixed_ref, probs_ref, qs_ref, kv_ref, gates_ref, slotcol_ref,
     near_ref, far_ref, cols_ref) = refs[:20]
    old = refs[20 : 20 + n_old]
    gtok_ref = refs[20 + n_old]
    outs = refs[21 + n_old : -6]
    gsum, gq_ref, gproj_ref, gkvr_ref, gfr_ref, gvec_ref = refs[-6:]
    step = pl.program_id(0)
    rows, width = mid_ref.shape
    lane = lane_iota(rows)
    low = lane < LANES // 2
    col = col_ref[0]
    chunk = 256
    cols = cols_ref[0]
    slot_c = [slotcol_ref[0, :, i : i + 1] for i in range(2)]
    lane_c = lane_iota(rows, chunk)
    accs = (gq_ref, gproj_ref, gkvr_ref, gfr_ref, gvec_ref)

    @pl.when(step == 0)
    def _():
        for k, ref in enumerate(accs):
            ref[...] = old[k][...] if old else jnp.zeros_like(ref)

    gsum[...] = jnp.zeros_like(gsum)

    chunks = near_ref.shape[0] // chunk

    def gather(k, carry):
        for kind, ref in enumerate((near_ref, far_ref)):
            block = ref[pl.ds(pl.multiple_of(k * chunk, chunk), chunk), :]
            base = lane_c + (k + kind * chunks) * chunk
            pick = jnp.where((base == slot_c[0]) | (base == slot_c[1]), 1.0, 0.0).astype(BF16)
            gsum[...] += mm(pick, block)
        return carry

    lax.fori_loop(0, chunks, gather, 0)
    glog = jnp.zeros((rows, LANES), F32)
    for i in range(2):
        glog = jnp.where(lane == col[:, 4 + i : 5 + i], cols[:, 2 + i : 3 + i], glog)
    glog = glog.astype(BF16)
    n2 = n2_ref[...]
    gfr_ref[...] += mm_tn(glog, n2)
    gn2 = gsum[...] + mm_nt(glog, frw_ref[...])
    hat2, rstd2 = norm_parts(mid_ref[...])
    grad = grad_ref[0].astype(F32)
    halting = cols[:, 0:1]
    gend = halting * grad + cols[:, 1:2] * vec_ref[4:5, :]
    gmid = gend + norm_back(hat2, rstd2, vec_ref[2:3, :], gn2)
    ggain2 = fold_rows(gn2 * hat2)
    gbias2 = fold_rows(gn2)
    gattn = gmid.astype(BF16)
    gproj_ref[...] += mm_tn(gattn, mixed_ref[...])
    gmixed = mm_nt(gattn, proj_ref[...]).astype(BF16).astype(F32)
    pairs = gmixed.shape[1] // LANES
    tiles = [gmixed[:, j * LANES : (j + 1) * LANES] for j in range(pairs)]
    kv = kv_ref[...]
    scale = 0.125
    routes = [col[:, i : i + 1] for i in range(4)]
    gkv = jnp.zeros((LANES, rows), F32)
    ggates = []
    parts = []
    for i in range(4):
        gate = gates_ref[:, i : i + 1]
        sel = pltpu.roll(pick_head(tiles, routes[i], lane), LANES // 2, 1)
        sel = jnp.where(low, 0.0, sel)
        probs = probs_ref[0, i]
        heads = mm(probs, kv)
        ggates.append(jnp.sum(heads * sel, axis=-1, keepdims=True))
        gheads = (gate * sel).astype(BF16)
        gprobs = mm_nt(gheads, kv)
        probs_f = probs.astype(F32)
        inner = jnp.sum(heads * gheads.astype(F32), axis=-1, keepdims=True)
        gscores = (probs_f * (gprobs - inner)).astype(BF16)
        gkv = gkv + mm_tn(gheads, probs) + mm_tn(qs_ref[0, i], gscores) * scale
        gq = mm(gscores, kv) * scale
        parts.append(jnp.where(low, gq, pltpu.roll(gq, LANES // 2, 1)))
    gtiles = place_heads(parts, routes, pairs, lane)
    gquery = jnp.concatenate([t.astype(BF16) for t in gtiles], axis=1)
    normed = normed_ref[...]
    gq_ref[...] += mm_tn(normed, gquery)
    mean = ggates[0] * gates_ref[:, 0:1]
    for i in range(1, 4):
        mean = mean + ggates[i] * gates_ref[:, i : i + 1]
    alog = jnp.zeros((rows, LANES), F32)
    for i in range(4):
        alog = jnp.where(lane == routes[i], gates_ref[:, i : i + 1] * (ggates[i] - mean), alog)
    gkvr = jnp.concatenate([jnp.transpose(gkv).astype(BF16), alog.astype(BF16)], axis=1)
    gkvr_ref[...] += mm_tn(gkvr, normed)
    gnormed = mm_nt(gquery, qw_ref[...]) + mm_nt(gkvr, kvr_ref[...])
    hat, rstd = norm_parts(x_ref[0].astype(F32))
    gtok_ref[0] = grad * (1.0 - halting) + gmid + norm_back(hat, rstd, vec_ref[0:1, :], gnormed)
    sub8 = lax.broadcasted_iota(jnp.int32, (8, width), 0)
    gvec = jnp.where(sub8 == 0, fold_rows(gnormed * hat), 0.0)
    gvec = jnp.where(sub8 == 1, fold_rows(gnormed), gvec)
    gvec = jnp.where(sub8 == 2, ggain2, gvec)
    gvec_ref[...] += jnp.where(sub8 == 3, gbias2, gvec)

    @pl.when(step == pl.num_programs(0) - 1)
    def _():
        if not last:
            for ref, out in zip(accs, outs):
                out[...] = ref[...]
            return
        pack, gvec_out = outs
        gvec_out[...] = gvec_ref[...]
        blocks = gq_ref.shape[1] // width
        for j in range(blocks):
            pack[j * width : (j + 1) * width, :] = gq_ref[:, j * width : (j + 1) * width].astype(BF16)
        place = blocks * width
        for j in range(blocks):
            pack[place : place + width, :] = jnp.transpose(gproj_ref[:, j * width : (j + 1) * width]).astype(BF16)
            place = place + width
        for ref in (gkvr_ref, gfr_ref):
            pack[place : place + ref.shape[0], :] = ref[...].astype(BF16)
            place = place + ref.shape[0]
        pack[place:, :] = jnp.zeros((pack.shape[0] - place, width), BF16)


def attention_backward(micro, last, packed_rows, tokens, grad, col, vec, qw, kvr, proj, frw, saved, near, far, cols, old, moving, cid):
    mid, n2, normed, mixed, probs, qs, kv, gates, slotcol = saved
    _, count, width = tokens.shape
    steps = count // SEQ
    inner = qw.shape[1]
    whole = lambda a: pl.BlockSpec(a.shape, lambda r: (0,) * a.ndim)
    by_row = lambda c: pl.BlockSpec((SEQ, c), lambda r: (r, 0))
    part = pl.BlockSpec((1, SEQ, width), lambda r: (micro, r, 0))
    grown = [qw.shape] + [a.shape[::-1] for a in (proj, kvr, frw)]
    out_shape = [jax.ShapeDtypeStruct(tokens.shape, F32)]
    if last:
        out_shape += [jax.ShapeDtypeStruct((packed_rows, width), BF16)]
    else:
        out_shape += [jax.ShapeDtypeStruct(s, F32) for s in grown]
    out_shape += [jax.ShapeDtypeStruct((8, width), F32)]
    old_in = [old[k] for k in (1, 2, 3, 4, 5)] if old else []
    hbm = pl.BlockSpec(memory_space=pl.ANY)
    cols_spec = pl.BlockSpec((1, SEQ, 8), lambda r: (micro, r, 0))
    in_specs = [
        part, part, cols_spec,
        whole(vec), whole(qw), whole(kvr), whole(proj), whole(frw),
        by_row(width), by_row(width), by_row(width), by_row(inner),
        pl.BlockSpec((1, 4, SEQ, SEQ), lambda r: (r, 0, 0, 0)),
        pl.BlockSpec((1, 4, SEQ, LANES), lambda r: (r, 0, 0, 0)),
        by_row(LANES), by_row(8), cols_spec,
        whole(near), whole(far), cols_spec,
    ] + [whole(o) for o in old_in] + [hbm] * (1 if old else 0)
    args = (
        tokens, grad, col, vec, qw, kvr, proj, frw, mid, n2, normed, mixed, probs, qs, kv, gates, slotcol, near, far, cols,
        *old_in, *(old[:1] if old else []),
    )
    return run_kernel(
        functools.partial(attention_backward_kernel, last, len(old_in) + (1 if old else 0)), args, in_specs,
        out_shape, [part] + [pl.BlockSpec(o.shape, lambda r: (0, 0)) for o in out_shape[1:]],
        [
            pltpu.VMEM((SEQ, width), F32),
            *[pltpu.VMEM(s, F32) for s in grown],
            pltpu.VMEM((8, width), F32),
        ],
        (steps,), "attention_backward",
        pl.CostEstimate(
            flops=2 * count * width * (4 * inner + 512 + 2 * near.shape[0]), bytes_accessed=24 << 20, transcendentals=0
        ),
        moving, cid, {25: 0} if old else None,
    )


def total_plan(n_expert, n_hidden, rows):
    ny = nx = n_hidden // 2
    nz = n_expert // nx
    unit = 16 * ny * nx * nz
    units = -(-rows // (2 * unit))
    count = min(units, STREAMS)
    streams = tuple((units // count + (i < units % count)) * unit for i in range(count))
    return (nz, nx, ny), streams


def total_kernel(
    sizes, streams, pack_ref, small_ref, out_ref, sum_ref,
    buf, done, core_in, land, small_got, small_part, small_got2, sems, small_sems,
):
    nz, nx, ny = sizes
    e, h = lax.axis_index("expert"), lax.axis_index("hidden")
    n_expert, n_hidden = nz * nx, ny * 2
    z, x = lax.div(e, nx), lax.rem(e, nx)
    y, c = lax.div(h, 2), lax.rem(h, 2)
    half = sum(streams)
    width = pack_ref.shape[1]
    mesh_id = pl.DeviceIdType.MESH
    barrier = pltpu.get_barrier_semaphore()
    for k in range(1, n_expert):
        pl.semaphore_signal(barrier, inc=1, device_id=(lax.rem(e + k, n_expert), h), device_id_type=mesh_id)
    for k in range(1, n_hidden):
        pl.semaphore_signal(barrier, inc=1, device_id=(e, lax.rem(h + k, n_hidden)), device_id_type=mesh_id)
    pl.semaphore_wait(barrier, n_expert + n_hidden - 2)
    used = {}

    def copy(source, target, device, pool=sems):
        i = used.get(id(pool), 0)
        used[id(pool)] = i + 1
        return pltpu.make_async_remote_copy(
            source, target, pool.at[0, i], pool.at[1, i], device_id=device, device_id_type=mesh_id
        )

    def rows_at(ref, start, count):
        return ref.at[pl.ds(pl.multiple_of(start, 16), count)]

    def add_rows(start, count, base, pieces):
        step = 64 if count % 64 == 0 else 16

        def body(i, carry):
            place = pl.ds(pl.multiple_of(start + i * step, 16), step)
            total = base[place, :].astype(F32)
            for ref in pieces:
                total = total + ref[pl.ds(pl.multiple_of(i * step, 16), step), :].astype(F32)
            buf[place, :] = total.astype(BF16)
            return carry

        lax.fori_loop(0, count // step, body, 0)

    axes = {
        "c": (2, c, lambda p: (e, y * 2 + p)),
        "y": (ny, y, lambda p: (e, p * 2 + c)),
        "x": (nx, x, lambda p: (z * nx + p, h)),
        "z": (nz, z, lambda p: (p * nx + x, h)),
    }
    landed = [0]

    def travel(first, count, order, delay):
        for _ in range(delay):
            yield
        moves = [copy(rows_at(pack_ref, (1 - c) * half + first, count), rows_at(core_in, first, count), axes["c"][2](1 - c))]
        for m in moves:
            m.start()
        yield
        for m in moves:
            m.wait()
        start, span = c * half + first, count
        add_rows(start, span, pack_ref, [core_in.at[pl.ds(first, count)]])
        trail = []
        for name in order:
            size, me, device = axes[name]
            chunk = span // size
            moves, pieces = [], []
            for k in range(1, size):
                peer = lax.rem(me + k, size)
                pieces.append(land.at[pl.ds(landed[0], chunk)])
                landed[0] += chunk
                moves.append(copy(rows_at(buf, start + peer * chunk, chunk), pieces[-1], device(peer)))
            for m in moves:
                m.start()
            yield
            for m in moves:
                m.wait()
            start, span = start + me * chunk, chunk
            trail.append((start, chunk, size, me, device))
            add_rows(start, span, buf, pieces)
        here = pl.ds(pl.multiple_of(start, 16), span)
        done[here, :] = buf[here, :]
        for begin, chunk, size, me, device in reversed(trail):
            place = rows_at(done, begin, chunk)
            moves = [copy(place, place, device(lax.rem(me + k, size))) for k in range(1, size)]
            for m in moves:
                m.start()
            yield
            for m in moves:
                m.wait()
        place = rows_at(done, c * half + first, count)
        moves = [copy(place, place, axes["c"][2](1 - c))]
        for m in moves:
            m.start()
        yield
        for m in moves:
            m.wait()

    def travel_small():
        moves = [
            copy(small_ref, small_got.at[e], (lax.rem(e + k, n_expert), h), small_sems) for k in range(1, n_expert)
        ]
        for m in moves:
            m.start()
        small_got[e] = small_ref[...]
        yield
        yield
        for m in moves:
            m.wait()
        small_part[...] = jnp.sum(small_got[...], axis=0)
        moves = [
            copy(small_part, small_got2.at[h], (e, lax.rem(h + k, n_hidden)), small_sems) for k in range(1, n_hidden)
        ]
        for m in moves:
            m.start()
        small_got2[h] = small_part[...]
        yield
        yield
        for m in moves:
            m.wait()
        sum_ref[...] = jnp.sum(small_got2[...], axis=0)

    going, first = [], 0
    for i, count in enumerate(streams):
        going.append(travel(first, count, ("yxz", "xyz")[i % 2], 2 * (i >= len(streams) // 2)))
        first += count
    going.append(travel_small())
    while going:
        going = [g for g in going if next(g, StopIteration) is not StopIteration]
    step = 64 if half % 64 == 0 else 16

    def body(i, carry):
        here = pl.ds(pl.multiple_of(i * step, step), step)
        out_ref[here, :] = done[here, :]
        return carry

    lax.fori_loop(0, 2 * half // step, body, 0)


def total_step(n_expert, n_hidden, rows, pack, small):
    sizes, streams = total_plan(n_expert, n_hidden, rows)
    nz, nx, ny = sizes
    width = pack.shape[1]
    half = sum(streams)
    vmem = pl.BlockSpec(memory_space=pltpu.VMEM)
    landing = 0
    for i, span in enumerate(streams):
        for size in ((ny, nx, nz), (nx, ny, nz))[i % 2]:
            span = span // size
            landing += span * (size - 1)
    steps = len(streams) * (2 + 2 * ((ny - 1) + (nx - 1) + (nz - 1)))
    return pl.pallas_call(
        functools.partial(total_kernel, sizes, streams),
        out_shape=(jax.ShapeDtypeStruct(pack.shape, BF16), jax.ShapeDtypeStruct(small.shape, F32)),
        in_specs=[vmem] * 2,
        out_specs=[vmem] * 2,
        scratch_shapes=[
            pltpu.VMEM((2 * half, width), BF16),
            pltpu.VMEM((2 * half, width), BF16),
            pltpu.VMEM((half, width), BF16),
            pltpu.VMEM((landing, width), BF16),
            pltpu.VMEM((n_expert,) + small.shape, F32),
            pltpu.VMEM(small.shape, F32),
            pltpu.VMEM((n_hidden,) + small.shape, F32),
            pltpu.SemaphoreType.DMA((2, steps)),
            pltpu.SemaphoreType.DMA((2, n_expert + n_hidden)),
        ],
        compiler_params=pltpu.CompilerParams(collective_id=8, has_side_effects=True, vmem_limit_bytes=VMEM_LIMIT),
        name="total_step",
    )(pack, small)


def unpack_kernel(
    pack_ref, near_a, near_b, far_a, far_b,
    gq_ref, gproj_ref, first_ref, second_ref, key_ref, value_ref, router_ref, ffn_ref,
):
    step = pl.program_id(0)
    width = pack_ref.shape[2]
    blocks = gproj_ref.shape[0]
    for j in range(blocks):
        gq_ref[:, j * width : (j + 1) * width] = pack_ref[j].astype(F32)
        gproj_ref[j] = pack_ref[blocks + j].astype(F32)
    first_ref[...] = near_a[...].astype(F32) + far_a[...].astype(F32)
    second_ref[...] = near_b[...].astype(F32) + far_b[...].astype(F32)
    head = key_ref.shape[0]

    @pl.when(step == 0)
    def _():
        key_ref[...] = pack_ref[2 * blocks, :head, :].astype(F32)
        value_ref[...] = pack_ref[2 * blocks, head : 2 * head, :].astype(F32)

    @pl.when(step == 1)
    def _():
        router_ref[...] = pack_ref[2 * blocks, : router_ref.shape[0], :].astype(F32)

    @pl.when(step == 2)
    def _():
        ffn_ref[...] = pack_ref[2 * blocks, : ffn_ref.shape[0], :].astype(F32)


def unpack_step(pack, near, far, head, routes, experts):
    steps = 4
    slabs, width, _ = pack.shape
    blocks = slabs // 2
    rows = width // steps
    out_shape = [
        jax.ShapeDtypeStruct((width, blocks * width), F32),
        jax.ShapeDtypeStruct((blocks, width, width), F32),
        *[jax.ShapeDtypeStruct(a.shape, F32) for a in near],
        *[jax.ShapeDtypeStruct((n, width), F32) for n in (head, head, routes, experts)],
    ]
    cut = lambda a: pl.BlockSpec((a.shape[0], a.shape[1] // steps, a.shape[2]), lambda i: (0, i, 0))
    return run_kernel(
        unpack_kernel, (pack, *near, *far), [cut(pack)] + [cut(a) for a in near] * 2, out_shape,
        [pl.BlockSpec((rows, blocks * width), lambda i: (i, 0)), cut(out_shape[1])] + [cut(a) for a in near]
        + [pl.BlockSpec(o.shape, lambda i: (0, 0)) for o in out_shape[4:]],
        (), (steps,), "unpack_step", pl.CostEstimate(flops=0, bytes_accessed=20 << 20, transcendentals=0),
    )


def pad_lanes(a):
    return jnp.pad(a, ((0, 0), (0, LANES - a.shape[1])))


def per_device(
    tokens, grad_out, attn_routes, ffn_routes, segments, pad_mask, norm1_gain, norm1_bias, attn_router,
    query_w, key_w, value_w, attn_proj, norm2_gain, norm2_bias, ffn_router, expert_in, expert_out, halt_w, halt_b,
    *, n_expert, n_hidden,
):
    micros, count, width = tokens.shape
    experts = ffn_router.shape[1]
    capacity = 4 * count // experts
    slots = experts * capacity
    per = experts // n_expert
    group = n_expert // 2
    across = [(i, (i + group) % n_expert) for i in range(n_expert)]

    def gathered(a):
        return lax.all_gather(a, "hidden", axis=0, tiled=False)

    crossed = [lax.ppermute(a, "expert", across) for a in (expert_in, expert_out)]
    near_first, near_second = gathered(expert_in), gathered(expert_out)
    seg = segments.reshape(micros, count)
    zeros = jnp.zeros_like(seg)
    mine = lax.axis_index("expert") // group
    kind = (ffn_routes // (experts // 2) != mine).astype(jnp.int32)
    base = (kind * (experts // 2) + ffn_routes % (experts // 2)) * capacity
    col = jnp.concatenate([attn_routes, ffn_routes, seg[:, :, None], pad_mask[:, :, None]], axis=2)
    row = jnp.stack(
        [seg, pad_mask, ffn_routes[:, :, 0], ffn_routes[:, :, 1], base[:, :, 0], base[:, :, 1], zeros, zeros], axis=1
    )
    none = jnp.zeros_like(halt_w)
    vec = jnp.stack([norm1_gain, norm1_bias, norm2_gain, norm2_bias, halt_w, none, none, none])
    kvr = jnp.concatenate([key_w, value_w, pad_lanes(attn_router)], axis=1)
    frw = pad_lanes(ffn_router)
    hb = jnp.broadcast_to(halt_b.reshape(1, 1), (8, LANES))
    shape = (2, group, per, capacity, width)
    packed = query_w.size // width + attn_proj.shape[0] + width
    packed_rows = 2 * sum(total_plan(n_expert, n_hidden, packed)[1])

    slotrow, slotcol = route_step(row)
    weights = (vec, hb, query_w, kvr, attn_proj, frw)
    f0 = attention_forward(0, tokens, grad_out, col, row, slotrow, *weights, slots, (), None)
    crossed[0], n0_out = lax.optimization_barrier((crossed[0], f0[9]))
    far_first = gathered(crossed[0])
    *f1, n0 = attention_forward(1, tokens, grad_out, col, row, slotrow, *weights, slots, [n0_out.reshape(shape)], 2)
    crossed[1], n1_out = lax.optimization_barrier((crossed[1], f1[9]))
    far_second = gathered(crossed[1])
    gs0, gs1, n1 = spread_step(slotrow, grad_out, slots, [n1_out.reshape(shape)], 3)
    rows = (n0, n1)
    y0, y1, g1 = expert_forward(0, rows, near_first, near_second, [gs1.reshape(shape)], 4)
    far0, far1, g0 = expert_forward(1, rows, far_first, far_second, [gs0.reshape(shape)], 1)
    grads = (g0, g1)
    scal = reading_step((y0, y1, far0, far1), grads, vec)
    cols, ab = scalar_step(scal, (f0[8], f1[8]), slotrow)
    gf_far, gs_far, bf0, bf1, r0, rf0, r1 = expert_backward(
        1, rows, grads, ab, vec, far_first, far_second, [y0, far0, y1], 9
    )
    gf_near, gs_near, bn0, bn1, qf0, qf1, rf1 = expert_backward(
        0, rows, grads, ab, vec, near_first, near_second, [bf0, bf1, far1], 10
    )

    flat = lambda a: a.reshape(slots // 2, width)

    def reduced(a):
        return lax.psum_scatter(a, "hidden", scatter_dimension=0, tiled=False)

    far_grads = [reduced(a) for a in (gf_far, gs_far)]
    near_grads = [reduced(a) for a in (gf_near, gs_near)]
    *res0, qn0, qn1 = result_step(0, tokens, f0[0], flat(r0), flat(rf0), cols, slotcol, (), [bn0, bn1], 11)
    common = (tokens, grad_out, col, vec, query_w, kvr, attn_proj, frw)
    far_grads[0], qn0 = lax.optimization_barrier((far_grads[0], qn0))
    far_grads[0] = lax.ppermute(far_grads[0], "expert", across)
    out = attention_backward(
        0, False, packed_rows, *common, list(f0[:8]) + [slotcol], flat(qn0), flat(qf0), cols, (), (), None
    )
    res1 = result_step(1, tokens, f1[0], flat(r1), flat(rf1), cols, slotcol, tuple(res0[:1]), (), None)
    out, far_grads, res1 = lax.optimization_barrier((tuple(out), far_grads, tuple(res1)))
    far_grads[1] = lax.ppermute(far_grads[1], "expert", across)
    out = attention_backward(
        1, True, packed_rows, *common, list(f1[:8]) + [slotcol], flat(qn1), flat(qf1), cols, tuple(out), (), None
    )
    packs = out[1]
    small = jnp.concatenate([out[2], res0[1] + res1[1]], axis=0)
    total, small = total_step(n_expert, n_hidden, packed, packs, small)
    near_grads = [a.reshape(a.shape[-3:]) for a in near_grads]
    far_grads = [a.reshape(a.shape[-3:]) for a in far_grads]
    gq, gproj, gfirst, gsecond, gkey, gvalue, grouter, gfr = unpack_step(
        total[:packed].reshape(-1, width, width), near_grads, far_grads, key_w.shape[1], attn_router.shape[1], experts
    )
    return (
        res1[0],
        out[0],
        small[0],
        small[1],
        grouter.T,
        gq,
        gkey.T,
        gvalue.T,
        gproj.reshape(attn_proj.shape),
        small[2],
        small[3],
        gfr.T,
        gfirst,
        gsecond,
        small[8],
        small[9, :1],
    )


def solution(mesh):
    rows = P(None, ("expert", "hidden"), None)
    in_specs = (rows,) * 5 + (P(None, ("expert", "hidden")),) + (P(),) * 10 + (
        P("expert", None, "hidden"), P("expert", "hidden", None), P(), P(),
    )
    out_specs = (rows,) * 2 + (P(),) * 10 + (P("expert", None, "hidden"), P("expert", "hidden", None), P(), P())
    return jax.shard_map(
        functools.partial(per_device, n_expert=mesh.shape["expert"], n_hidden=mesh.shape["hidden"]),
        mesh=mesh, in_specs=in_specs, out_specs=out_specs, check_vma=False,
    )
```

```python
import functools
import math

import jax
import jax.numpy as jnp
from jax import lax
from jax.experimental import pallas as pl
from jax.experimental.pallas import tpu as pltpu
from jax.sharding import PartitionSpec as P

SEQ = 256
LANES = 128
F32 = jnp.float32
BF16 = jnp.bfloat16
GELU_C = math.sqrt(2.0 / math.pi)
GELU_A = 0.044715
VMEM_LIMIT = 60 * 1024 * 1024
STREAMS = 7


def mm(left, right):
    return jnp.dot(left, right, preferred_element_type=F32)


def mm_nt(left, right):
    return lax.dot_general(left, right, (((1,), (1,)), ((), ())), preferred_element_type=F32)


def mm_tn(left, right):
    return lax.dot_general(left, right, (((0,), (0,)), ((), ())), preferred_element_type=F32)


def lane_iota(rows, lanes=LANES):
    return lax.broadcasted_iota(jnp.int32, (rows, lanes), 1)


def norm_parts(value):
    center = value - jnp.mean(value, axis=-1, keepdims=True)
    rstd = lax.rsqrt(jnp.mean(center * center, axis=-1, keepdims=True) + 1e-05)
    return center * rstd, rstd


def norm_back(hat, rstd, gain, grad):
    scaled = grad * gain
    first = jnp.mean(scaled, axis=-1, keepdims=True)
    second = jnp.mean(scaled * hat, axis=-1, keepdims=True)
    return rstd * (scaled - first - hat * second)


def fold_rows(value):
    return jnp.sum(value, axis=0, keepdims=True)


def pick_head(tiles, route, lane):
    route = jnp.broadcast_to(route, lane.shape)
    pair = lax.shift_right_logical(route, 1)
    out = tiles[0]
    for j in range(1, len(tiles)):
        out = jnp.where(pair == j, tiles[j], out)
    odd = (route & 1) == 1
    return jnp.where(odd, pltpu.roll(out, LANES // 2, 1), out)


def place_heads(parts, routes, count, lane):
    half = lax.shift_right_logical(lane, 6)
    routes = [jnp.broadcast_to(r, lane.shape) for r in routes]
    kept = [jnp.where(half == (r & 1), p, 0.0) for p, r in zip(parts, routes)]
    pairs = [lax.shift_right_logical(r, 1) for r in routes]
    tiles = []
    for j in range(count):
        total = jnp.where(pairs[0] == j, kept[0], 0.0)
        for k, p in zip(kept[1:], pairs[1:]):
            total = total + jnp.where(p == j, k, 0.0)
        tiles.append(total)
    return tiles


def softmax_cols(cols):
    top = functools.reduce(jnp.maximum, cols)
    expo = [jnp.exp(c - top) for c in cols]
    total = functools.reduce(jnp.add, expo)
    return [e / total for e in expo]


def put_cols(cols, rows, width):
    lane = lane_iota(rows, width)
    out = jnp.zeros((rows, width), cols[0].dtype)
    for i, c in enumerate(cols):
        out = jnp.where(lane == i, c, out)
    return out


def split_three(value):
    high = value.astype(BF16)
    rest = value - high.astype(F32)
    middle = rest.astype(BF16)
    last = (rest - middle.astype(F32)).astype(BF16)
    return jnp.concatenate([high.astype(F32), middle.astype(F32), last.astype(F32)], axis=0).astype(BF16)


def join_three(value):
    n = value.shape[0] // 3
    return value[:n] + value[n : 2 * n] + value[2 * n :]


def row_to_col(row):
    n = row.shape[1]
    place = lax.broadcasted_iota(jnp.int32, (n, n), 0)
    other = lax.broadcasted_iota(jnp.int32, (n, n), 1)
    return jnp.sum(jnp.where(place == other, row, 0.0), axis=-1, keepdims=True)


def dispatch(slot_rows, values, out_ref):
    chunk = 256
    tokens = values[0].shape[0]
    spot = lax.broadcasted_iota(jnp.int32, (chunk, tokens), 0)

    def body(k, carry):
        base = spot + k * chunk
        if len(values) == 1:
            pick = jnp.where((base == slot_rows[0]) | (base == slot_rows[1]), 1.0, 0.0).astype(BF16)
            out = mm(pick, values[0][...])
        else:
            out = mm(jnp.where(base == slot_rows[0], 1.0, 0.0).astype(BF16), values[0][...])
            out = out + mm(jnp.where(base == slot_rows[1], 1.0, 0.0).astype(BF16), values[1][...])
        out_ref[pl.ds(pl.multiple_of(k * chunk, chunk), chunk), :] = out.astype(BF16)
        return carry

    lax.fori_loop(0, out_ref.shape[0] // chunk, body, 0)


def group_of():
    size = lax.axis_size("expert") // 2
    e = lax.axis_index("expert")
    me = lax.rem(e, size)
    return me, size, e - me


def other_core():
    e, h = lax.axis_index("expert"), lax.axis_index("hidden")
    return e, h + 1 - 2 * lax.rem(h, 2)


def group_greet(mate=False):
    me, size, base = group_of()
    other = lax.axis_index("hidden")
    barrier = pltpu.get_barrier_semaphore()
    for k in range(1, size):
        pl.semaphore_signal(
            barrier, inc=1, device_id=(base + lax.rem(me + k, size), other), device_id_type=pl.DeviceIdType.MESH
        )
    if mate:
        pl.semaphore_signal(barrier, inc=1, device_id=other_core(), device_id_type=pl.DeviceIdType.MESH)
    pl.semaphore_wait(barrier, size if mate else size - 1)


def group_copies(source, target, send_sem, recv_sem):
    me, size, base = group_of()
    other = lax.axis_index("hidden")
    moves = []
    for k in range(1, size):
        peer = lax.rem(me + k, size)
        moves.append(
            pltpu.make_async_remote_copy(
                source.at[peer], target.at[me], send_sem.at[k - 1], recv_sem.at[k - 1],
                device_id=(base + peer, other), device_id_type=pl.DeviceIdType.MESH,
            )
        )
    return moves


def at_step(which):
    found = True
    for axis, size in enumerate(which[1]):
        here = pl.program_id(axis) == (0 if which[0] == 0 else size - 1)
        found = here if found is True else found & here
    return found


def run_kernel(kernel, args, in_specs, out_shape, out_specs, scratch, grid, name, cost, moving=(), cid=None, aliases=None, mate=False):
    n_in, n_out, n_move = len(args), len(out_shape), len(moving)
    peers = lax.axis_size("expert") // 2 - 1
    hbm = pl.BlockSpec(memory_space=pl.ANY)

    def body(*refs):
        ins, sources = refs[:n_in], refs[n_in : n_in + n_move]
        outs = refs[n_in + n_move : n_in + n_move + n_out]
        targets = refs[n_in + n_move + n_out : n_in + 2 * n_move + n_out]
        rest = refs[n_in + 2 * n_move + n_out :]
        sems = rest[len(scratch) :]
        moves, owns = [], []
        me = group_of()[0]
        pairs = []
        for a, b in zip(sources, targets):
            pairs += [(a, b)] if len(a.shape) == 4 else [(a.at[i], b.at[i]) for i in range(a.shape[0])]
        for i, (a, b) in enumerate(pairs):
            moves += group_copies(a, b, sems[3 * i], sems[3 * i + 1])
            owns.append(pltpu.make_async_copy(a.at[me], b.at[me], sems[3 * i + 2]))

        if moving:

            @pl.when(at_step((0, grid)))
            def _():
                group_greet(mate)
                for c in moves + owns:
                    c.start()

        kernel(*ins, *outs, *rest[: len(scratch)])

        if moving:

            @pl.when(at_step((1, grid)))
            def _():
                for c in moves + owns:
                    c.wait()

    sems = []
    for _ in range(sum(1 if a.ndim == 4 else a.shape[0] for a in moving)):
        sems += [pltpu.SemaphoreType.DMA((peers,)), pltpu.SemaphoreType.DMA((peers,)), pltpu.SemaphoreType.DMA]
    more = dict(collective_id=cid, has_side_effects=True) if moving else {}
    return pl.pallas_call(
        body,
        grid=grid,
        out_shape=tuple(out_shape) + tuple(jax.ShapeDtypeStruct(a.shape, a.dtype) for a in moving),
        in_specs=list(in_specs) + [hbm] * n_move,
        out_specs=list(out_specs) + [hbm] * n_move,
        scratch_shapes=list(scratch) + sems,
        input_output_aliases=aliases or {},
        compiler_params=pltpu.CompilerParams(vmem_limit_bytes=VMEM_LIMIT, **more),
        cost_estimate=cost,
        name=name,
    )(*args, *moving)


def route_kernel(row_ref, slotrow_ref, slotcol_ref):
    tokens = row_ref.shape[2]
    before = lax.broadcasted_iota(jnp.int32, (tokens, tokens), 0)
    after = lax.broadcasted_iota(jnp.int32, (tokens, tokens), 1)
    upper = jnp.where(before < after, 1.0, 0.0).astype(BF16)
    sub = lax.broadcasted_iota(jnp.int32, (LANES, tokens), 0)
    sub8 = lax.broadcasted_iota(jnp.int32, (8, tokens), 0)
    for m in range(row_ref.shape[0]):
        row = row_ref[m]
        named = [jnp.where(sub == row[2 + i : 3 + i, :], 1.0, 0.0) for i in range(2)]
        rank = mm((named[0] + named[1]).astype(BF16), upper)
        slots = [fold_rows(named[i] * rank).astype(jnp.int32) + row[4 + i : 5 + i, :] for i in range(2)]
        slotrow_ref[m] = jnp.where(sub8 == 0, slots[0], slots[1])
        table = jnp.where(sub == 0, slots[0].astype(F32), slots[1].astype(F32))
        slotcol_ref[m] = jnp.transpose(table)[:, :8].astype(jnp.int32)


def route_step(row):
    micros, _, count = row.shape
    out_shape = (
        jax.ShapeDtypeStruct((micros, 8, count), jnp.int32),
        jax.ShapeDtypeStruct((micros, count, 8), jnp.int32),
    )
    whole = lambda s: pl.BlockSpec(s, lambda i: (0,) * len(s))
    return run_kernel(
        route_kernel, (row,), [whole(row.shape)], out_shape, [whole(o.shape) for o in out_shape], (), (1,), "route_step",
        pl.CostEstimate(flops=10**8, bytes_accessed=1 << 20, transcendentals=0),
    )


def spread_kernel(slotrow_ref, grad_ref, out0_ref, out1_ref):
    for m, out_ref in enumerate((out0_ref, out1_ref)):
        dispatch([slotrow_ref[m, 0:1, :], slotrow_ref[m, 1:2, :]], [grad_ref.at[m]], out_ref)


def spread_step(slotrow, grad, slots, moving, cid):
    width = grad.shape[2]
    whole = lambda s: pl.BlockSpec(s, lambda i: (0,) * len(s))
    return run_kernel(
        spread_kernel, (slotrow, grad), [whole(slotrow.shape), whole(grad.shape)],
        [jax.ShapeDtypeStruct((slots, width), BF16)] * 2, [whole((slots, width))] * 2, (), (1,), "spread_step",
        pl.CostEstimate(flops=8 * slots * width * grad.shape[1], bytes_accessed=6 << 20, transcendentals=0), moving, cid,
    )


def attention_forward_kernel(
    x_ref, grad_ref, col_ref, row_ref, slotrow_ref, vec_ref, hb_ref, qw_ref, kvr_ref, proj_ref, frw_ref,
    mid_ref, n2_ref, normed_ref, mixed_ref, probs_ref, qs_ref, kv_ref, gates_ref, scal_ref, out_ref,
    n2_all,
):
    step = pl.program_id(0)
    rows = x_ref.shape[1]
    top_attn = 4
    lane = lane_iota(rows)
    x = x_ref[0].astype(F32)
    col = col_ref[0]
    row = row_ref[0]
    hat, _ = norm_parts(x)
    normed = (hat * vec_ref[0:1, :] + vec_ref[1:2, :]).astype(BF16)
    normed_ref[...] = normed
    kvr = mm(normed, kvr_ref[...])
    kv = kvr[:, :LANES].astype(BF16)
    kv_ref[...] = kv
    logits = kvr[:, LANES:]
    routes = [col[:, i : i + 1] for i in range(top_attn)]
    picked = [
        jnp.sum(jnp.where(lane == r, logits, 0.0), axis=-1, keepdims=True) for r in routes
    ]
    gates = softmax_cols(picked)
    query = mm(normed, qw_ref[...])
    heads_pairs = query.shape[1] // LANES
    tiles = [query[:, j * LANES : (j + 1) * LANES] for j in range(heads_pairs)]
    low = lane < LANES // 2
    same = col[:, 6:7] == row[0:1, :]
    place = lax.broadcasted_iota(jnp.int32, (rows, rows), 0)
    other = lax.broadcasted_iota(jnp.int32, (rows, rows), 1)
    allowed = same & ((row[1:2, :] == 1) | (place == other))
    scale = 0.125
    shares = []
    for i in range(top_attn):
        sel = jnp.where(low, pick_head(tiles, routes[i], lane), 0.0).astype(BF16)
        qs_ref[0, i] = sel
        scores = mm_nt(sel, kv) * scale
        scores = jnp.where(allowed, scores, -1e30)
        expo = jnp.exp(scores - jnp.max(scores, axis=-1, keepdims=True))
        probs = (expo * (1.0 / jnp.sum(expo, axis=-1, keepdims=True))).astype(BF16)
        probs_ref[0, i] = probs
        heads = mm(probs, kv) * gates[i]
        shares.append(jnp.where(low, pltpu.roll(heads, LANES // 2, 1), heads))
    mixed_tiles = place_heads(shares, routes, heads_pairs, lane)
    mixed = jnp.concatenate([t.astype(BF16) for t in mixed_tiles], axis=1)
    mixed_ref[...] = mixed
    mid = x + mm(mixed, proj_ref[...])
    mid_ref[...] = mid
    hat2, _ = norm_parts(mid)
    n2 = (hat2 * vec_ref[2:3, :] + vec_ref[3:4, :]).astype(BF16)
    n2_ref[...] = n2
    n2_all[pl.ds(pl.multiple_of(step * rows, rows), rows), :] = n2
    logits_ffn = mm(n2, frw_ref[...])
    gates_ffn = softmax_cols(
        [
            jnp.sum(jnp.where(lane == col[:, 4 + i : 5 + i], logits_ffn, 0.0), axis=-1, keepdims=True)
            for i in range(2)
        ]
    )
    gates_ref[...] = put_cols(gates, rows, gates_ref.shape[1])
    stop = jnp.sum(mid * vec_ref[4:5, :], axis=-1, keepdims=True) + hb_ref[0:1, 0:1]
    pull = jnp.sum(grad_ref[0].astype(F32) * (mid - x), axis=-1, keepdims=True)
    scal_ref[...] = jnp.transpose(put_cols([stop, pull] + gates_ffn, rows, LANES))[:8, :]

    @pl.when(step == pl.num_programs(0) - 1)
    def _():
        dispatch([slotrow_ref[0, 0:1, :], slotrow_ref[0, 1:2, :]], [n2_all], out_ref)


def attention_forward(micro, tokens, grad, col, row, slotrow, vec, hb, qw, kvr, proj, frw, slots, moving, cid):
    _, count, width = tokens.shape
    steps = count // SEQ
    inner = qw.shape[1]
    whole = lambda a: pl.BlockSpec(a.shape, lambda r: (0,) * a.ndim)
    out_shape = (
        jax.ShapeDtypeStruct((count, width), F32),
        jax.ShapeDtypeStruct((count, width), BF16),
        jax.ShapeDtypeStruct((count, width), BF16),
        jax.ShapeDtypeStruct((count, inner), BF16),
        jax.ShapeDtypeStruct((steps, 4, SEQ, SEQ), BF16),
        jax.ShapeDtypeStruct((steps, 4, SEQ, LANES), BF16),
        jax.ShapeDtypeStruct((count, LANES), BF16),
        jax.ShapeDtypeStruct((count, 8), F32),
        jax.ShapeDtypeStruct((8, count), F32),
        jax.ShapeDtypeStruct((slots, width), BF16),
    )
    by_row = lambda c: pl.BlockSpec((SEQ, c), lambda r: (r, 0))
    in_specs = [
        pl.BlockSpec((1, SEQ, width), lambda r: (micro, r, 0)),
        pl.BlockSpec((1, SEQ, width), lambda r: (micro, r, 0)),
        pl.BlockSpec((1, SEQ, 8), lambda r: (micro, r, 0)),
        pl.BlockSpec((1, 8, SEQ), lambda r: (micro, 0, r)),
        pl.BlockSpec((1, 8, count), lambda r: (micro, 0, 0)),
        whole(vec), whole(hb), whole(qw), whole(kvr), whole(proj), whole(frw),
    ]
    out_specs = [
        by_row(width), by_row(width), by_row(width), by_row(inner),
        pl.BlockSpec((1, 4, SEQ, SEQ), lambda r: (r, 0, 0, 0)),
        pl.BlockSpec((1, 4, SEQ, LANES), lambda r: (r, 0, 0, 0)),
        by_row(LANES), by_row(8),
        pl.BlockSpec((8, SEQ), lambda r: (0, r)),
        pl.BlockSpec((slots, width), lambda r: (0, 0)),
    ]
    return run_kernel(
        attention_forward_kernel, (tokens, grad, col, row, slotrow, vec, hb, qw, kvr, proj, frw), in_specs,
        out_shape, out_specs, [pltpu.VMEM((count, width), BF16)], (steps,), "attention_forward",
        pl.CostEstimate(
            flops=2 * count * width * (2 * inner + 256 + slots), bytes_accessed=12 << 20, transcendentals=count * 4 * SEQ
        ),
        moving, cid,
    )


def gelu_parts(pre):
    square = pre * pre
    inner = jnp.tanh(GELU_C * pre * (1.0 + GELU_A * square))
    return square, inner


def expert_forward_kernel(rows0_ref, rows1_ref, first_ref, second_ref, out0_ref, out1_ref, total):
    part = pl.program_id(1)
    _, src, _, cap, width = rows0_ref.shape
    half = src * cap
    rows = jnp.concatenate([r[...].reshape(half, width) for r in (rows0_ref, rows1_ref)], axis=0)
    pre = mm(rows, first_ref[0, 0])
    _, inner = gelu_parts(pre)
    act = (0.5 * pre * (1.0 + inner)).astype(BF16)
    res = mm(act, second_ref[0, 0])

    @pl.when(part == 0)
    def _():
        total[...] = res

    @pl.when(part > 0)
    def _():
        total[...] += res

    @pl.when(part == pl.num_programs(1) - 1)
    def _():
        out0_ref[...] = total[:half, :].astype(BF16).reshape(out0_ref.shape)
        out1_ref[...] = total[half:, :].astype(BF16).reshape(out1_ref.shape)


def expert_forward(kind, rows, first, second, moving, cid):
    _, src, local, cap, width = rows[0].shape
    parts, _, _, hid = first.shape
    spec_in = pl.BlockSpec((1, src, 1, cap, width), lambda e, h: (kind, 0, e, 0, 0))
    spec_rows = pl.BlockSpec((src, 1, cap, width), lambda e, h: (0, e, 0, 0))
    work = 2 * src * local * cap * width * hid * parts
    return run_kernel(
        expert_forward_kernel, (*rows, first, second),
        [
            spec_in, spec_in,
            pl.BlockSpec((1, 1, width, hid), lambda e, h: (h, e, 0, 0)),
            pl.BlockSpec((1, 1, hid, width), lambda e, h: (h, e, 0, 0)),
        ],
        [jax.ShapeDtypeStruct(r.shape[1:], BF16) for r in rows], [spec_rows] * 2,
        [pltpu.VMEM((2 * src * cap, width), F32)], (local, parts), "expert_forward",
        pl.CostEstimate(flops=4 * work, bytes_accessed=24 << 20, transcendentals=work // width), moving, cid,
    )


def reading_kernel(*refs):
    outs, grads = refs[:4], refs[4:8]
    vec_ref, scal_ref = refs[8:]
    src, _, cap, width = outs[0].shape
    halt = split_three(jnp.broadcast_to(vec_ref[4:5, :], (8, width)))
    ones = jnp.ones((8, width), BF16)
    sub8 = lax.broadcasted_iota(jnp.int32, (8, cap), 0)
    for kind in range(2):
        for m in range(2):
            for s in range(src):
                low = outs[2 * kind + m][s, 0]
                stop = join_three(mm_nt(halt, low))
                prod = low.astype(F32) * grads[2 * kind + m][0, s, 0].astype(F32)
                high = prod.astype(BF16)
                rest = (prod - high.astype(F32)).astype(BF16)
                pull = mm_nt(ones, high) + mm_nt(ones, rest)
                scal_ref[s, m, kind, 0] = jnp.where(sub8 == 0, stop, pull)


def reading_step(outs, grads, vec):
    src, local, cap, width = outs[0].shape
    spec_rows = pl.BlockSpec((src, 1, cap, width), lambda e: (0, e, 0, 0))
    spec_grad = lambda kind: pl.BlockSpec((1, src, 1, cap, width), lambda e: (kind, 0, e, 0, 0))
    return run_kernel(
        reading_kernel, (*outs, *grads, *grads, vec),
        [spec_rows] * 4 + [spec_grad(0)] * 2 + [spec_grad(1)] * 2 + [pl.BlockSpec(vec.shape, lambda e: (0, 0))],
        [jax.ShapeDtypeStruct((src, 2, 2, local, 8, cap), F32)],
        [pl.BlockSpec((src, 2, 2, 1, 8, cap), lambda e: (0, 0, 0, e, 0, 0))], (), (local,), "reading_step",
        pl.CostEstimate(flops=10**9, bytes_accessed=8 << 20, transcendentals=0),
    )[0].reshape(src, 2, 2 * local, 8, cap)


def add_cores(grown, gfirst_ref, gsecond_ref, keep, away, land, send_sem, recv_sem):
    step = pl.program_id(0) * pl.num_programs(1) + pl.program_id(1)
    steps = pl.num_programs(0) * pl.num_programs(1)
    pair = lax.div(step, 2)
    owned = lax.rem(step, 2) == lax.rem(lax.axis_index("hidden"), 2)

    def crossing(k):
        return [
            pltpu.make_async_remote_copy(
                away[i].at[k], land[i].at[k], send_sem.at[i, k], recv_sem.at[i, k],
                device_id=other_core(), device_id_type=pl.DeviceIdType.MESH,
            )
            for i in range(2)
        ]

    @pl.when(owned)
    def _():
        for i in range(2):
            keep[i][pair] = grown[i]

    @pl.when(jnp.logical_not(owned))
    def _():
        for i in range(2):
            away[i][pair] = grown[i]
        for c in crossing(pair):
            c.start()

    def finish(k):
        for c in crossing(k):
            c.wait()
        local, y = lax.div(k, gfirst_ref.shape[0]), lax.rem(k, gfirst_ref.shape[0])
        for ref, mine, got in ((gfirst_ref, keep[0], land[0]), (gsecond_ref, keep[1], land[1])):
            ref[y, local] = (mine[k].astype(F32) + got[k].astype(F32)).astype(BF16)

    @pl.when((lax.rem(step, 2) == 0) & (step >= 2))
    def _():
        finish(pair - 1)

    @pl.when(step == steps - 1)
    def _():
        finish(pair)


def expert_backward_kernel(
    fold, rows0_ref, rows1_ref, grad0_ref, grad1_ref, ab_ref, vec_ref, first_ref, second_ref,
    gfirst_ref, gsecond_ref, out0_ref, out1_ref, total, gin_all, *crossed,
):
    part = pl.program_id(1)
    _, src, _, cap, width = rows0_ref.shape
    half = src * cap

    @pl.when(part == 0)
    def _():
        for m, grad_ref in enumerate((grad0_ref, grad1_ref)):
            for s in range(src):
                ab = ab_ref[s, m, 0]
                scaled = row_to_col(ab[0:1, :]) * grad_ref[0, s, 0].astype(F32) + row_to_col(ab[1:2, :]) * vec_ref[4:5, :]
                gin_all[m * half + s * cap : m * half + (s + 1) * cap, :] = scaled.astype(BF16)

    rows = jnp.concatenate([r[...].reshape(half, width) for r in (rows0_ref, rows1_ref)], axis=0)
    gin = gin_all[...]
    first = first_ref[0, 0]
    second = second_ref[0, 0]
    pre = mm(rows, first)
    gact = mm_nt(gin, second)
    square, inner = gelu_parts(pre)
    part_one = 0.5 * (1.0 + inner)
    act = (pre * part_one).astype(BF16)
    slope = part_one + 0.5 * pre * (1.0 - inner * inner) * (GELU_C + (3.0 * GELU_C * GELU_A) * square)
    gpre = (gact * slope).astype(BF16)
    grown = (mm_tn(rows, gpre).astype(BF16), mm_tn(act, gin).astype(BF16))
    if fold:
        add_cores(grown, gfirst_ref, gsecond_ref, *crossed)
    else:
        gfirst_ref[0, 0], gsecond_ref[0, 0] = grown
    res = mm_nt(gpre, first)

    @pl.when(part == 0)
    def _():
        total[...] = res

    @pl.when(part > 0)
    def _():
        total[...] += res

    @pl.when(part == pl.num_programs(1) - 1)
    def _():
        out0_ref[...] = total[:half, :].astype(BF16).reshape(out0_ref.shape)
        out1_ref[...] = total[half:, :].astype(BF16).reshape(out1_ref.shape)


def expert_backward(kind, rows, grads, ab, vec, first, second, moving, cid):
    _, src, local, cap, width = rows[0].shape
    parts, _, _, hid = first.shape
    spec_in = pl.BlockSpec((1, src, 1, cap, width), lambda e, h: (kind, 0, e, 0, 0))
    spec_rows = pl.BlockSpec((src, 1, cap, width), lambda e, h: (0, e, 0, 0))
    spec_first = pl.BlockSpec((1, 1, width, hid), lambda e, h: (h, e, 0, 0))
    spec_second = pl.BlockSpec((1, 1, hid, width), lambda e, h: (h, e, 0, 0))
    work = 2 * src * local * cap * width * hid * parts
    fold = kind == 0
    grown = [((parts // 2,) + a.shape[1:] if fold else a.shape) for a in (first, second)]
    pairs = local * parts // 2
    kept = [pltpu.VMEM((pairs,) + a.shape[2:], BF16) for a in (first, second)]
    return run_kernel(
        functools.partial(expert_backward_kernel, fold), (*rows, *grads, ab, vec, first, second),
        [spec_in] * 4
        + [pl.BlockSpec((src, 2, 1, 8, cap), lambda e, h: (0, 0, kind * local + e, 0, 0)), pl.BlockSpec(vec.shape, lambda e, h: (0, 0))]
        + [spec_first, spec_second],
        [jax.ShapeDtypeStruct(s, BF16) for s in grown] + [jax.ShapeDtypeStruct(r.shape[1:], BF16) for r in rows],
        ([pl.BlockSpec(s, lambda e, h: (0, 0, 0, 0)) for s in grown] if fold else [spec_first, spec_second]) + [spec_rows] * 2,
        [pltpu.VMEM((2 * src * cap, width), F32), pltpu.VMEM((2 * src * cap, width), BF16)]
        + ([kept] * 3 + [pltpu.SemaphoreType.DMA((2, pairs))] * 2 if fold else []),
        (local, parts), "expert_backward",
        pl.CostEstimate(flops=10 * work, bytes_accessed=48 << 20, transcendentals=work // width), moving, cid, mate=fold,
    )


def scalar_kernel(scal_ref, rowsc0_ref, rowsc1_ref, slotrow_ref, cols_ref, ab_ref, got, sent, got2, send_sem, recv_sem, send_sem2, recv_sem2):
    src, micros, local, _, cap = scal_ref.shape
    tokens = rowsc0_ref.shape[1]
    me = group_of()[0]
    group_greet()
    moves = group_copies(scal_ref, got, send_sem, recv_sem)
    for c in moves:
        c.start()
    got[me] = scal_ref[me]
    for c in moves:
        c.wait()
    spot = lax.broadcasted_iota(jnp.int32, (cap, tokens), 0)
    sub = lax.broadcasted_iota(jnp.int32, (LANES, tokens), 0)
    sub8 = lax.broadcasted_iota(jnp.int32, (8, tokens), 0)
    slots = [[slotrow_ref[m, i : i + 1, :] for i in range(2)] for m in range(micros)]

    def onehot(m, s, which):
        per = local // 2
        base = (which // per) * (src * per) + s * per + which % per
        base = spot + base * cap
        return [jnp.where(base == t, 1.0, 0.0).astype(BF16) for t in slots[m]]

    zero = jnp.zeros((24, tokens), F32)

    def collect(s, carry):
        carry = list(carry)
        for which in range(local):
            for m in range(micros):
                values = split_three(got[s, m, which])
                for i, p in enumerate(onehot(m, s, which)):
                    carry[2 * m + i] = carry[2 * m + i] + mm(values, p)
        return tuple(carry)

    found_all = [join_three(f) for f in lax.fori_loop(0, src, collect, (zero,) * (2 * micros))]
    shares = []
    for m, rowsc_ref in enumerate((rowsc0_ref, rowsc1_ref)):
        found = found_all[2 * m : 2 * m + 2]
        stop, pull, gate0, gate1 = [rowsc_ref[i : i + 1, :] for i in range(4)]
        gates = [gate0, gate1]
        yh = [f[0:1, :] for f in found]
        yg = [f[1:2, :] for f in found]
        halting = jax.nn.sigmoid(stop + gate0 * yh[0] + gate1 * yh[1])
        s = (pull + gate0 * yg[0] + gate1 * yg[1]) * halting * (1.0 - halting)
        u = [halting * g + s * h for g, h in zip(yg, yh)]
        mean = gate0 * u[0] + gate1 * u[1]
        keep = [halting, s, gate0 * (u[0] - mean), gate1 * (u[1] - mean), gate0, gate1]
        table = jnp.zeros((LANES, tokens), F32)
        for i, r in enumerate(keep):
            table = jnp.where(sub == i, r, table)
        cols_ref[m] = jnp.transpose(table)[:, :8]
        shares.append(
            [split_three(jnp.where(sub8 == 0, g * halting, jnp.where(sub8 == 1, g * s, 0.0))) for g in gates]
        )

    def spread(s, carry):
        for which in range(local):
            for m in range(micros):
                picks = onehot(m, s, which)
                sent[s, m, which] = join_three(mm_nt(shares[m][0], picks[0]) + mm_nt(shares[m][1], picks[1]))
        return carry

    lax.fori_loop(0, src, spread, 0)
    moves = group_copies(sent, got2, send_sem2, recv_sem2)
    for c in moves:
        c.start()
    got2[me] = sent[me]
    for c in moves:
        c.wait()
    ab_ref[...] = got2[...]


def scalar_step(scal, rowsc, slotrow):
    vmem = pl.BlockSpec(memory_space=pltpu.VMEM)
    tokens = rowsc[0].shape[1]
    peers = scal.shape[0] - 1
    return pl.pallas_call(
        scalar_kernel,
        out_shape=(jax.ShapeDtypeStruct((2, tokens, 8), F32), jax.ShapeDtypeStruct(scal.shape, F32)),
        in_specs=[vmem] * 4,
        out_specs=[vmem] * 2,
        scratch_shapes=[pltpu.VMEM(scal.shape, F32)] * 3 + [pltpu.SemaphoreType.DMA((peers,))] * 4,
        compiler_params=pltpu.CompilerParams(collective_id=0, has_side_effects=True),
        cost_estimate=pl.CostEstimate(flops=10**9, bytes_accessed=1 << 20, transcendentals=tokens),
        name="scalar_step",
    )(scal, *rowsc, slotrow)


def result_kernel(has_old, *refs):
    x_ref, mid_ref, near_ref, far_ref, cols_ref, slotcol_ref = refs[:6]
    result_ref, hsum_ref = refs[-2:]
    tokens, width = mid_ref.shape
    chunk = 256
    chunks = near_ref.shape[0] // chunk
    lane = lane_iota(tokens, chunk)
    slot_c = [slotcol_ref[0, :, i : i + 1] for i in range(2)]

    def gather(k, carry):
        for kind, ref in enumerate((near_ref, far_ref)):
            block = ref[pl.ds(pl.multiple_of(k * chunk, chunk), chunk), :]
            base = lane + (k + kind * chunks) * chunk
            carry = tuple(
                c + mm(jnp.where(base == s, 1.0, 0.0).astype(BF16), block) for c, s in zip(carry, slot_c)
            )
        return carry

    zero = jnp.zeros((tokens, width), F32)
    picked = lax.fori_loop(0, chunks, gather, (zero, zero))
    cols = cols_ref[0]
    halting, s = cols[:, 0:1], cols[:, 1:2]
    x = x_ref[0].astype(F32)
    end = mid_ref[...] + (cols[:, 4:5] * picked[0] + cols[:, 5:6] * picked[1])
    result_ref[0] = (x + halting * (end - x)).astype(BF16)
    sub8 = lax.broadcasted_iota(jnp.int32, (8, width), 0)
    ssum = jnp.broadcast_to(jnp.sum(s, axis=0, keepdims=True), (1, width))
    hsum_ref[...] = jnp.where(sub8 == 0, fold_rows(s * end), jnp.where(sub8 == 1, ssum, 0.0))


def result_step(micro, tokens, mid, near, far, cols, slotcol, old, moving, cid):
    _, count, width = tokens.shape
    whole = lambda a: pl.BlockSpec(a.shape, lambda i: (0,) * a.ndim)
    part = pl.BlockSpec((1, count, width), lambda i: (micro, 0, 0))
    cols_spec = pl.BlockSpec((1, count, 8), lambda i: (micro, 0, 0))
    return run_kernel(
        functools.partial(result_kernel, bool(old)), (tokens, mid, near, far, cols, slotcol, *old),
        [part, whole(mid), whole(near), whole(far), cols_spec, cols_spec] + [pl.BlockSpec(memory_space=pl.ANY)] * len(old),
        (jax.ShapeDtypeStruct(tokens.shape, BF16), jax.ShapeDtypeStruct((8, width), F32)),
        [part, pl.BlockSpec((8, width), lambda i: (0, 0))], (), (1,), "result_step",
        pl.CostEstimate(
            flops=8 * count * near.shape[0] * width, bytes_accessed=5 << 20, transcendentals=count
        ),
        moving, cid, {6: 0} if old else None,
    )


def attention_backward_kernel(last, n_old, *refs):
    (x_ref, grad_ref, col_ref, vec_ref, qw_ref, kvr_ref, proj_ref, frw_ref,
     mid_ref, n2_ref, normed_ref, mixed_ref, probs_ref, qs_ref, kv_ref, gates_ref, slotcol_ref,
     near_ref, far_ref, cols_ref) = refs[:20]
    old = refs[20 : 20 + n_old]
    gtok_ref = refs[20 + n_old]
    outs = refs[21 + n_old : -6]
    gsum, gq_ref, gproj_ref, gkvr_ref, gfr_ref, gvec_ref = refs[-6:]
    step = pl.program_id(0)
    rows, width = mid_ref.shape
    lane = lane_iota(rows)
    low = lane < LANES // 2
    col = col_ref[0]
    chunk = 256
    cols = cols_ref[0]
    slot_c = [slotcol_ref[0, :, i : i + 1] for i in range(2)]
    lane_c = lane_iota(rows, chunk)
    accs = (gq_ref, gproj_ref, gkvr_ref, gfr_ref, gvec_ref)

    @pl.when(step == 0)
    def _():
        for k, ref in enumerate(accs):
            ref[...] = old[k][...] if old else jnp.zeros_like(ref)

    gsum[...] = jnp.zeros_like(gsum)

    chunks = near_ref.shape[0] // chunk

    def gather(k, carry):
        for kind, ref in enumerate((near_ref, far_ref)):
            block = ref[pl.ds(pl.multiple_of(k * chunk, chunk), chunk), :]
            base = lane_c + (k + kind * chunks) * chunk
            pick = jnp.where((base == slot_c[0]) | (base == slot_c[1]), 1.0, 0.0).astype(BF16)
            gsum[...] += mm(pick, block)
        return carry

    lax.fori_loop(0, chunks, gather, 0)
    glog = jnp.zeros((rows, LANES), F32)
    for i in range(2):
        glog = jnp.where(lane == col[:, 4 + i : 5 + i], cols[:, 2 + i : 3 + i], glog)
    glog = glog.astype(BF16)
    n2 = n2_ref[...]
    gfr_ref[...] += mm_tn(glog, n2)
    gn2 = gsum[...] + mm_nt(glog, frw_ref[...])
    hat2, rstd2 = norm_parts(mid_ref[...])
    grad = grad_ref[0].astype(F32)
    halting = cols[:, 0:1]
    gend = halting * grad + cols[:, 1:2] * vec_ref[4:5, :]
    gmid = gend + norm_back(hat2, rstd2, vec_ref[2:3, :], gn2)
    ggain2 = fold_rows(gn2 * hat2)
    gbias2 = fold_rows(gn2)
    gattn = gmid.astype(BF16)
    gproj_ref[...] += mm_tn(gattn, mixed_ref[...])
    gmixed = mm_nt(gattn, proj_ref[...]).astype(BF16).astype(F32)
    pairs = gmixed.shape[1] // LANES
    tiles = [gmixed[:, j * LANES : (j + 1) * LANES] for j in range(pairs)]
    kv = kv_ref[...]
    scale = 0.125
    routes = [col[:, i : i + 1] for i in range(4)]
    gkv = jnp.zeros((LANES, rows), F32)
    ggates = []
    parts = []
    for i in range(4):
        gate = gates_ref[:, i : i + 1]
        sel = pltpu.roll(pick_head(tiles, routes[i], lane), LANES // 2, 1)
        sel = jnp.where(low, 0.0, sel)
        probs = probs_ref[0, i]
        heads = mm(probs, kv)
        ggates.append(jnp.sum(heads * sel, axis=-1, keepdims=True))
        gheads = (gate * sel).astype(BF16)
        gprobs = mm_nt(gheads, kv)
        probs_f = probs.astype(F32)
        inner = jnp.sum(heads * gheads.astype(F32), axis=-1, keepdims=True)
        gscores = (probs_f * (gprobs - inner)).astype(BF16)
        gkv = gkv + mm_tn(gheads, probs) + mm_tn(qs_ref[0, i], gscores) * scale
        gq = mm(gscores, kv) * scale
        parts.append(jnp.where(low, gq, pltpu.roll(gq, LANES // 2, 1)))
    gtiles = place_heads(parts, routes, pairs, lane)
    gquery = jnp.concatenate([t.astype(BF16) for t in gtiles], axis=1)
    normed = normed_ref[...]
    gq_ref[...] += mm_tn(normed, gquery)
    mean = ggates[0] * gates_ref[:, 0:1]
    for i in range(1, 4):
        mean = mean + ggates[i] * gates_ref[:, i : i + 1]
    alog = jnp.zeros((rows, LANES), F32)
    for i in range(4):
        alog = jnp.where(lane == routes[i], gates_ref[:, i : i + 1] * (ggates[i] - mean), alog)
    gkvr = jnp.concatenate([jnp.transpose(gkv).astype(BF16), alog.astype(BF16)], axis=1)
    gkvr_ref[...] += mm_tn(gkvr, normed)
    gnormed = mm_nt(gquery, qw_ref[...]) + mm_nt(gkvr, kvr_ref[...])
    hat, rstd = norm_parts(x_ref[0].astype(F32))
    gtok_ref[0] = grad * (1.0 - halting) + gmid + norm_back(hat, rstd, vec_ref[0:1, :], gnormed)
    sub8 = lax.broadcasted_iota(jnp.int32, (8, width), 0)
    gvec = jnp.where(sub8 == 0, fold_rows(gnormed * hat), 0.0)
    gvec = jnp.where(sub8 == 1, fold_rows(gnormed), gvec)
    gvec = jnp.where(sub8 == 2, ggain2, gvec)
    gvec_ref[...] += jnp.where(sub8 == 3, gbias2, gvec)

    @pl.when(step == pl.num_programs(0) - 1)
    def _():
        if not last:
            for ref, out in zip(accs, outs):
                out[...] = ref[...]
            return
        pack, gvec_out = outs
        gvec_out[...] = gvec_ref[...]
        blocks = gq_ref.shape[1] // width
        for j in range(blocks):
            pack[j * width : (j + 1) * width, :] = gq_ref[:, j * width : (j + 1) * width].astype(BF16)
        place = blocks * width
        for j in range(blocks):
            pack[place : place + width, :] = jnp.transpose(gproj_ref[:, j * width : (j + 1) * width]).astype(BF16)
            place = place + width
        for ref in (gkvr_ref, gfr_ref):
            pack[place : place + ref.shape[0], :] = ref[...].astype(BF16)
            place = place + ref.shape[0]
        pack[place:, :] = jnp.zeros((pack.shape[0] - place, width), BF16)


def attention_backward(micro, last, packed_rows, tokens, grad, col, vec, qw, kvr, proj, frw, saved, near, far, cols, old, moving, cid):
    mid, n2, normed, mixed, probs, qs, kv, gates, slotcol = saved
    _, count, width = tokens.shape
    steps = count // SEQ
    inner = qw.shape[1]
    whole = lambda a: pl.BlockSpec(a.shape, lambda r: (0,) * a.ndim)
    by_row = lambda c: pl.BlockSpec((SEQ, c), lambda r: (r, 0))
    part = pl.BlockSpec((1, SEQ, width), lambda r: (micro, r, 0))
    grown = [qw.shape] + [a.shape[::-1] for a in (proj, kvr, frw)]
    out_shape = [jax.ShapeDtypeStruct(tokens.shape, F32)]
    if last:
        out_shape += [jax.ShapeDtypeStruct((packed_rows, width), BF16)]
    else:
        out_shape += [jax.ShapeDtypeStruct(s, F32) for s in grown]
    out_shape += [jax.ShapeDtypeStruct((8, width), F32)]
    old_in = [old[k] for k in (1, 2, 3, 4, 5)] if old else []
    hbm = pl.BlockSpec(memory_space=pl.ANY)
    cols_spec = pl.BlockSpec((1, SEQ, 8), lambda r: (micro, r, 0))
    in_specs = [
        part, part, cols_spec,
        whole(vec), whole(qw), whole(kvr), whole(proj), whole(frw),
        by_row(width), by_row(width), by_row(width), by_row(inner),
        pl.BlockSpec((1, 4, SEQ, SEQ), lambda r: (r, 0, 0, 0)),
        pl.BlockSpec((1, 4, SEQ, LANES), lambda r: (r, 0, 0, 0)),
        by_row(LANES), by_row(8), cols_spec,
        whole(near), whole(far), cols_spec,
    ] + [whole(o) for o in old_in] + [hbm] * (1 if old else 0)
    args = (
        tokens, grad, col, vec, qw, kvr, proj, frw, mid, n2, normed, mixed, probs, qs, kv, gates, slotcol, near, far, cols,
        *old_in, *(old[:1] if old else []),
    )
    return run_kernel(
        functools.partial(attention_backward_kernel, last, len(old_in) + (1 if old else 0)), args, in_specs,
        out_shape, [part] + [pl.BlockSpec(o.shape, lambda r: (0, 0)) for o in out_shape[1:]],
        [
            pltpu.VMEM((SEQ, width), F32),
            *[pltpu.VMEM(s, F32) for s in grown],
            pltpu.VMEM((8, width), F32),
        ],
        (steps,), "attention_backward",
        pl.CostEstimate(
            flops=2 * count * width * (4 * inner + 512 + 2 * near.shape[0]), bytes_accessed=24 << 20, transcendentals=0
        ),
        moving, cid, {25: 0} if old else None,
    )


def total_plan(n_expert, n_hidden, rows):
    ny = nx = n_hidden // 2
    nz = n_expert // nx
    unit = 16 * ny * nx * nz
    units = -(-rows // (2 * unit))
    count = min(units, STREAMS)
    streams = tuple((units // count + (i < units % count)) * unit for i in range(count))
    return (nz, nx, ny), streams


def total_kernel(
    sizes, streams, pack_ref, small_ref, out_ref, sum_ref,
    buf, done, core_in, land, small_got, small_part, small_got2, sems, small_sems,
):
    nz, nx, ny = sizes
    e, h = lax.axis_index("expert"), lax.axis_index("hidden")
    n_expert, n_hidden = nz * nx, ny * 2
    z, x = lax.div(e, nx), lax.rem(e, nx)
    y, c = lax.div(h, 2), lax.rem(h, 2)
    half = sum(streams)
    width = pack_ref.shape[1]
    mesh_id = pl.DeviceIdType.MESH
    barrier = pltpu.get_barrier_semaphore()
    for k in range(1, n_expert):
        pl.semaphore_signal(barrier, inc=1, device_id=(lax.rem(e + k, n_expert), h), device_id_type=mesh_id)
    for k in range(1, n_hidden):
        pl.semaphore_signal(barrier, inc=1, device_id=(e, lax.rem(h + k, n_hidden)), device_id_type=mesh_id)
    pl.semaphore_wait(barrier, n_expert + n_hidden - 2)
    used = {}

    def copy(source, target, device, pool=sems):
        i = used.get(id(pool), 0)
        used[id(pool)] = i + 1
        return pltpu.make_async_remote_copy(
            source, target, pool.at[0, i], pool.at[1, i], device_id=device, device_id_type=mesh_id
        )

    def rows_at(ref, start, count):
        return ref.at[pl.ds(pl.multiple_of(start, 16), count)]

    def add_rows(start, count, base, pieces):
        step = 64 if count % 64 == 0 else 16

        def body(i, carry):
            place = pl.ds(pl.multiple_of(start + i * step, 16), step)
            total = base[place, :].astype(F32)
            for ref in pieces:
                total = total + ref[pl.ds(pl.multiple_of(i * step, 16), step), :].astype(F32)
            buf[place, :] = total.astype(BF16)
            return carry

        lax.fori_loop(0, count // step, body, 0)

    axes = {
        "c": (2, c, lambda p: (e, y * 2 + p)),
        "y": (ny, y, lambda p: (e, p * 2 + c)),
        "x": (nx, x, lambda p: (z * nx + p, h)),
        "z": (nz, z, lambda p: (p * nx + x, h)),
    }
    landed = [0]

    def travel(first, count, order, delay):
        for _ in range(delay):
            yield
        moves = [copy(rows_at(pack_ref, (1 - c) * half + first, count), rows_at(core_in, first, count), axes["c"][2](1 - c))]
        for m in moves:
            m.start()
        yield
        for m in moves:
            m.wait()
        start, span = c * half + first, count
        add_rows(start, span, pack_ref, [core_in.at[pl.ds(first, count)]])
        trail = []
        for name in order:
            size, me, device = axes[name]
            chunk = span // size
            moves, pieces = [], []
            for k in range(1, size):
                peer = lax.rem(me + k, size)
                pieces.append(land.at[pl.ds(landed[0], chunk)])
                landed[0] += chunk
                moves.append(copy(rows_at(buf, start + peer * chunk, chunk), pieces[-1], device(peer)))
            for m in moves:
                m.start()
            yield
            for m in moves:
                m.wait()
            start, span = start + me * chunk, chunk
            trail.append((start, chunk, size, me, device))
            add_rows(start, span, buf, pieces)
        here = pl.ds(pl.multiple_of(start, 16), span)
        done[here, :] = buf[here, :]
        for begin, chunk, size, me, device in reversed(trail):
            place = rows_at(done, begin, chunk)
            moves = [copy(place, place, device(lax.rem(me + k, size))) for k in range(1, size)]
            for m in moves:
                m.start()
            yield
            for m in moves:
                m.wait()
        place = rows_at(done, c * half + first, count)
        moves = [copy(place, place, axes["c"][2](1 - c))]
        for m in moves:
            m.start()
        yield
        for m in moves:
            m.wait()

    def travel_small():
        moves = [
            copy(small_ref, small_got.at[e], (lax.rem(e + k, n_expert), h), small_sems) for k in range(1, n_expert)
        ]
        for m in moves:
            m.start()
        small_got[e] = small_ref[...]
        yield
        yield
        for m in moves:
            m.wait()
        small_part[...] = jnp.sum(small_got[...], axis=0)
        moves = [
            copy(small_part, small_got2.at[h], (e, lax.rem(h + k, n_hidden)), small_sems) for k in range(1, n_hidden)
        ]
        for m in moves:
            m.start()
        small_got2[h] = small_part[...]
        yield
        yield
        for m in moves:
            m.wait()
        sum_ref[...] = jnp.sum(small_got2[...], axis=0)

    going, first = [], 0
    for i, count in enumerate(streams):
        going.append(travel(first, count, ("yxz", "xyz")[i % 2], 2 * (i >= len(streams) // 2)))
        first += count
    going.append(travel_small())
    while going:
        going = [g for g in going if next(g, StopIteration) is not StopIteration]
    step = 64 if half % 64 == 0 else 16

    def body(i, carry):
        here = pl.ds(pl.multiple_of(i * step, step), step)
        out_ref[here, :] = done[here, :]
        return carry

    lax.fori_loop(0, 2 * half // step, body, 0)


def total_step(n_expert, n_hidden, rows, pack, small):
    sizes, streams = total_plan(n_expert, n_hidden, rows)
    nz, nx, ny = sizes
    width = pack.shape[1]
    half = sum(streams)
    vmem = pl.BlockSpec(memory_space=pltpu.VMEM)
    landing = 0
    for i, span in enumerate(streams):
        for size in ((ny, nx, nz), (nx, ny, nz))[i % 2]:
            span = span // size
            landing += span * (size - 1)
    steps = len(streams) * (2 + 2 * ((ny - 1) + (nx - 1) + (nz - 1)))
    return pl.pallas_call(
        functools.partial(total_kernel, sizes, streams),
        out_shape=(jax.ShapeDtypeStruct(pack.shape, BF16), jax.ShapeDtypeStruct(small.shape, F32)),
        in_specs=[vmem] * 2,
        out_specs=[vmem] * 2,
        scratch_shapes=[
            pltpu.VMEM((2 * half, width), BF16),
            pltpu.VMEM((2 * half, width), BF16),
            pltpu.VMEM((half, width), BF16),
            pltpu.VMEM((landing, width), BF16),
            pltpu.VMEM((n_expert,) + small.shape, F32),
            pltpu.VMEM(small.shape, F32),
            pltpu.VMEM((n_hidden,) + small.shape, F32),
            pltpu.SemaphoreType.DMA((2, steps)),
            pltpu.SemaphoreType.DMA((2, n_expert + n_hidden)),
        ],
        compiler_params=pltpu.CompilerParams(collective_id=8, has_side_effects=True, vmem_limit_bytes=VMEM_LIMIT),
        name="total_step",
    )(pack, small)


def unpack_kernel(
    pack_ref, near_a, near_b, far_a, far_b,
    gq_ref, gproj_ref, first_ref, second_ref, key_ref, value_ref, router_ref, ffn_ref,
):
    step = pl.program_id(0)
    width = pack_ref.shape[2]
    blocks = gproj_ref.shape[0]
    for j in range(blocks):
        gq_ref[:, j * width : (j + 1) * width] = pack_ref[j].astype(F32)
        gproj_ref[j] = pack_ref[blocks + j].astype(F32)
    first_ref[...] = near_a[...].astype(F32) + far_a[...].astype(F32)
    second_ref[...] = near_b[...].astype(F32) + far_b[...].astype(F32)
    head = key_ref.shape[0]

    @pl.when(step == 0)
    def _():
        key_ref[...] = pack_ref[2 * blocks, :head, :].astype(F32)
        value_ref[...] = pack_ref[2 * blocks, head : 2 * head, :].astype(F32)

    @pl.when(step == 1)
    def _():
        router_ref[...] = pack_ref[2 * blocks, : router_ref.shape[0], :].astype(F32)

    @pl.when(step == 2)
    def _():
        ffn_ref[...] = pack_ref[2 * blocks, : ffn_ref.shape[0], :].astype(F32)


def unpack_step(pack, near, far, head, routes, experts):
    steps = 4
    slabs, width, _ = pack.shape
    blocks = slabs // 2
    rows = width // steps
    out_shape = [
        jax.ShapeDtypeStruct((width, blocks * width), F32),
        jax.ShapeDtypeStruct((blocks, width, width), F32),
        *[jax.ShapeDtypeStruct(a.shape, F32) for a in near],
        *[jax.ShapeDtypeStruct((n, width), F32) for n in (head, head, routes, experts)],
    ]
    cut = lambda a: pl.BlockSpec((a.shape[0], a.shape[1] // steps, a.shape[2]), lambda i: (0, i, 0))
    return run_kernel(
        unpack_kernel, (pack, *near, *far), [cut(pack)] + [cut(a) for a in near] * 2, out_shape,
        [pl.BlockSpec((rows, blocks * width), lambda i: (i, 0)), cut(out_shape[1])] + [cut(a) for a in near]
        + [pl.BlockSpec(o.shape, lambda i: (0, 0)) for o in out_shape[4:]],
        (), (steps,), "unpack_step", pl.CostEstimate(flops=0, bytes_accessed=20 << 20, transcendentals=0),
    )


def pad_lanes(a):
    return jnp.pad(a, ((0, 0), (0, LANES - a.shape[1])))


def per_device(
    tokens, grad_out, attn_routes, ffn_routes, segments, pad_mask, norm1_gain, norm1_bias, attn_router,
    query_w, key_w, value_w, attn_proj, norm2_gain, norm2_bias, ffn_router, expert_in, expert_out, halt_w, halt_b,
    *, n_expert, n_hidden,
):
    micros, count, width = tokens.shape
    experts = ffn_router.shape[1]
    capacity = 4 * count // experts
    slots = experts * capacity
    per = experts // n_expert
    group = n_expert // 2
    across = [(i, (i + group) % n_expert) for i in range(n_expert)]

    def gathered(a):
        return lax.all_gather(a, "hidden", axis=0, tiled=False)

    crossed = [lax.ppermute(a, "expert", across) for a in (expert_in, expert_out)]
    near_first, near_second = gathered(expert_in), gathered(expert_out)
    seg = segments.reshape(micros, count)
    zeros = jnp.zeros_like(seg)
    mine = lax.axis_index("expert") // group
    kind = (ffn_routes // (experts // 2) != mine).astype(jnp.int32)
    base = (kind * (experts // 2) + ffn_routes % (experts // 2)) * capacity
    col = jnp.concatenate([attn_routes, ffn_routes, seg[:, :, None], pad_mask[:, :, None]], axis=2)
    row = jnp.stack(
        [seg, pad_mask, ffn_routes[:, :, 0], ffn_routes[:, :, 1], base[:, :, 0], base[:, :, 1], zeros, zeros], axis=1
    )
    none = jnp.zeros_like(halt_w)
    vec = jnp.stack([norm1_gain, norm1_bias, norm2_gain, norm2_bias, halt_w, none, none, none])
    kvr = jnp.concatenate([key_w, value_w, pad_lanes(attn_router)], axis=1)
    frw = pad_lanes(ffn_router)
    hb = jnp.broadcast_to(halt_b.reshape(1, 1), (8, LANES))
    shape = (2, group, per, capacity, width)
    packed = query_w.size // width + attn_proj.shape[0] + width
    packed_rows = 2 * sum(total_plan(n_expert, n_hidden, packed)[1])

    slotrow, slotcol = route_step(row)
    weights = (vec, hb, query_w, kvr, attn_proj, frw)
    f0 = attention_forward(0, tokens, grad_out, col, row, slotrow, *weights, slots, (), None)
    crossed[0], n0_out = lax.optimization_barrier((crossed[0], f0[9]))
    far_first = gathered(crossed[0])
    *f1, n0 = attention_forward(1, tokens, grad_out, col, row, slotrow, *weights, slots, [n0_out.reshape(shape)], 2)
    crossed[1], n1_out = lax.optimization_barrier((crossed[1], f1[9]))
    far_second = gathered(crossed[1])
    gs0, gs1, n1 = spread_step(slotrow, grad_out, slots, [n1_out.reshape(shape)], 3)
    rows = (n0, n1)
    y0, y1, g1 = expert_forward(0, rows, near_first, near_second, [gs1.reshape(shape)], 4)
    far0, far1, g0 = expert_forward(1, rows, far_first, far_second, [gs0.reshape(shape)], 1)
    grads = (g0, g1)
    scal = reading_step((y0, y1, far0, far1), grads, vec)
    cols, ab = scalar_step(scal, (f0[8], f1[8]), slotrow)
    gf_far, gs_far, bf0, bf1, r0, rf0, r1 = expert_backward(
        1, rows, grads, ab, vec, far_first, far_second, [y0, far0, y1], 9
    )
    gf_near, gs_near, bn0, bn1, qf0, qf1, rf1 = expert_backward(
        0, rows, grads, ab, vec, near_first, near_second, [bf0, bf1, far1], 10
    )

    flat = lambda a: a.reshape(slots // 2, width)

    def reduced(a):
        ranks = [[2 * y + c for y in range(n_hidden // 2)] for c in range(2)]
        groups = ranks if a.shape[0] < n_hidden else None
        return lax.psum_scatter(a, "hidden", scatter_dimension=0, axis_index_groups=groups, tiled=False)

    far_grads = [reduced(a) for a in (gf_far, gs_far)]
    near_grads = [reduced(a) for a in (gf_near, gs_near)]
    *res0, qn0, qn1 = result_step(0, tokens, f0[0], flat(r0), flat(rf0), cols, slotcol, (), [bn0, bn1], 11)
    common = (tokens, grad_out, col, vec, query_w, kvr, attn_proj, frw)
    far_grads[0], qn0 = lax.optimization_barrier((far_grads[0], qn0))
    far_grads[0] = lax.ppermute(far_grads[0], "expert", across)
    out = attention_backward(
        0, False, packed_rows, *common, list(f0[:8]) + [slotcol], flat(qn0), flat(qf0), cols, (), (), None
    )
    res1 = result_step(1, tokens, f1[0], flat(r1), flat(rf1), cols, slotcol, tuple(res0[:1]), (), None)
    out, far_grads[1] = lax.optimization_barrier((tuple(out), far_grads[1]))
    far_grads[1] = lax.ppermute(far_grads[1], "expert", across)
    out = attention_backward(
        1, True, packed_rows, *common, list(f1[:8]) + [slotcol], flat(qn1), flat(qf1), cols, tuple(out), (), None
    )
    packs = out[1]
    small = jnp.concatenate([out[2], res0[1] + res1[1]], axis=0)
    total, small = total_step(n_expert, n_hidden, packed, packs, small)
    near_grads = [a.reshape(a.shape[-3:]) for a in near_grads]
    far_grads = [a.reshape(a.shape[-3:]) for a in far_grads]
    gq, gproj, gfirst, gsecond, gkey, gvalue, grouter, gfr = unpack_step(
        total[:packed].reshape(-1, width, width), near_grads, far_grads, key_w.shape[1], attn_router.shape[1], experts
    )
    return (
        res1[0],
        out[0],
        small[0],
        small[1],
        grouter.T,
        gq,
        gkey.T,
        gvalue.T,
        gproj.reshape(attn_proj.shape),
        small[2],
        small[3],
        gfr.T,
        gfirst,
        gsecond,
        small[8],
        small[9, :1],
    )


def solution(mesh):
    rows = P(None, ("expert", "hidden"), None)
    in_specs = (rows,) * 5 + (P(None, ("expert", "hidden")),) + (P(),) * 10 + (
        P("expert", None, "hidden"), P("expert", "hidden", None), P(), P(),
    )
    out_specs = (rows,) * 2 + (P(),) * 10 + (P("expert", None, "hidden"), P("expert", "hidden", None), P(), P())
    return jax.shard_map(
        functools.partial(per_device, n_expert=mesh.shape["expert"], n_hidden=mesh.shape["hidden"]),
        mesh=mesh, in_specs=in_specs, out_specs=out_specs, check_vma=False,
    )
```

```python
import functools
import math

import jax
import jax.numpy as jnp
from jax import lax
from jax.experimental import pallas as pl
from jax.experimental.pallas import tpu as pltpu
from jax.sharding import PartitionSpec as P

SEQ = 256
LANES = 128
F32 = jnp.float32
BF16 = jnp.bfloat16
GELU_C = math.sqrt(2.0 / math.pi)
GELU_A = 0.044715
VMEM_LIMIT = 60 * 1024 * 1024
STREAMS = 7


def mm(left, right):
    return jnp.dot(left, right, preferred_element_type=F32)


def mm_nt(left, right):
    return lax.dot_general(left, right, (((1,), (1,)), ((), ())), preferred_element_type=F32)


def mm_tn(left, right):
    return lax.dot_general(left, right, (((0,), (0,)), ((), ())), preferred_element_type=F32)


def lane_iota(rows, lanes=LANES):
    return lax.broadcasted_iota(jnp.int32, (rows, lanes), 1)


def norm_parts(value):
    center = value - jnp.mean(value, axis=-1, keepdims=True)
    rstd = lax.rsqrt(jnp.mean(center * center, axis=-1, keepdims=True) + 1e-05)
    return center * rstd, rstd


def norm_back(hat, rstd, gain, grad):
    scaled = grad * gain
    first = jnp.mean(scaled, axis=-1, keepdims=True)
    second = jnp.mean(scaled * hat, axis=-1, keepdims=True)
    return rstd * (scaled - first - hat * second)


def fold_rows(value):
    return jnp.sum(value, axis=0, keepdims=True)


def pick_head(tiles, route, lane):
    route = jnp.broadcast_to(route, lane.shape)
    pair = lax.shift_right_logical(route, 1)
    out = tiles[0]
    for j in range(1, len(tiles)):
        out = jnp.where(pair == j, tiles[j], out)
    odd = (route & 1) == 1
    return jnp.where(odd, pltpu.roll(out, LANES // 2, 1), out)


def place_heads(parts, routes, count, lane):
    half = lax.shift_right_logical(lane, 6)
    routes = [jnp.broadcast_to(r, lane.shape) for r in routes]
    kept = [jnp.where(half == (r & 1), p, 0.0) for p, r in zip(parts, routes)]
    pairs = [lax.shift_right_logical(r, 1) for r in routes]
    tiles = []
    for j in range(count):
        total = jnp.where(pairs[0] == j, kept[0], 0.0)
        for k, p in zip(kept[1:], pairs[1:]):
            total = total + jnp.where(p == j, k, 0.0)
        tiles.append(total)
    return tiles


def softmax_cols(cols):
    top = functools.reduce(jnp.maximum, cols)
    expo = [jnp.exp(c - top) for c in cols]
    total = functools.reduce(jnp.add, expo)
    return [e / total for e in expo]


def put_cols(cols, rows, width):
    lane = lane_iota(rows, width)
    out = jnp.zeros((rows, width), cols[0].dtype)
    for i, c in enumerate(cols):
        out = jnp.where(lane == i, c, out)
    return out


def split_three(value):
    high = value.astype(BF16)
    rest = value - high.astype(F32)
    middle = rest.astype(BF16)
    last = (rest - middle.astype(F32)).astype(BF16)
    return jnp.concatenate([high.astype(F32), middle.astype(F32), last.astype(F32)], axis=0).astype(BF16)


def join_three(value):
    n = value.shape[0] // 3
    return value[:n] + value[n : 2 * n] + value[2 * n :]


def row_to_col(row):
    n = row.shape[1]
    place = lax.broadcasted_iota(jnp.int32, (n, n), 0)
    other = lax.broadcasted_iota(jnp.int32, (n, n), 1)
    return jnp.sum(jnp.where(place == other, row, 0.0), axis=-1, keepdims=True)


def dispatch(slot_rows, values, out_ref):
    chunk = 256
    tokens = values[0].shape[0]
    spot = lax.broadcasted_iota(jnp.int32, (chunk, tokens), 0)

    def body(k, carry):
        base = spot + k * chunk
        if len(values) == 1:
            pick = jnp.where((base == slot_rows[0]) | (base == slot_rows[1]), 1.0, 0.0).astype(BF16)
            out = mm(pick, values[0][...])
        else:
            out = mm(jnp.where(base == slot_rows[0], 1.0, 0.0).astype(BF16), values[0][...])
            out = out + mm(jnp.where(base == slot_rows[1], 1.0, 0.0).astype(BF16), values[1][...])
        out_ref[pl.ds(pl.multiple_of(k * chunk, chunk), chunk), :] = out.astype(BF16)
        return carry

    lax.fori_loop(0, out_ref.shape[0] // chunk, body, 0)


def group_of():
    size = lax.axis_size("expert") // 2
    e = lax.axis_index("expert")
    me = lax.rem(e, size)
    return me, size, e - me


def other_core():
    e, h = lax.axis_index("expert"), lax.axis_index("hidden")
    return e, h + 1 - 2 * lax.rem(h, 2)


def group_greet(mate=False):
    me, size, base = group_of()
    other = lax.axis_index("hidden")
    barrier = pltpu.get_barrier_semaphore()
    for k in range(1, size):
        pl.semaphore_signal(
            barrier, inc=1, device_id=(base + lax.rem(me + k, size), other), device_id_type=pl.DeviceIdType.MESH
        )
    if mate:
        pl.semaphore_signal(barrier, inc=1, device_id=other_core(), device_id_type=pl.DeviceIdType.MESH)
    pl.semaphore_wait(barrier, size if mate else size - 1)


def group_copies(source, target, send_sem, recv_sem):
    me, size, base = group_of()
    other = lax.axis_index("hidden")
    moves = []
    for k in range(1, size):
        peer = lax.rem(me + k, size)
        moves.append(
            pltpu.make_async_remote_copy(
                source.at[peer], target.at[me], send_sem.at[k - 1], recv_sem.at[k - 1],
                device_id=(base + peer, other), device_id_type=pl.DeviceIdType.MESH,
            )
        )
    return moves


def at_step(which):
    found = True
    for axis, size in enumerate(which[1]):
        here = pl.program_id(axis) == (0 if which[0] == 0 else size - 1)
        found = here if found is True else found & here
    return found


def run_kernel(kernel, args, in_specs, out_shape, out_specs, scratch, grid, name, cost, moving=(), cid=None, aliases=None, mate=False):
    n_in, n_out, n_move = len(args), len(out_shape), len(moving)
    peers = lax.axis_size("expert") // 2 - 1
    hbm = pl.BlockSpec(memory_space=pl.ANY)

    def body(*refs):
        ins, sources = refs[:n_in], refs[n_in : n_in + n_move]
        outs = refs[n_in + n_move : n_in + n_move + n_out]
        targets = refs[n_in + n_move + n_out : n_in + 2 * n_move + n_out]
        rest = refs[n_in + 2 * n_move + n_out :]
        sems = rest[len(scratch) :]
        moves, owns = [], []
        me = group_of()[0]
        pairs = []
        for a, b in zip(sources, targets):
            pairs += [(a, b)] if len(a.shape) == 4 else [(a.at[i], b.at[i]) for i in range(a.shape[0])]
        for i, (a, b) in enumerate(pairs):
            moves += group_copies(a, b, sems[3 * i], sems[3 * i + 1])
            owns.append(pltpu.make_async_copy(a.at[me], b.at[me], sems[3 * i + 2]))

        if moving:

            @pl.when(at_step((0, grid)))
            def _():
                group_greet(mate)
                for c in moves + owns:
                    c.start()

        kernel(*ins, *outs, *rest[: len(scratch)])

        if moving:

            @pl.when(at_step((1, grid)))
            def _():
                for c in moves + owns:
                    c.wait()

    sems = []
    for _ in range(sum(1 if a.ndim == 4 else a.shape[0] for a in moving)):
        sems += [pltpu.SemaphoreType.DMA((peers,)), pltpu.SemaphoreType.DMA((peers,)), pltpu.SemaphoreType.DMA]
    more = dict(collective_id=cid, has_side_effects=True) if moving else {}
    return pl.pallas_call(
        body,
        grid=grid,
        out_shape=tuple(out_shape) + tuple(jax.ShapeDtypeStruct(a.shape, a.dtype) for a in moving),
        in_specs=list(in_specs) + [hbm] * n_move,
        out_specs=list(out_specs) + [hbm] * n_move,
        scratch_shapes=list(scratch) + sems,
        input_output_aliases=aliases or {},
        compiler_params=pltpu.CompilerParams(vmem_limit_bytes=VMEM_LIMIT, **more),
        cost_estimate=cost,
        name=name,
    )(*args, *moving)


def route_kernel(row_ref, slotrow_ref, slotcol_ref):
    tokens = row_ref.shape[2]
    before = lax.broadcasted_iota(jnp.int32, (tokens, tokens), 0)
    after = lax.broadcasted_iota(jnp.int32, (tokens, tokens), 1)
    upper = jnp.where(before < after, 1.0, 0.0).astype(BF16)
    sub = lax.broadcasted_iota(jnp.int32, (LANES, tokens), 0)
    sub8 = lax.broadcasted_iota(jnp.int32, (8, tokens), 0)
    for m in range(row_ref.shape[0]):
        row = row_ref[m]
        named = [jnp.where(sub == row[2 + i : 3 + i, :], 1.0, 0.0) for i in range(2)]
        rank = mm((named[0] + named[1]).astype(BF16), upper)
        slots = [fold_rows(named[i] * rank).astype(jnp.int32) + row[4 + i : 5 + i, :] for i in range(2)]
        slotrow_ref[m] = jnp.where(sub8 == 0, slots[0], slots[1])
        table = jnp.where(sub == 0, slots[0].astype(F32), slots[1].astype(F32))
        slotcol_ref[m] = jnp.transpose(table)[:, :8].astype(jnp.int32)


def route_step(row):
    micros, _, count = row.shape
    out_shape = (
        jax.ShapeDtypeStruct((micros, 8, count), jnp.int32),
        jax.ShapeDtypeStruct((micros, count, 8), jnp.int32),
    )
    whole = lambda s: pl.BlockSpec(s, lambda i: (0,) * len(s))
    return run_kernel(
        route_kernel, (row,), [whole(row.shape)], out_shape, [whole(o.shape) for o in out_shape], (), (1,), "route_step",
        pl.CostEstimate(flops=10**8, bytes_accessed=1 << 20, transcendentals=0),
    )


def spread_kernel(slotrow_ref, grad_ref, out0_ref, out1_ref):
    for m, out_ref in enumerate((out0_ref, out1_ref)):
        dispatch([slotrow_ref[m, 0:1, :], slotrow_ref[m, 1:2, :]], [grad_ref.at[m]], out_ref)


def spread_step(slotrow, grad, slots, moving, cid):
    width = grad.shape[2]
    whole = lambda s: pl.BlockSpec(s, lambda i: (0,) * len(s))
    return run_kernel(
        spread_kernel, (slotrow, grad), [whole(slotrow.shape), whole(grad.shape)],
        [jax.ShapeDtypeStruct((slots, width), BF16)] * 2, [whole((slots, width))] * 2, (), (1,), "spread_step",
        pl.CostEstimate(flops=8 * slots * width * grad.shape[1], bytes_accessed=6 << 20, transcendentals=0), moving, cid,
    )


def attention_forward_kernel(
    x_ref, grad_ref, col_ref, row_ref, slotrow_ref, vec_ref, hb_ref, qw_ref, kvr_ref, proj_ref, frw_ref,
    mid_ref, n2_ref, normed_ref, mixed_ref, probs_ref, qs_ref, kv_ref, gates_ref, scal_ref, out_ref,
    n2_all,
):
    step = pl.program_id(0)
    rows = x_ref.shape[1]
    top_attn = 4
    lane = lane_iota(rows)
    x = x_ref[0].astype(F32)
    col = col_ref[0]
    row = row_ref[0]
    hat, _ = norm_parts(x)
    normed = (hat * vec_ref[0:1, :] + vec_ref[1:2, :]).astype(BF16)
    normed_ref[...] = normed
    kvr = mm(normed, kvr_ref[...])
    kv = kvr[:, :LANES].astype(BF16)
    kv_ref[...] = kv
    logits = kvr[:, LANES:]
    routes = [col[:, i : i + 1] for i in range(top_attn)]
    picked = [
        jnp.sum(jnp.where(lane == r, logits, 0.0), axis=-1, keepdims=True) for r in routes
    ]
    gates = softmax_cols(picked)
    query = mm(normed, qw_ref[...])
    heads_pairs = query.shape[1] // LANES
    tiles = [query[:, j * LANES : (j + 1) * LANES] for j in range(heads_pairs)]
    low = lane < LANES // 2
    same = col[:, 6:7] == row[0:1, :]
    place = lax.broadcasted_iota(jnp.int32, (rows, rows), 0)
    other = lax.broadcasted_iota(jnp.int32, (rows, rows), 1)
    allowed = same & ((row[1:2, :] == 1) | (place == other))
    scale = 0.125
    shares = []
    for i in range(top_attn):
        sel = jnp.where(low, pick_head(tiles, routes[i], lane), 0.0).astype(BF16)
        qs_ref[0, i] = sel
        scores = mm_nt(sel, kv) * scale
        scores = jnp.where(allowed, scores, -1e30)
        expo = jnp.exp(scores - jnp.max(scores, axis=-1, keepdims=True))
        probs = (expo * (1.0 / jnp.sum(expo, axis=-1, keepdims=True))).astype(BF16)
        probs_ref[0, i] = probs
        heads = mm(probs, kv) * gates[i]
        shares.append(jnp.where(low, pltpu.roll(heads, LANES // 2, 1), heads))
    mixed_tiles = place_heads(shares, routes, heads_pairs, lane)
    mixed = jnp.concatenate([t.astype(BF16) for t in mixed_tiles], axis=1)
    mixed_ref[...] = mixed
    mid = x + mm(mixed, proj_ref[...])
    mid_ref[...] = mid
    hat2, _ = norm_parts(mid)
    n2 = (hat2 * vec_ref[2:3, :] + vec_ref[3:4, :]).astype(BF16)
    n2_ref[...] = n2
    n2_all[pl.ds(pl.multiple_of(step * rows, rows), rows), :] = n2
    logits_ffn = mm(n2, frw_ref[...])
    gates_ffn = softmax_cols(
        [
            jnp.sum(jnp.where(lane == col[:, 4 + i : 5 + i], logits_ffn, 0.0), axis=-1, keepdims=True)
            for i in range(2)
        ]
    )
    gates_ref[...] = put_cols(gates, rows, gates_ref.shape[1])
    stop = jnp.sum(mid * vec_ref[4:5, :], axis=-1, keepdims=True) + hb_ref[0:1, 0:1]
    pull = jnp.sum(grad_ref[0].astype(F32) * (mid - x), axis=-1, keepdims=True)
    scal_ref[...] = jnp.transpose(put_cols([stop, pull] + gates_ffn, rows, LANES))[:8, :]

    @pl.when(step == pl.num_programs(0) - 1)
    def _():
        dispatch([slotrow_ref[0, 0:1, :], slotrow_ref[0, 1:2, :]], [n2_all], out_ref)


def attention_forward(micro, tokens, grad, col, row, slotrow, vec, hb, qw, kvr, proj, frw, slots, moving, cid):
    _, count, width = tokens.shape
    steps = count // SEQ
    inner = qw.shape[1]
    whole = lambda a: pl.BlockSpec(a.shape, lambda r: (0,) * a.ndim)
    out_shape = (
        jax.ShapeDtypeStruct((count, width), F32),
        jax.ShapeDtypeStruct((count, width), BF16),
        jax.ShapeDtypeStruct((count, width), BF16),
        jax.ShapeDtypeStruct((count, inner), BF16),
        jax.ShapeDtypeStruct((steps, 4, SEQ, SEQ), BF16),
        jax.ShapeDtypeStruct((steps, 4, SEQ, LANES), BF16),
        jax.ShapeDtypeStruct((count, LANES), BF16),
        jax.ShapeDtypeStruct((count, 8), F32),
        jax.ShapeDtypeStruct((8, count), F32),
        jax.ShapeDtypeStruct((slots, width), BF16),
    )
    by_row = lambda c: pl.BlockSpec((SEQ, c), lambda r: (r, 0))
    in_specs = [
        pl.BlockSpec((1, SEQ, width), lambda r: (micro, r, 0)),
        pl.BlockSpec((1, SEQ, width), lambda r: (micro, r, 0)),
        pl.BlockSpec((1, SEQ, 8), lambda r: (micro, r, 0)),
        pl.BlockSpec((1, 8, SEQ), lambda r: (micro, 0, r)),
        pl.BlockSpec((1, 8, count), lambda r: (micro, 0, 0)),
        whole(vec), whole(hb), whole(qw), whole(kvr), whole(proj), whole(frw),
    ]
    out_specs = [
        by_row(width), by_row(width), by_row(width), by_row(inner),
        pl.BlockSpec((1, 4, SEQ, SEQ), lambda r: (r, 0, 0, 0)),
        pl.BlockSpec((1, 4, SEQ, LANES), lambda r: (r, 0, 0, 0)),
        by_row(LANES), by_row(8),
        pl.BlockSpec((8, SEQ), lambda r: (0, r)),
        pl.BlockSpec((slots, width), lambda r: (0, 0)),
    ]
    return run_kernel(
        attention_forward_kernel, (tokens, grad, col, row, slotrow, vec, hb, qw, kvr, proj, frw), in_specs,
        out_shape, out_specs, [pltpu.VMEM((count, width), BF16)], (steps,), "attention_forward",
        pl.CostEstimate(
            flops=2 * count * width * (2 * inner + 256 + slots), bytes_accessed=12 << 20, transcendentals=count * 4 * SEQ
        ),
        moving, cid,
    )


def gelu_parts(pre):
    square = pre * pre
    inner = jnp.tanh(GELU_C * pre * (1.0 + GELU_A * square))
    return square, inner


def read_rows(low, grad, vec_ref):
    cap, width = low.shape
    halt = split_three(jnp.broadcast_to(vec_ref[4:5, :], (8, width)))
    ones = jnp.ones((8, width), BF16)
    sub8 = lax.broadcasted_iota(jnp.int32, (8, cap), 0)
    stop = join_three(mm_nt(halt, low))
    prod = low.astype(F32) * grad.astype(F32)
    high = prod.astype(BF16)
    rest = (prod - high.astype(F32)).astype(BF16)
    pull = mm_nt(ones, high) + mm_nt(ones, rest)
    return jnp.where(sub8 == 0, stop, pull)


def expert_forward_kernel(rows0_ref, rows1_ref, first_ref, second_ref, *refs):
    total = refs[-1]
    if len(refs) == 3:
        out0_ref, out1_ref = refs[:2]
    else:
        near_ref, near_grad_ref, far_grad_ref, vec_ref, out0_ref, out1_ref, scal_ref = refs[:-1]
    part = pl.program_id(1)
    _, src, _, cap, width = rows0_ref.shape
    half = src * cap
    rows = jnp.concatenate([r[...].reshape(half, width) for r in (rows0_ref, rows1_ref)], axis=0)
    pre = mm(rows, first_ref[0, 0])
    _, inner = gelu_parts(pre)
    act = (0.5 * pre * (1.0 + inner)).astype(BF16)
    res = mm(act, second_ref[0, 0])

    @pl.when(part == 0)
    def _():
        total[...] = res

    @pl.when(part > 0)
    def _():
        total[...] += res

    @pl.when(part == pl.num_programs(1) - 1)
    def _():
        out0_ref[...] = total[:half, :].astype(BF16).reshape(out0_ref.shape)
        out1_ref[...] = total[half:, :].astype(BF16).reshape(out1_ref.shape)
        if len(refs) > 3:
            for s in range(src):
                scal_ref[s, 0, 0] = read_rows(near_ref[s, 0], near_grad_ref[0, s, 0], vec_ref)
                mine = total[half + s * cap : half + (s + 1) * cap, :].astype(BF16)
                scal_ref[s, 1, 0] = read_rows(mine, far_grad_ref[0, s, 0], vec_ref)


def expert_forward(kind, rows, first, second, moving, cid, read=()):
    _, src, local, cap, width = rows[0].shape
    parts, _, _, hid = first.shape
    spec_in = pl.BlockSpec((1, src, 1, cap, width), lambda e, h: (kind, 0, e, 0, 0))
    spec_rows = pl.BlockSpec((src, 1, cap, width), lambda e, h: (0, e, 0, 0))
    work = 2 * src * local * cap * width * hid * parts
    args, more, shapes, specs = (), [], [], []
    if read:
        near, grad, vec = read
        spec_grad = lambda k: pl.BlockSpec((1, src, 1, cap, width), lambda e, h: (k, 0, e, 0, 0))
        args = (near, grad, grad, vec)
        more = [spec_rows, spec_grad(0), spec_grad(1), pl.BlockSpec(vec.shape, lambda e, h: (0, 0))]
        shapes = [jax.ShapeDtypeStruct((src, 2, local, 8, cap), F32)]
        specs = [pl.BlockSpec((src, 2, 1, 8, cap), lambda e, h: (0, 0, e, 0, 0))]
    return run_kernel(
        expert_forward_kernel, (*rows, first, second, *args),
        [
            spec_in, spec_in,
            pl.BlockSpec((1, 1, width, hid), lambda e, h: (h, e, 0, 0)),
            pl.BlockSpec((1, 1, hid, width), lambda e, h: (h, e, 0, 0)),
        ] + more,
        [jax.ShapeDtypeStruct(r.shape[1:], BF16) for r in rows] + shapes, [spec_rows] * 2 + specs,
        [pltpu.VMEM((2 * src * cap, width), F32)], (local, parts), "expert_forward",
        pl.CostEstimate(flops=4 * work, bytes_accessed=24 << 20, transcendentals=work // width), moving, cid,
    )


def reading_kernel(near_ref, far_ref, near_grad_ref, far_grad_ref, vec_ref, scal_ref):
    for kind, (ref, grad_ref) in enumerate(((near_ref, near_grad_ref), (far_ref, far_grad_ref))):
        for s in range(ref.shape[0]):
            scal_ref[s, kind, 0] = read_rows(ref[s, 0], grad_ref[0, s, 0], vec_ref)


def reading_step(near, far, grad, vec):
    src, local, cap, width = near.shape
    spec_rows = pl.BlockSpec((src, 1, cap, width), lambda e: (0, e, 0, 0))
    spec_grad = lambda kind: pl.BlockSpec((1, src, 1, cap, width), lambda e: (kind, 0, e, 0, 0))
    return run_kernel(
        reading_kernel, (near, far, grad, grad, vec),
        [spec_rows] * 2 + [spec_grad(0), spec_grad(1), pl.BlockSpec(vec.shape, lambda e: (0, 0))],
        [jax.ShapeDtypeStruct((src, 2, local, 8, cap), F32)],
        [pl.BlockSpec((src, 2, 1, 8, cap), lambda e: (0, 0, e, 0, 0))], (), (local,), "reading_step",
        pl.CostEstimate(flops=10**9, bytes_accessed=4 << 20, transcendentals=0),
    )[0]


def add_cores(grown, gfirst_ref, gsecond_ref, stash, land, send_sem, recv_sem):
    step = pl.program_id(0) * pl.num_programs(1) + pl.program_id(1)
    steps = pl.num_programs(0) * pl.num_programs(1)
    core = lax.rem(lax.axis_index("hidden"), 2)
    pair = lax.div(step, 2)
    for i in range(2):
        stash[i][step] = grown[i]

    def crossing(k):
        return [
            pltpu.make_async_remote_copy(
                stash[i].at[2 * k + 1 - core], land[i].at[k], send_sem.at[i, k], recv_sem.at[i, k],
                device_id=other_core(), device_id_type=pl.DeviceIdType.MESH,
            )
            for i in range(2)
        ]

    @pl.when(lax.rem(step, 2) != core)
    def _():
        for c in crossing(pair):
            c.start()

    def finish(k):
        for c in crossing(k):
            c.wait()
        local, y = lax.div(k, gfirst_ref.shape[0]), lax.rem(k, gfirst_ref.shape[0])
        for ref, mine, got in ((gfirst_ref, stash[0], land[0]), (gsecond_ref, stash[1], land[1])):
            ref[y, local] = (mine[2 * k + core].astype(F32) + got[k].astype(F32)).astype(BF16)

    @pl.when((lax.rem(step, 2) == 0) & (step >= 2))
    def _():
        finish(pair - 1)

    @pl.when(step == steps - 1)
    def _():
        finish(pair)


def expert_backward_kernel(
    fold, rows0_ref, rows1_ref, grad0_ref, grad1_ref, ab_ref, vec_ref, first_ref, second_ref,
    gfirst_ref, gsecond_ref, out0_ref, out1_ref, total, gin_all, *crossed,
):
    part = pl.program_id(1)
    _, src, _, cap, width = rows0_ref.shape
    half = src * cap

    @pl.when(part == 0)
    def _():
        for m, grad_ref in enumerate((grad0_ref, grad1_ref)):
            for s in range(src):
                ab = ab_ref[s, m, 0]
                scaled = row_to_col(ab[0:1, :]) * grad_ref[0, s, 0].astype(F32) + row_to_col(ab[1:2, :]) * vec_ref[4:5, :]
                gin_all[m * half + s * cap : m * half + (s + 1) * cap, :] = scaled.astype(BF16)

    rows = jnp.concatenate([r[...].reshape(half, width) for r in (rows0_ref, rows1_ref)], axis=0)
    gin = gin_all[...]
    first = first_ref[0, 0]
    second = second_ref[0, 0]
    pre = mm(rows, first)
    gact = mm_nt(gin, second)
    square, inner = gelu_parts(pre)
    part_one = 0.5 * (1.0 + inner)
    act = (pre * part_one).astype(BF16)
    slope = part_one + 0.5 * pre * (1.0 - inner * inner) * (GELU_C + (3.0 * GELU_C * GELU_A) * square)
    gpre = (gact * slope).astype(BF16)
    grown = (mm_tn(rows, gpre).astype(BF16), mm_tn(act, gin).astype(BF16))
    if fold:
        add_cores(grown, gfirst_ref, gsecond_ref, *crossed)
    else:
        gfirst_ref[0, 0], gsecond_ref[0, 0] = grown
    res = mm_nt(gpre, first)

    @pl.when(part == 0)
    def _():
        total[...] = res

    @pl.when(part > 0)
    def _():
        total[...] += res

    @pl.when(part == pl.num_programs(1) - 1)
    def _():
        out0_ref[...] = total[:half, :].astype(BF16).reshape(out0_ref.shape)
        out1_ref[...] = total[half:, :].astype(BF16).reshape(out1_ref.shape)


def expert_backward(kind, rows, grads, ab, vec, first, second, moving, cid):
    _, src, local, cap, width = rows[0].shape
    parts, _, _, hid = first.shape
    spec_in = pl.BlockSpec((1, src, 1, cap, width), lambda e, h: (kind, 0, e, 0, 0))
    spec_rows = pl.BlockSpec((src, 1, cap, width), lambda e, h: (0, e, 0, 0))
    spec_first = pl.BlockSpec((1, 1, width, hid), lambda e, h: (h, e, 0, 0))
    spec_second = pl.BlockSpec((1, 1, hid, width), lambda e, h: (h, e, 0, 0))
    work = 2 * src * local * cap * width * hid * parts
    fold = kind == 0
    grown = [((parts // 2,) + a.shape[1:] if fold else a.shape) for a in (first, second)]
    pairs = local * parts // 2
    stash, kept = [[pltpu.VMEM((n,) + a.shape[2:], BF16) for a in (first, second)] for n in (2 * pairs, pairs)]
    return run_kernel(
        functools.partial(expert_backward_kernel, fold), (*rows, *grads, ab, vec, first, second),
        [spec_in] * 4
        + [pl.BlockSpec((src, 2, 1, 8, cap), lambda e, h: (0, 0, kind * local + e, 0, 0)), pl.BlockSpec(vec.shape, lambda e, h: (0, 0))]
        + [spec_first, spec_second],
        [jax.ShapeDtypeStruct(s, BF16) for s in grown] + [jax.ShapeDtypeStruct(r.shape[1:], BF16) for r in rows],
        ([pl.BlockSpec(s, lambda e, h: (0, 0, 0, 0)) for s in grown] if fold else [spec_first, spec_second]) + [spec_rows] * 2,
        [pltpu.VMEM((2 * src * cap, width), F32), pltpu.VMEM((2 * src * cap, width), BF16)]
        + ([stash, kept] + [pltpu.SemaphoreType.DMA((2, pairs))] * 2 if fold else []),
        (local, parts), "expert_backward",
        pl.CostEstimate(flops=10 * work, bytes_accessed=48 << 20, transcendentals=work // width), moving, cid, mate=fold,
    )


def scalar_kernel(
    scal0_ref, scal1_ref, rowsc0_ref, rowsc1_ref, slotrow_ref, cols_ref, ab_ref,
    got0, got1, sent, got2, send_sem, recv_sem, send_sem1, recv_sem1, send_sem2, recv_sem2,
):
    src, local, _, cap = scal0_ref.shape
    micros = 2
    got = (got0, got1)
    tokens = rowsc0_ref.shape[1]
    me = group_of()[0]
    group_greet()
    moves = group_copies(scal0_ref, got0, send_sem, recv_sem) + group_copies(scal1_ref, got1, send_sem1, recv_sem1)
    for c in moves:
        c.start()
    got0[me] = scal0_ref[me]
    got1[me] = scal1_ref[me]
    for c in moves:
        c.wait()
    spot = lax.broadcasted_iota(jnp.int32, (cap, tokens), 0)
    sub = lax.broadcasted_iota(jnp.int32, (LANES, tokens), 0)
    sub8 = lax.broadcasted_iota(jnp.int32, (8, tokens), 0)
    slots = [[slotrow_ref[m, i : i + 1, :] for i in range(2)] for m in range(micros)]

    def onehot(m, s, which):
        per = local // 2
        base = (which // per) * (src * per) + s * per + which % per
        base = spot + base * cap
        return [jnp.where(base == t, 1.0, 0.0).astype(BF16) for t in slots[m]]

    zero = jnp.zeros((24, tokens), F32)

    def collect(s, carry):
        carry = list(carry)
        for which in range(local):
            for m in range(micros):
                values = split_three(got[m][s, which])
                for i, p in enumerate(onehot(m, s, which)):
                    carry[2 * m + i] = carry[2 * m + i] + mm(values, p)
        return tuple(carry)

    found_all = [join_three(f) for f in lax.fori_loop(0, src, collect, (zero,) * (2 * micros))]
    shares = []
    for m, rowsc_ref in enumerate((rowsc0_ref, rowsc1_ref)):
        found = found_all[2 * m : 2 * m + 2]
        stop, pull, gate0, gate1 = [rowsc_ref[i : i + 1, :] for i in range(4)]
        gates = [gate0, gate1]
        yh = [f[0:1, :] for f in found]
        yg = [f[1:2, :] for f in found]
        halting = jax.nn.sigmoid(stop + gate0 * yh[0] + gate1 * yh[1])
        s = (pull + gate0 * yg[0] + gate1 * yg[1]) * halting * (1.0 - halting)
        u = [halting * g + s * h for g, h in zip(yg, yh)]
        mean = gate0 * u[0] + gate1 * u[1]
        keep = [halting, s, gate0 * (u[0] - mean), gate1 * (u[1] - mean), gate0, gate1]
        table = jnp.zeros((LANES, tokens), F32)
        for i, r in enumerate(keep):
            table = jnp.where(sub == i, r, table)
        cols_ref[m] = jnp.transpose(table)[:, :8]
        shares.append(
            [split_three(jnp.where(sub8 == 0, g * halting, jnp.where(sub8 == 1, g * s, 0.0))) for g in gates]
        )

    def spread(s, carry):
        for which in range(local):
            for m in range(micros):
                picks = onehot(m, s, which)
                sent[s, m, which] = join_three(mm_nt(shares[m][0], picks[0]) + mm_nt(shares[m][1], picks[1]))
        return carry

    lax.fori_loop(0, src, spread, 0)
    moves = group_copies(sent, got2, send_sem2, recv_sem2)
    for c in moves:
        c.start()
    got2[me] = sent[me]
    for c in moves:
        c.wait()
    ab_ref[...] = got2[...]


def scalar_step(scal, rowsc, slotrow):
    vmem = pl.BlockSpec(memory_space=pltpu.VMEM)
    tokens = rowsc[0].shape[1]
    src = scal[0].shape[0]
    both = (src, 2) + scal[0].shape[1:]
    return pl.pallas_call(
        scalar_kernel,
        out_shape=(jax.ShapeDtypeStruct((2, tokens, 8), F32), jax.ShapeDtypeStruct(both, F32)),
        in_specs=[vmem] * 5,
        out_specs=[vmem] * 2,
        scratch_shapes=[pltpu.VMEM(scal[0].shape, F32)] * 2 + [pltpu.VMEM(both, F32)] * 2
        + [pltpu.SemaphoreType.DMA((src - 1,))] * 6,
        compiler_params=pltpu.CompilerParams(collective_id=0, has_side_effects=True),
        cost_estimate=pl.CostEstimate(flops=10**9, bytes_accessed=1 << 20, transcendentals=tokens),
        name="scalar_step",
    )(*scal, *rowsc, slotrow)


def result_kernel(has_old, *refs):
    x_ref, mid_ref, near_ref, far_ref, cols_ref, slotcol_ref = refs[:6]
    result_ref, hsum_ref = refs[-2:]
    tokens, width = mid_ref.shape
    chunk = 256
    chunks = near_ref.shape[0] // chunk
    lane = lane_iota(tokens, chunk)
    slot_c = [slotcol_ref[0, :, i : i + 1] for i in range(2)]

    def gather(k, carry):
        for kind, ref in enumerate((near_ref, far_ref)):
            block = ref[pl.ds(pl.multiple_of(k * chunk, chunk), chunk), :]
            base = lane + (k + kind * chunks) * chunk
            carry = tuple(
                c + mm(jnp.where(base == s, 1.0, 0.0).astype(BF16), block) for c, s in zip(carry, slot_c)
            )
        return carry

    zero = jnp.zeros((tokens, width), F32)
    picked = lax.fori_loop(0, chunks, gather, (zero, zero))
    cols = cols_ref[0]
    halting, s = cols[:, 0:1], cols[:, 1:2]
    x = x_ref[0].astype(F32)
    end = mid_ref[...] + (cols[:, 4:5] * picked[0] + cols[:, 5:6] * picked[1])
    result_ref[0] = (x + halting * (end - x)).astype(BF16)
    sub8 = lax.broadcasted_iota(jnp.int32, (8, width), 0)
    ssum = jnp.broadcast_to(jnp.sum(s, axis=0, keepdims=True), (1, width))
    hsum_ref[...] = jnp.where(sub8 == 0, fold_rows(s * end), jnp.where(sub8 == 1, ssum, 0.0))


def result_step(micro, tokens, mid, near, far, cols, slotcol, old, moving, cid):
    _, count, width = tokens.shape
    whole = lambda a: pl.BlockSpec(a.shape, lambda i: (0,) * a.ndim)
    part = pl.BlockSpec((1, count, width), lambda i: (micro, 0, 0))
    cols_spec = pl.BlockSpec((1, count, 8), lambda i: (micro, 0, 0))
    return run_kernel(
        functools.partial(result_kernel, bool(old)), (tokens, mid, near, far, cols, slotcol, *old),
        [part, whole(mid), whole(near), whole(far), cols_spec, cols_spec] + [pl.BlockSpec(memory_space=pl.ANY)] * len(old),
        (jax.ShapeDtypeStruct(tokens.shape, BF16), jax.ShapeDtypeStruct((8, width), F32)),
        [part, pl.BlockSpec((8, width), lambda i: (0, 0))], (), (1,), "result_step",
        pl.CostEstimate(
            flops=8 * count * near.shape[0] * width, bytes_accessed=5 << 20, transcendentals=count
        ),
        moving, cid, {6: 0} if old else None,
    )


def attention_backward_kernel(last, n_old, *refs):
    (x_ref, grad_ref, col_ref, vec_ref, qw_ref, kvr_ref, proj_ref, frw_ref,
     mid_ref, n2_ref, normed_ref, mixed_ref, probs_ref, qs_ref, kv_ref, gates_ref, slotcol_ref,
     near_ref, far_ref, cols_ref) = refs[:20]
    old = refs[20 : 20 + n_old]
    gtok_ref = refs[20 + n_old]
    outs = refs[21 + n_old : -6]
    gsum, gq_ref, gproj_ref, gkvr_ref, gfr_ref, gvec_ref = refs[-6:]
    step = pl.program_id(0)
    rows, width = mid_ref.shape
    lane = lane_iota(rows)
    low = lane < LANES // 2
    col = col_ref[0]
    chunk = 256
    cols = cols_ref[0]
    slot_c = [slotcol_ref[0, :, i : i + 1] for i in range(2)]
    lane_c = lane_iota(rows, chunk)
    accs = (gq_ref, gproj_ref, gkvr_ref, gfr_ref, gvec_ref)

    @pl.when(step == 0)
    def _():
        for k, ref in enumerate(accs):
            ref[...] = old[k][...] if old else jnp.zeros_like(ref)

    gsum[...] = jnp.zeros_like(gsum)

    chunks = near_ref.shape[0] // chunk

    def gather(k, carry):
        for kind, ref in enumerate((near_ref, far_ref)):
            block = ref[pl.ds(pl.multiple_of(k * chunk, chunk), chunk), :]
            base = lane_c + (k + kind * chunks) * chunk
            pick = jnp.where((base == slot_c[0]) | (base == slot_c[1]), 1.0, 0.0).astype(BF16)
            gsum[...] += mm(pick, block)
        return carry

    lax.fori_loop(0, chunks, gather, 0)
    glog = jnp.zeros((rows, LANES), F32)
    for i in range(2):
        glog = jnp.where(lane == col[:, 4 + i : 5 + i], cols[:, 2 + i : 3 + i], glog)
    glog = glog.astype(BF16)
    n2 = n2_ref[...]
    gfr_ref[...] += mm_tn(glog, n2)
    gn2 = gsum[...] + mm_nt(glog, frw_ref[...])
    hat2, rstd2 = norm_parts(mid_ref[...])
    grad = grad_ref[0].astype(F32)
    halting = cols[:, 0:1]
    gend = halting * grad + cols[:, 1:2] * vec_ref[4:5, :]
    gmid = gend + norm_back(hat2, rstd2, vec_ref[2:3, :], gn2)
    ggain2 = fold_rows(gn2 * hat2)
    gbias2 = fold_rows(gn2)
    gattn = gmid.astype(BF16)
    gproj_ref[...] += mm_tn(gattn, mixed_ref[...])
    gmixed = mm_nt(gattn, proj_ref[...]).astype(BF16).astype(F32)
    pairs = gmixed.shape[1] // LANES
    tiles = [gmixed[:, j * LANES : (j + 1) * LANES] for j in range(pairs)]
    kv = kv_ref[...]
    scale = 0.125
    routes = [col[:, i : i + 1] for i in range(4)]
    gkv = jnp.zeros((LANES, rows), F32)
    ggates = []
    parts = []
    for i in range(4):
        gate = gates_ref[:, i : i + 1]
        sel = pltpu.roll(pick_head(tiles, routes[i], lane), LANES // 2, 1)
        sel = jnp.where(low, 0.0, sel)
        probs = probs_ref[0, i]
        heads = mm(probs, kv)
        ggates.append(jnp.sum(heads * sel, axis=-1, keepdims=True))
        gheads = (gate * sel).astype(BF16)
        gprobs = mm_nt(gheads, kv)
        probs_f = probs.astype(F32)
        inner = jnp.sum(heads * gheads.astype(F32), axis=-1, keepdims=True)
        gscores = (probs_f * (gprobs - inner)).astype(BF16)
        gkv = gkv + mm_tn(gheads, probs) + mm_tn(qs_ref[0, i], gscores) * scale
        gq = mm(gscores, kv) * scale
        parts.append(jnp.where(low, gq, pltpu.roll(gq, LANES // 2, 1)))
    gtiles = place_heads(parts, routes, pairs, lane)
    gquery = jnp.concatenate([t.astype(BF16) for t in gtiles], axis=1)
    normed = normed_ref[...]
    gq_ref[...] += mm_tn(normed, gquery)
    mean = ggates[0] * gates_ref[:, 0:1]
    for i in range(1, 4):
        mean = mean + ggates[i] * gates_ref[:, i : i + 1]
    alog = jnp.zeros((rows, LANES), F32)
    for i in range(4):
        alog = jnp.where(lane == routes[i], gates_ref[:, i : i + 1] * (ggates[i] - mean), alog)
    gkvr = jnp.concatenate([jnp.transpose(gkv).astype(BF16), alog.astype(BF16)], axis=1)
    gkvr_ref[...] += mm_tn(gkvr, normed)
    gnormed = mm_nt(gquery, qw_ref[...]) + mm_nt(gkvr, kvr_ref[...])
    hat, rstd = norm_parts(x_ref[0].astype(F32))
    gtok_ref[0] = grad * (1.0 - halting) + gmid + norm_back(hat, rstd, vec_ref[0:1, :], gnormed)
    sub8 = lax.broadcasted_iota(jnp.int32, (8, width), 0)
    gvec = jnp.where(sub8 == 0, fold_rows(gnormed * hat), 0.0)
    gvec = jnp.where(sub8 == 1, fold_rows(gnormed), gvec)
    gvec = jnp.where(sub8 == 2, ggain2, gvec)
    gvec_ref[...] += jnp.where(sub8 == 3, gbias2, gvec)

    @pl.when(step == pl.num_programs(0) - 1)
    def _():
        if not last:
            for ref, out in zip(accs, outs):
                out[...] = ref[...]
            return
        pack, gvec_out = outs
        gvec_out[...] = gvec_ref[...]
        blocks = gq_ref.shape[1] // width
        for j in range(blocks):
            pack[j * width : (j + 1) * width, :] = gq_ref[:, j * width : (j + 1) * width].astype(BF16)
        place = blocks * width
        for j in range(blocks):
            pack[place : place + width, :] = jnp.transpose(gproj_ref[:, j * width : (j + 1) * width]).astype(BF16)
            place = place + width
        for ref in (gkvr_ref, gfr_ref):
            pack[place : place + ref.shape[0], :] = ref[...].astype(BF16)
            place = place + ref.shape[0]
        pack[place:, :] = jnp.zeros((pack.shape[0] - place, width), BF16)


def attention_backward(micro, last, packed_rows, tokens, grad, col, vec, qw, kvr, proj, frw, saved, near, far, cols, old, moving, cid):
    mid, n2, normed, mixed, probs, qs, kv, gates, slotcol = saved
    _, count, width = tokens.shape
    steps = count // SEQ
    inner = qw.shape[1]
    whole = lambda a: pl.BlockSpec(a.shape, lambda r: (0,) * a.ndim)
    by_row = lambda c: pl.BlockSpec((SEQ, c), lambda r: (r, 0))
    part = pl.BlockSpec((1, SEQ, width), lambda r: (micro, r, 0))
    grown = [qw.shape] + [a.shape[::-1] for a in (proj, kvr, frw)]
    out_shape = [jax.ShapeDtypeStruct(tokens.shape, F32)]
    if last:
        out_shape += [jax.ShapeDtypeStruct((packed_rows, width), BF16)]
    else:
        out_shape += [jax.ShapeDtypeStruct(s, F32) for s in grown]
    out_shape += [jax.ShapeDtypeStruct((8, width), F32)]
    old_in = [old[k] for k in (1, 2, 3, 4, 5)] if old else []
    hbm = pl.BlockSpec(memory_space=pl.ANY)
    cols_spec = pl.BlockSpec((1, SEQ, 8), lambda r: (micro, r, 0))
    in_specs = [
        part, part, cols_spec,
        whole(vec), whole(qw), whole(kvr), whole(proj), whole(frw),
        by_row(width), by_row(width), by_row(width), by_row(inner),
        pl.BlockSpec((1, 4, SEQ, SEQ), lambda r: (r, 0, 0, 0)),
        pl.BlockSpec((1, 4, SEQ, LANES), lambda r: (r, 0, 0, 0)),
        by_row(LANES), by_row(8), cols_spec,
        whole(near), whole(far), cols_spec,
    ] + [whole(o) for o in old_in] + [hbm] * (1 if old else 0)
    args = (
        tokens, grad, col, vec, qw, kvr, proj, frw, mid, n2, normed, mixed, probs, qs, kv, gates, slotcol, near, far, cols,
        *old_in, *(old[:1] if old else []),
    )
    return run_kernel(
        functools.partial(attention_backward_kernel, last, len(old_in) + (1 if old else 0)), args, in_specs,
        out_shape, [part] + [pl.BlockSpec(o.shape, lambda r: (0, 0)) for o in out_shape[1:]],
        [
            pltpu.VMEM((SEQ, width), F32),
            *[pltpu.VMEM(s, F32) for s in grown],
            pltpu.VMEM((8, width), F32),
        ],
        (steps,), "attention_backward",
        pl.CostEstimate(
            flops=2 * count * width * (4 * inner + 512 + 2 * near.shape[0]), bytes_accessed=24 << 20, transcendentals=0
        ),
        moving, cid, {25: 0} if old else None,
    )


def total_plan(n_expert, n_hidden, rows):
    ny = nx = n_hidden // 2
    nz = n_expert // nx
    unit = 16 * ny * nx * nz
    units = -(-rows // (2 * unit))
    count = min(units, STREAMS)
    streams = tuple((units // count + (i < units % count)) * unit for i in range(count))
    return (nz, nx, ny), streams


def total_kernel(
    sizes, streams, pack_ref, small_ref, out_ref, sum_ref,
    buf, done, core_in, land, small_got, small_part, small_got2, sems, small_sems,
):
    nz, nx, ny = sizes
    e, h = lax.axis_index("expert"), lax.axis_index("hidden")
    n_expert, n_hidden = nz * nx, ny * 2
    z, x = lax.div(e, nx), lax.rem(e, nx)
    y, c = lax.div(h, 2), lax.rem(h, 2)
    half = sum(streams)
    width = pack_ref.shape[1]
    mesh_id = pl.DeviceIdType.MESH
    barrier = pltpu.get_barrier_semaphore()
    for k in range(1, n_expert):
        pl.semaphore_signal(barrier, inc=1, device_id=(lax.rem(e + k, n_expert), h), device_id_type=mesh_id)
    for k in range(1, n_hidden):
        pl.semaphore_signal(barrier, inc=1, device_id=(e, lax.rem(h + k, n_hidden)), device_id_type=mesh_id)
    pl.semaphore_wait(barrier, n_expert + n_hidden - 2)
    used = {}

    def copy(source, target, device, pool=sems):
        i = used.get(id(pool), 0)
        used[id(pool)] = i + 1
        return pltpu.make_async_remote_copy(
            source, target, pool.at[0, i], pool.at[1, i], device_id=device, device_id_type=mesh_id
        )

    def rows_at(ref, start, count):
        return ref.at[pl.ds(pl.multiple_of(start, 16), count)]

    def add_rows(start, count, base, pieces):
        step = 64 if count % 64 == 0 else 16

        def body(i, carry):
            place = pl.ds(pl.multiple_of(start + i * step, 16), step)
            total = base[place, :].astype(F32)
            for ref in pieces:
                total = total + ref[pl.ds(pl.multiple_of(i * step, 16), step), :].astype(F32)
            buf[place, :] = total.astype(BF16)
            return carry

        lax.fori_loop(0, count // step, body, 0)

    axes = {
        "c": (2, c, lambda p: (e, y * 2 + p)),
        "y": (ny, y, lambda p: (e, p * 2 + c)),
        "x": (nx, x, lambda p: (z * nx + p, h)),
        "z": (nz, z, lambda p: (p * nx + x, h)),
    }
    landed = [0]

    def travel(first, count, order, delay):
        for _ in range(delay):
            yield
        moves = [copy(rows_at(pack_ref, (1 - c) * half + first, count), rows_at(core_in, first, count), axes["c"][2](1 - c))]
        for m in moves:
            m.start()
        yield
        for m in moves:
            m.wait()
        start, span = c * half + first, count
        add_rows(start, span, pack_ref, [core_in.at[pl.ds(first, count)]])
        trail = []
        for name in order:
            size, me, device = axes[name]
            chunk = span // size
            moves, pieces = [], []
            for k in range(1, size):
                peer = lax.rem(me + k, size)
                pieces.append(land.at[pl.ds(landed[0], chunk)])
                landed[0] += chunk
                moves.append(copy(rows_at(buf, start + peer * chunk, chunk), pieces[-1], device(peer)))
            for m in moves:
                m.start()
            yield
            for m in moves:
                m.wait()
            start, span = start + me * chunk, chunk
            trail.append((start, chunk, size, me, device))
            add_rows(start, span, buf, pieces)
        here = pl.ds(pl.multiple_of(start, 16), span)
        done[here, :] = buf[here, :]
        for begin, chunk, size, me, device in reversed(trail):
            place = rows_at(done, begin, chunk)
            moves = [copy(place, place, device(lax.rem(me + k, size))) for k in range(1, size)]
            for m in moves:
                m.start()
            yield
            for m in moves:
                m.wait()
        place = rows_at(done, c * half + first, count)
        moves = [copy(place, place, axes["c"][2](1 - c))]
        for m in moves:
            m.start()
        yield
        for m in moves:
            m.wait()

    def travel_small():
        moves = [
            copy(small_ref, small_got.at[e], (lax.rem(e + k, n_expert), h), small_sems) for k in range(1, n_expert)
        ]
        for m in moves:
            m.start()
        small_got[e] = small_ref[...]
        yield
        yield
        for m in moves:
            m.wait()
        small_part[...] = jnp.sum(small_got[...], axis=0)
        moves = [
            copy(small_part, small_got2.at[h], (e, lax.rem(h + k, n_hidden)), small_sems) for k in range(1, n_hidden)
        ]
        for m in moves:
            m.start()
        small_got2[h] = small_part[...]
        yield
        yield
        for m in moves:
            m.wait()
        sum_ref[...] = jnp.sum(small_got2[...], axis=0)

    going, first = [], 0
    for i, count in enumerate(streams):
        going.append(travel(first, count, ("yxz", "xyz")[i % 2], 2 * (i >= len(streams) // 2)))
        first += count
    going.append(travel_small())
    while going:
        going = [g for g in going if next(g, StopIteration) is not StopIteration]
    step = 64 if half % 64 == 0 else 16

    def body(i, carry):
        here = pl.ds(pl.multiple_of(i * step, step), step)
        out_ref[here, :] = done[here, :]
        return carry

    lax.fori_loop(0, 2 * half // step, body, 0)


def total_step(n_expert, n_hidden, rows, pack, small):
    sizes, streams = total_plan(n_expert, n_hidden, rows)
    nz, nx, ny = sizes
    width = pack.shape[1]
    half = sum(streams)
    vmem = pl.BlockSpec(memory_space=pltpu.VMEM)
    landing = 0
    for i, span in enumerate(streams):
        for size in ((ny, nx, nz), (nx, ny, nz))[i % 2]:
            span = span // size
            landing += span * (size - 1)
    steps = len(streams) * (2 + 2 * ((ny - 1) + (nx - 1) + (nz - 1)))
    return pl.pallas_call(
        functools.partial(total_kernel, sizes, streams),
        out_shape=(jax.ShapeDtypeStruct(pack.shape, BF16), jax.ShapeDtypeStruct(small.shape, F32)),
        in_specs=[vmem] * 2,
        out_specs=[vmem] * 2,
        scratch_shapes=[
            pltpu.VMEM((2 * half, width), BF16),
            pltpu.VMEM((2 * half, width), BF16),
            pltpu.VMEM((half, width), BF16),
            pltpu.VMEM((landing, width), BF16),
            pltpu.VMEM((n_expert,) + small.shape, F32),
            pltpu.VMEM(small.shape, F32),
            pltpu.VMEM((n_hidden,) + small.shape, F32),
            pltpu.SemaphoreType.DMA((2, steps)),
            pltpu.SemaphoreType.DMA((2, n_expert + n_hidden)),
        ],
        compiler_params=pltpu.CompilerParams(collective_id=8, has_side_effects=True, vmem_limit_bytes=VMEM_LIMIT),
        name="total_step",
    )(pack, small)


def unpack_kernel(
    pack_ref, near_a, near_b, far_a, far_b,
    gq_ref, gproj_ref, first_ref, second_ref, key_ref, value_ref, router_ref, ffn_ref,
):
    step = pl.program_id(0)
    width = pack_ref.shape[2]
    blocks = gproj_ref.shape[0]
    for j in range(blocks):
        gq_ref[:, j * width : (j + 1) * width] = pack_ref[j].astype(F32)
        gproj_ref[j] = pack_ref[blocks + j].astype(F32)
    first_ref[...] = near_a[...].astype(F32) + far_a[...].astype(F32)
    second_ref[...] = near_b[...].astype(F32) + far_b[...].astype(F32)
    head = key_ref.shape[0]

    @pl.when(step == 0)
    def _():
        key_ref[...] = pack_ref[2 * blocks, :head, :].astype(F32)
        value_ref[...] = pack_ref[2 * blocks, head : 2 * head, :].astype(F32)

    @pl.when(step == 1)
    def _():
        router_ref[...] = pack_ref[2 * blocks, : router_ref.shape[0], :].astype(F32)

    @pl.when(step == 2)
    def _():
        ffn_ref[...] = pack_ref[2 * blocks, : ffn_ref.shape[0], :].astype(F32)


def unpack_step(pack, near, far, head, routes, experts):
    steps = 4
    slabs, width, _ = pack.shape
    blocks = slabs // 2
    rows = width // steps
    out_shape = [
        jax.ShapeDtypeStruct((width, blocks * width), F32),
        jax.ShapeDtypeStruct((blocks, width, width), F32),
        *[jax.ShapeDtypeStruct(a.shape, F32) for a in near],
        *[jax.ShapeDtypeStruct((n, width), F32) for n in (head, head, routes, experts)],
    ]
    cut = lambda a: pl.BlockSpec((a.shape[0], a.shape[1] // steps, a.shape[2]), lambda i: (0, i, 0))
    return run_kernel(
        unpack_kernel, (pack, *near, *far), [cut(pack)] + [cut(a) for a in near] * 2, out_shape,
        [pl.BlockSpec((rows, blocks * width), lambda i: (i, 0)), cut(out_shape[1])] + [cut(a) for a in near]
        + [pl.BlockSpec(o.shape, lambda i: (0, 0)) for o in out_shape[4:]],
        (), (steps,), "unpack_step", pl.CostEstimate(flops=0, bytes_accessed=20 << 20, transcendentals=0),
    )


def pad_lanes(a):
    return jnp.pad(a, ((0, 0), (0, LANES - a.shape[1])))


def per_device(
    tokens, grad_out, attn_routes, ffn_routes, segments, pad_mask, norm1_gain, norm1_bias, attn_router,
    query_w, key_w, value_w, attn_proj, norm2_gain, norm2_bias, ffn_router, expert_in, expert_out, halt_w, halt_b,
    *, n_expert, n_hidden,
):
    micros, count, width = tokens.shape
    experts = ffn_router.shape[1]
    capacity = 4 * count // experts
    slots = experts * capacity
    per = experts // n_expert
    group = n_expert // 2
    across = [(i, (i + group) % n_expert) for i in range(n_expert)]

    def gathered(a):
        return lax.all_gather(a, "hidden", axis=0, tiled=False)

    crossed = [lax.ppermute(a, "expert", across) for a in (expert_in, expert_out)]
    near_first, near_second = gathered(expert_in), gathered(expert_out)
    seg = segments.reshape(micros, count)
    zeros = jnp.zeros_like(seg)
    mine = lax.axis_index("expert") // group
    kind = (ffn_routes // (experts // 2) != mine).astype(jnp.int32)
    base = (kind * (experts // 2) + ffn_routes % (experts // 2)) * capacity
    col = jnp.concatenate([attn_routes, ffn_routes, seg[:, :, None], pad_mask[:, :, None]], axis=2)
    row = jnp.stack(
        [seg, pad_mask, ffn_routes[:, :, 0], ffn_routes[:, :, 1], base[:, :, 0], base[:, :, 1], zeros, zeros], axis=1
    )
    none = jnp.zeros_like(halt_w)
    vec = jnp.stack([norm1_gain, norm1_bias, norm2_gain, norm2_bias, halt_w, none, none, none])
    kvr = jnp.concatenate([key_w, value_w, pad_lanes(attn_router)], axis=1)
    frw = pad_lanes(ffn_router)
    hb = jnp.broadcast_to(halt_b.reshape(1, 1), (8, LANES))
    shape = (2, group, per, capacity, width)
    packed = query_w.size // width + attn_proj.shape[0] + width
    packed_rows = 2 * sum(total_plan(n_expert, n_hidden, packed)[1])

    slotrow, slotcol = route_step(row)
    weights = (vec, hb, query_w, kvr, attn_proj, frw)
    f0 = attention_forward(0, tokens, grad_out, col, row, slotrow, *weights, slots, (), None)
    crossed[0], n0_out = lax.optimization_barrier((crossed[0], f0[9]))
    far_first = gathered(crossed[0])
    *f1, n0 = attention_forward(1, tokens, grad_out, col, row, slotrow, *weights, slots, [n0_out.reshape(shape)], 2)
    crossed[1], n1_out = lax.optimization_barrier((crossed[1], f1[9]))
    far_second = gathered(crossed[1])
    gs0, gs1, n1 = spread_step(slotrow, grad_out, slots, [n1_out.reshape(shape)], 3)
    rows = (n0, n1)
    y0, y1, g1 = expert_forward(0, rows, near_first, near_second, [gs1.reshape(shape)], 4)
    far0, far1, scal1, g0 = expert_forward(1, rows, far_first, far_second, [gs0.reshape(shape)], 1, (y1, g1, vec))
    grads = (g0, g1)
    scal = [a.reshape(group, 2 * per, 8, capacity) for a in (reading_step(y0, far0, g0, vec), scal1)]
    cols, ab = scalar_step(scal, (f0[8], f1[8]), slotrow)
    gf_far, gs_far, bf0, bf1, r0, rf0, r1 = expert_backward(
        1, rows, grads, ab, vec, far_first, far_second, [y0, far0, y1], 9
    )
    gf_near, gs_near, bn0, bn1, qf0, qf1, rf1 = expert_backward(
        0, rows, grads, ab, vec, near_first, near_second, [bf0, bf1, far1], 10
    )

    flat = lambda a: a.reshape(slots // 2, width)

    def reduced(a):
        ranks = [[2 * y + c for y in range(n_hidden // 2)] for c in range(2)]
        groups = ranks if a.shape[0] < n_hidden else None
        return lax.psum_scatter(a, "hidden", scatter_dimension=0, axis_index_groups=groups, tiled=False)

    far_grads = [reduced(a) for a in (gf_far, gs_far)]
    near_grads = [reduced(a) for a in (gf_near, gs_near)]
    *res0, qn0, qn1 = result_step(0, tokens, f0[0], flat(r0), flat(rf0), cols, slotcol, (), [bn0, bn1], 11)
    common = (tokens, grad_out, col, vec, query_w, kvr, attn_proj, frw)
    far_grads[0], qn0 = lax.optimization_barrier((far_grads[0], qn0))
    far_grads[0] = lax.ppermute(far_grads[0], "expert", across)
    out = attention_backward(
        0, False, packed_rows, *common, list(f0[:8]) + [slotcol], flat(qn0), flat(qf0), cols, (), (), None
    )
    res1 = result_step(1, tokens, f1[0], flat(r1), flat(rf1), cols, slotcol, tuple(res0[:1]), (), None)
    out, far_grads[1] = lax.optimization_barrier((tuple(out), far_grads[1]))
    far_grads[1] = lax.ppermute(far_grads[1], "expert", across)
    out = attention_backward(
        1, True, packed_rows, *common, list(f1[:8]) + [slotcol], flat(qn1), flat(qf1), cols, tuple(out), (), None
    )
    packs = out[1]
    small = jnp.concatenate([out[2], res0[1] + res1[1]], axis=0)
    total, small = total_step(n_expert, n_hidden, packed, packs, small)
    near_grads = [a.reshape(a.shape[-3:]) for a in near_grads]
    far_grads = [a.reshape(a.shape[-3:]) for a in far_grads]
    gq, gproj, gfirst, gsecond, gkey, gvalue, grouter, gfr = unpack_step(
        total[:packed].reshape(-1, width, width), near_grads, far_grads, key_w.shape[1], attn_router.shape[1], experts
    )
    return (
        res1[0],
        out[0],
        small[0],
        small[1],
        grouter.T,
        gq,
        gkey.T,
        gvalue.T,
        gproj.reshape(attn_proj.shape),
        small[2],
        small[3],
        gfr.T,
        gfirst,
        gsecond,
        small[8],
        small[9, :1],
    )


def solution(mesh):
    rows = P(None, ("expert", "hidden"), None)
    in_specs = (rows,) * 5 + (P(None, ("expert", "hidden")),) + (P(),) * 10 + (
        P("expert", None, "hidden"), P("expert", "hidden", None), P(), P(),
    )
    out_specs = (rows,) * 2 + (P(),) * 10 + (P("expert", None, "hidden"), P("expert", "hidden", None), P(), P())
    return jax.shard_map(
        functools.partial(per_device, n_expert=mesh.shape["expert"], n_hidden=mesh.shape["hidden"]),
        mesh=mesh, in_specs=in_specs, out_specs=out_specs, check_vma=False,
    )
```
